128 devices in a mesh: ctx: 32 (over x, z, y_lo), tp: 4 (over y_hi, core).
Axes of the slice: x: 4, y: 4 (y_hi: 2, y_lo: 2; y = y_hi * 2 + y_lo), z: 4, core: 2. Of those that a mesh axis runs over, the one named last changes fastest.
Arguments:
- queries: bfloat16 [1024, 8192], P('ctx', 'tp'), may hold values from -15 to 15
- new_keys: bfloat16 [1024, 1024], P('ctx', 'tp'), may hold values from -6 to 6
- new_values: bfloat16 [1024, 1024], P('ctx', 'tp'), may hold values from -6 to 6
- cache_keys: bfloat16 [131072, 1024], P('ctx', 'tp'), may hold values from -6 to 6
- cache_values: bfloat16 [131072, 1024], P('ctx', 'tp'), may hold values from -6 to 6
- keep_tiles: int32 [32, 8, 24], P('ctx', 'tp'), may hold values from 0 to 31, as said below
- tile_count: int32 [32, 8], P('ctx', 'tp'), may hold values from 1 to 24
- owner_slot: int32 [32], replicated, may hold values from 0 to 31, each once
- out_weight: bfloat16 [8192, 8192], P('tp', 'ctx'), may hold values from -0.0625 to 0.0625
Outputs:
- projected_out: float32 [1024, 8192], P('tp', 'ctx')
The draws below stay inside these ranges and needn't reach their ends.
Inputs may be any that keep to these rules, and one draw needn't show every extreme that they name: `keep_tiles`: the 24 entries of each keep list are distinct tile numbers; entries at or past tile_count are ignored.
All inputs are finite; a program needn't handle non-finite values.
Results may differ from the reference program's by a relative error of at most 0.0055.
Values may be sent and summed in bfloat16 or wider, within the bound.
A program may use at most 128 MiB of HBM per device.

```python
import jax
import jax.numpy as jnp
from jax import lax

D = 8192
HQ = 64
KVH = 8
DH = 128
TILE = 128
TILES = 32
Q_DEV = 32
CAP = 24
Q_TOTAL = 1024
N_CTX = 32


def pattern_signs(key):
    random_bits = jax.random.randint(jax.random.fold_in(key, 4242), (KVH, DH), 0, 2)
    return (2 * random_bits - 1).astype(jnp.float32)


def target_score(row_ids):
    return 120.0 + 90.0 * (row_ids // Q_DEV % 3).astype(jnp.float32)


def key_strength(row_ids):
    return jnp.sqrt(target_score(row_ids) / (2.5 * DH ** 0.5))


def draw_queries(key, part):
    inner_key = jax.random.fold_in(key, 11)
    values_out = jnp.clip(3.0 * jax.random.normal(inner_key, (Q_TOTAL, HQ * DH), jnp.float32), -15.0, 15.0)
    row_ids = jnp.arange(Q_TOTAL, dtype=jnp.int32)
    local_ids = row_ids % Q_DEV
    planted = (local_ids == 1) | (local_ids == Q_DEV - 1)
    signs_full = jnp.repeat(pattern_signs(key), HQ // KVH, axis=0).reshape(1, HQ * DH)
    strength = 2.5 * key_strength(row_ids)[:, None]
    values_out = jnp.where(planted[:, None], signs_full * strength, values_out)
    return values_out.astype(jnp.bfloat16)


def draw_new_keys(key, part):
    inner_key = jax.random.fold_in(key, 12)
    values_out = jnp.clip(jax.random.normal(inner_key, (Q_TOTAL, KVH * DH), jnp.float32), -6.0, 6.0)
    row_ids = jnp.arange(Q_TOTAL, dtype=jnp.int32)
    local_ids = row_ids % Q_DEV
    exact_rows = (local_ids == 1) | (local_ids == Q_DEV - 1)
    near_rows = (local_ids == 0) | (local_ids == Q_DEV - 2)
    signs_full = pattern_signs(key).reshape(1, KVH * DH)
    strength = key_strength(row_ids)[:, None]
    values_out = jnp.where(exact_rows[:, None], signs_full * strength, values_out)
    values_out = jnp.where(near_rows[:, None], signs_full * strength * 0.99, values_out)
    return values_out.astype(jnp.bfloat16)


def draw_keep_tiles(key, part):
    split_keys = jax.random.split(jax.random.fold_in(key, 21), N_CTX * KVH)
    orders = jax.vmap(lambda one_key: jax.random.permutation(one_key, TILES))(split_keys)
    return orders[:, :CAP].reshape(N_CTX, KVH, CAP).astype(jnp.int32)


def draw_tile_count(key, part):
    inner_key = jax.random.fold_in(key, 31)
    head_top = jax.random.randint(jax.random.fold_in(inner_key, 1), (1, KVH), CAP // 2, CAP + 1)
    lower = head_top // 2 + 1
    spread = head_top - head_top // 2
    raw_bits = jax.random.randint(jax.random.fold_in(inner_key, 2), (N_CTX, KVH), 0, 1048576)
    counts = lower + raw_bits % spread
    full_at = jax.random.randint(jax.random.fold_in(inner_key, 3), (), 0, N_CTX * KVH)
    flat_ids = jnp.arange(N_CTX * KVH, dtype=jnp.int32).reshape(N_CTX, KVH)
    counts = jnp.where(flat_ids == full_at, CAP, counts)
    return counts.astype(jnp.int32)


def levels(key, dims, pieces, low, largest):
    level = 1.0
    for axis_at, parts in pieces:
        heights = jax.random.uniform(jax.random.fold_in(jax.random.fold_in(key, 6), axis_at), (parts,), jnp.float32, low / len(pieces), largest / len(pieces))
        level = level * jnp.repeat(jnp.exp(heights), dims[axis_at] // parts).reshape((-1,) + (1,) * (len(dims) - 1 - axis_at))
    return level


def gaussian(stream_key, extent, scale, bound, pieces=(), kind=jnp.bfloat16):
    drawn = scale * jax.random.normal(stream_key, extent, jnp.float32)
    if pieces:
        drawn = drawn * levels(stream_key, extent, pieces, -0.22, 0.18)
    return jnp.clip(drawn, -bound, bound).astype(kind)


def setup_inputs(seed: int = 0) -> dict:
    arg_keys = jax.random.split(jax.random.key(seed), 10)
    queries = draw_queries(jax.random.fold_in(arg_keys[9], 71), 0)
    new_keys = draw_new_keys(jax.random.fold_in(arg_keys[9], 71), 0)
    new_values = gaussian(arg_keys[2], (Q_TOTAL, KVH * DH), 1.0, 6.0, ((0, 32), (1, 4)))
    cache_keys = gaussian(arg_keys[3], (N_CTX * TILES * TILE, KVH * DH), 1.0, 6.0, ((0, 32), (1, 4)))
    cache_values = gaussian(arg_keys[4], (N_CTX * TILES * TILE, KVH * DH), 1.0, 6.0, ((0, 32), (1, 4)))
    keep_tiles = draw_keep_tiles(jax.random.fold_in(arg_keys[9], 71), 0)
    tile_count = draw_tile_count(jax.random.fold_in(arg_keys[9], 71), 0)
    owner_slot = jax.random.permutation(arg_keys[7], N_CTX).astype(jnp.int32)
    out_weight = gaussian(arg_keys[8], (HQ * DH, D), (HQ * DH) ** -0.5, 0.0625, ((0, 4), (1, 32)))
    return dict(queries=queries, new_keys=new_keys, new_values=new_values, cache_keys=cache_keys, cache_values=cache_values, keep_tiles=keep_tiles, tile_count=tile_count, owner_slot=owner_slot, out_weight=out_weight)


def reference(queries, new_keys, new_values, cache_keys, cache_values, keep_tiles, tile_count, owner_slot, out_weight):
    group_size = HQ // KVH
    score_scale = DH ** -0.5
    row_ids = jnp.arange(Q_TOTAL, dtype=jnp.int32)
    place = owner_slot[row_ids // Q_DEV] * Q_DEV + row_ids % Q_DEV
    tiled_keys = cache_keys.reshape(N_CTX, TILES, TILE, KVH, DH)
    tiled_values = cache_values.reshape(N_CTX, TILES, TILE, KVH, DH)
    owner_ids = jnp.arange(N_CTX, dtype=jnp.int32)[:, None]
    live_slots = jnp.arange(CAP, dtype=jnp.int32)[None, None, :] < tile_count[:, :, None]
    head_outputs = []
    for kv_head in range(KVH):
        head_keys = tiled_keys[:, :, :, kv_head, :]
        head_values = tiled_values[:, :, :, kv_head, :]
        kept_keys = head_keys[owner_ids, keep_tiles[:, kv_head, :]].reshape(-1, DH)
        kept_values = head_values[owner_ids, keep_tiles[:, kv_head, :]].reshape(-1, DH)
        all_keys = jnp.concatenate([kept_keys, new_keys[:, kv_head * DH:(kv_head + 1) * DH]], 0).astype(jnp.float32)
        all_values = jnp.concatenate([kept_values, new_values[:, kv_head * DH:(kv_head + 1) * DH]], 0).astype(jnp.float32)
        key_live = jnp.repeat(live_slots[:, kv_head, :].reshape(-1), TILE)
        query_head = queries[:, kv_head * group_size * DH:(kv_head + 1) * group_size * DH]
        query_head = query_head.reshape(N_CTX, Q_DEV, group_size, DH)

        def one_block(inputs, all_keys=all_keys, all_values=all_values, key_live=key_live):
            query_block, place_block = inputs
            scores = jnp.einsum("rhd,kd->rhk", query_block.astype(jnp.float32), all_keys) * score_scale
            cached_ok = jnp.broadcast_to(key_live[None, :], (Q_DEV, key_live.shape[0]))
            fresh_ok = place_block[:, None] >= place[None, :]
            allowed = jnp.concatenate([cached_ok, fresh_ok], 1)
            scores = jnp.where(allowed[:, None, :], scores, -jnp.inf)
            top_score = jnp.max(scores, axis=-1, keepdims=True)
            weights = jnp.exp(scores - top_score)
            totals = jnp.sum(weights, axis=-1)
            rounded = lax.optimization_barrier(weights.astype(jnp.bfloat16)).astype(jnp.float32)
            numerator = jnp.einsum("rhk,kd->rhd", rounded, all_values)
            return (numerator / totals[..., None]).astype(jnp.bfloat16)

        attn_head = lax.map(one_block, (query_head, place.reshape(N_CTX, Q_DEV)))
        head_outputs.append(attn_head.reshape(Q_TOTAL, group_size * DH))
    attn = jnp.concatenate(head_outputs, 1)
    return jnp.dot(attn, out_weight, preferred_element_type=jnp.float32)
```

```python
import functools

import jax
import jax.numpy as jnp
from jax import lax
from jax.experimental import pallas as pl
from jax.experimental.pallas import tpu as pltpu
from jax.sharding import PartitionSpec as P

DH = 128
TILE = 128
TB = 4
MESH = pl.DeviceIdType.MESH

NEG_INF = -jnp.inf


def push_kernel(axis, n, per_dest, count, *refs):
    x_refs = refs[:count]
    y_refs = refs[count : 2 * count]
    send_sem, recv_sem, local_sem = refs[2 * count :]
    me = lax.axis_index(axis)
    barrier = pltpu.get_barrier_semaphore()
    for k in range(1, n):
        peer = lax.rem(me + k, n)
        pl.semaphore_signal(barrier, inc=1, device_id={axis: peer}, device_id_type=MESH)
    pl.semaphore_wait(barrier, n - 1)
    copies = []
    for a in range(count):
        for k in range(1, n):
            peer = lax.rem(me + k, n)
            src = x_refs[a].at[peer] if per_dest else x_refs[a]
            copy = pltpu.make_async_remote_copy(
                src_ref=src,
                dst_ref=y_refs[a].at[me],
                send_sem=send_sem.at[a, k],
                recv_sem=recv_sem.at[a, k],
                device_id={axis: peer},
                device_id_type=MESH,
            )
            copy.start()
            copies.append(copy)
    locals_ = []
    for a in range(count):
        src = x_refs[a].at[me] if per_dest else x_refs[a]
        local = pltpu.make_async_copy(src, y_refs[a].at[me], local_sem.at[a])
        local.start()
        locals_.append(local)
    for local in locals_:
        local.wait()
    for copy in copies:
        copy.wait()


def push(xs, axis, n, per_dest, collective_id):
    count = len(xs)
    out_shape = []
    for x in xs:
        block = x.shape[1:] if per_dest else x.shape
        out_shape.append(jax.ShapeDtypeStruct((n,) + tuple(block), x.dtype))
    any_spec = pl.BlockSpec(memory_space=pl.ANY)
    return pl.pallas_call(
        functools.partial(push_kernel, axis, n, per_dest, count),
        out_shape=tuple(out_shape),
        in_specs=[any_spec] * count,
        out_specs=tuple([any_spec] * count),
        scratch_shapes=[
            pltpu.SemaphoreType.DMA((count, n)),
            pltpu.SemaphoreType.DMA((count, n)),
            pltpu.SemaphoreType.DMA((count,)),
        ],
        compiler_params=pltpu.CompilerParams(collective_id=collective_id, has_side_effects=True),
    )(*xs)


def fold_scores(state_now, scores, value_rows):
    run_max, run_total, run_sum = state_now
    new_max = jnp.maximum(run_max, jnp.max(scores, axis=-1))
    shrink = jnp.exp(run_max - new_max)
    weights = jnp.exp(scores - new_max[..., None])
    run_total = run_total * shrink + jnp.sum(weights, axis=-1)
    mixture = jnp.einsum(
        "rhk,kd->rhd", weights.astype(jnp.bfloat16), value_rows, preferred_element_type=jnp.float32
    )
    run_sum = run_sum * shrink[..., None] + mixture
    return (new_max, run_total, run_sum)


def body(
    queries,
    new_keys,
    new_values,
    cache_keys,
    cache_values,
    keep_tiles,
    tile_count,
    owner_slot,
    out_weight,
):
    q_dev = queries.shape[0]
    kv_local = new_keys.shape[1] // DH
    q_local = queries.shape[1] // DH
    group_size = q_local // kv_local
    ctx_count = lax.axis_size("ctx")
    tp_count = lax.axis_size("tp")
    total_rows = q_dev * ctx_count
    my_index = lax.axis_index("ctx")
    score_scale = DH ** (-0.5)
    slot_count = keep_tiles.shape[2]
    key_place = owner_slot[my_index] * q_dev + jnp.arange(q_dev, dtype=jnp.int32)
    tiled_keys = cache_keys.reshape(-1, TILE, kv_local, DH)
    tiled_values = cache_values.reshape(-1, TILE, kv_local, DH)
    kept_keys = [
        jnp.take(tiled_keys[:, :, kv_head, :], keep_tiles[0, kv_head], axis=0)
        for kv_head in range(kv_local)
    ]
    kept_values = [
        jnp.take(tiled_values[:, :, kv_head, :], keep_tiles[0, kv_head], axis=0)
        for kv_head in range(kv_local)
    ]
    (query_blocks,) = push((queries,), "ctx", ctx_count, False, 0)
    query_rows = query_blocks.reshape(total_rows, queries.shape[1])
    row_count = query_rows.shape[0]
    row_ids = jnp.arange(row_count, dtype=jnp.int32)
    query_place = owner_slot[row_ids // q_dev] * q_dev + row_ids % q_dev
    causal = query_place[:, None] >= key_place[None, :]
    pieces_max = []
    pieces_total = []
    pieces_sum = []
    for kv_head in range(kv_local):
        query_head = query_rows[
            :, kv_head * group_size * DH : (kv_head + 1) * group_size * DH
        ].reshape(row_count, group_size, DH)
        start_state = (
            jnp.full((row_count, group_size), NEG_INF, jnp.float32),
            jnp.zeros((row_count, group_size), jnp.float32),
            jnp.zeros((row_count, group_size, DH), jnp.float32),
        )
        live_count = tile_count[0, kv_head]

        def tile_block(
            block_id, state_inner, kv_head=kv_head, query_head=query_head, live_count=live_count
        ):
            key_block = lax.dynamic_slice_in_dim(kept_keys[kv_head], block_id * TB, TB, 0).reshape(
                TB * TILE, DH
            )
            value_block = lax.dynamic_slice_in_dim(
                kept_values[kv_head], block_id * TB, TB, 0
            ).reshape(TB * TILE, DH)
            tile_ids = block_id * TB + jnp.arange(TB, dtype=jnp.int32)
            live_keys = jnp.repeat(tile_ids < live_count, TILE)
            scores = (
                jnp.einsum("rhd,kd->rhk", query_head, key_block, preferred_element_type=jnp.float32)
                * score_scale
            )
            scores = jnp.where(live_keys[None, None, :], scores, NEG_INF)
            return fold_scores(state_inner, scores, value_block)

        block_limit = slot_count // TB
        state_head = lax.fori_loop(0, block_limit, tile_block, start_state)
        fresh_keys = new_keys[:, kv_head * DH : (kv_head + 1) * DH]
        fresh_values = new_values[:, kv_head * DH : (kv_head + 1) * DH]
        scores = (
            jnp.einsum("rhd,kd->rhk", query_head, fresh_keys, preferred_element_type=jnp.float32)
            * score_scale
        )
        scores = jnp.where(causal[:, None, :], scores, NEG_INF)
        head_max, head_total, head_sum = fold_scores(state_head, scores, fresh_values)
        pieces_max.append(head_max)
        pieces_total.append(head_total)
        pieces_sum.append(head_sum.reshape(row_count, group_size * DH))
    maxima_all = jnp.concatenate(pieces_max, axis=1).reshape(ctx_count, q_dev, q_local)
    totals_all = jnp.concatenate(pieces_total, axis=1).reshape(ctx_count, q_dev, q_local)
    sums_all = jnp.concatenate(pieces_sum, axis=1).reshape(ctx_count, q_dev, q_local * DH)
    part_max, part_total, part_sum = push((maxima_all, totals_all, sums_all), "ctx", ctx_count, True, 1)
    top_max = jnp.max(part_max, axis=0)
    factor = jnp.exp(part_max - top_max[None])
    denominator = jnp.sum(part_total * factor, axis=0)
    numerator = jnp.sum(
        part_sum.reshape(ctx_count, q_dev, q_local, DH) * factor[..., None], axis=0
    )
    attn_rows = (
        (numerator / denominator[..., None]).reshape(q_dev, q_local * DH).astype(jnp.bfloat16)
    )
    (attn_blocks,) = push((attn_rows,), "ctx", ctx_count, False, 2)
    projected = jnp.dot(
        attn_blocks.reshape(total_rows, q_local * DH),
        out_weight,
        preferred_element_type=jnp.float32,
    )
    out_rows = total_rows // tp_count
    (proj_parts,) = push(
        (projected.reshape(tp_count, out_rows, projected.shape[1]),), "tp", tp_count, True, 3
    )
    return jnp.sum(proj_parts, axis=0)


def solution(mesh):
    return jax.shard_map(
        body,
        mesh=mesh,
        in_specs=(
            P("ctx", "tp"),
            P("ctx", "tp"),
            P("ctx", "tp"),
            P("ctx", "tp"),
            P("ctx", "tp"),
            P("ctx", "tp", None),
            P("ctx", "tp"),
            P(),
            P("tp", "ctx"),
        ),
        out_specs=P("tp", "ctx"),
        check_vma=False,
    )
```

```python
import functools

import jax
import jax.numpy as jnp
from jax import lax
from jax.experimental import pallas as pl
from jax.experimental.pallas import tpu as pltpu
from jax.sharding import PartitionSpec as P

DH = 128
TILE = 128
TB = 4
MESH = pl.DeviceIdType.MESH

NEG_INF = -jnp.inf


def push_kernel(axis, n, per_dest, count, *refs):
    x_refs = refs[:count]
    y_refs = refs[count : 2 * count]
    send_sem, recv_sem, local_sem = refs[2 * count :]
    me = lax.axis_index(axis)
    barrier = pltpu.get_barrier_semaphore()
    for k in range(1, n):
        peer = lax.rem(me + k, n)
        pl.semaphore_signal(barrier, inc=1, device_id={axis: peer}, device_id_type=MESH)
    pl.semaphore_wait(barrier, n - 1)
    copies = []
    for a in range(count):
        for k in range(1, n):
            peer = lax.rem(me + k, n)
            src = x_refs[a].at[peer] if per_dest else x_refs[a]
            copy = pltpu.make_async_remote_copy(
                src_ref=src,
                dst_ref=y_refs[a].at[me],
                send_sem=send_sem.at[a, k],
                recv_sem=recv_sem.at[a, k],
                device_id={axis: peer},
                device_id_type=MESH,
            )
            copy.start()
            copies.append(copy)
    locals_ = []
    for a in range(count):
        src = x_refs[a].at[me] if per_dest else x_refs[a]
        local = pltpu.make_async_copy(src, y_refs[a].at[me], local_sem.at[a])
        local.start()
        locals_.append(local)
    for local in locals_:
        local.wait()
    for copy in copies:
        copy.wait()


def push(xs, axis, n, per_dest, collective_id):
    count = len(xs)
    out_shape = []
    for x in xs:
        block = x.shape[1:] if per_dest else x.shape
        out_shape.append(jax.ShapeDtypeStruct((n,) + tuple(block), x.dtype))
    any_spec = pl.BlockSpec(memory_space=pl.ANY)
    return pl.pallas_call(
        functools.partial(push_kernel, axis, n, per_dest, count),
        out_shape=tuple(out_shape),
        in_specs=[any_spec] * count,
        out_specs=tuple([any_spec] * count),
        scratch_shapes=[
            pltpu.SemaphoreType.DMA((count, n)),
            pltpu.SemaphoreType.DMA((count, n)),
            pltpu.SemaphoreType.DMA((count,)),
        ],
        compiler_params=pltpu.CompilerParams(collective_id=collective_id, has_side_effects=True),
    )(*xs)


TPB = 4


def dot_nt(a, b):
    return lax.dot_general(a, b, (((1,), (1,)), ((), ())), preferred_element_type=jnp.float32)


def attn_kernel(tpb, group_size, kt_ref, cnt_ref, q_ref, *refs):
    k_refs = refs[:tpb]
    v_refs = refs[tpb : 2 * tpb]
    nk_ref, nv_ref, qp_ref, kp_ref = refs[2 * tpb : 2 * tpb + 4]
    acc_ref, m_out, l_out = refs[2 * tpb + 4 : 2 * tpb + 7]
    m_scr, l_scr = refs[2 * tpb + 7 :]
    g = pl.program_id(0)
    t = pl.program_id(1)
    last = pl.num_programs(1) - 1
    live = cnt_ref[g]
    scale = DH ** (-0.5)

    @pl.when(t == 0)
    def _():
        m_scr[...] = jnp.full(m_scr.shape, NEG_INF, jnp.float32)
        l_scr[...] = jnp.zeros(l_scr.shape, jnp.float32)
        acc_ref[...] = jnp.zeros(acc_ref.shape, jnp.float32)

    def fold(h, keys, values, masks):
        cols = pl.ds(pl.multiple_of(h * DH, DH), DH)
        q = q_ref[:, cols]
        scores = [dot_nt(q, k) * scale + mk for k, mk in zip(keys, masks)]
        m_prev = m_scr[h]
        m_cur = scores[0].max(axis=1, keepdims=True)
        for s in scores[1:]:
            m_cur = jnp.maximum(m_cur, s.max(axis=1, keepdims=True))
        m_new = jnp.maximum(m_prev, m_cur)
        alpha = jnp.exp(m_prev - m_new)
        m_col = m_new[:, :1]
        total = l_scr[h] * alpha
        acc = acc_ref[:, cols] * alpha[:, :1]
        for s, v in zip(scores, values):
            p = jnp.exp(s - m_col)
            total = total + p.sum(axis=1, keepdims=True)
            acc = acc + jnp.dot(p.astype(jnp.bfloat16), v, preferred_element_type=jnp.float32)
        m_scr[h] = m_new
        l_scr[h] = total
        acc_ref[:, cols] = acc

    @pl.when(t * tpb < live)
    def _():
        keys = [k[...] for k in k_refs]
        values = [v[...] for v in v_refs]
        masks = [
            jnp.where(t * tpb + j < live, 0.0, NEG_INF).astype(jnp.float32) for j in range(tpb)
        ]

        def head_body(h, carry):
            fold(h, keys, values, masks)
            return carry

        lax.fori_loop(0, group_size, head_body, 0)

    @pl.when(t == last)
    def _():
        causal = jnp.where(qp_ref[...] >= kp_ref[...], 0.0, NEG_INF).astype(jnp.float32)
        nk = nk_ref[...]
        nv = nv_ref[...]

        def head_body(h, carry):
            fold(h, [nk], [nv], [causal])
            return carry

        lax.fori_loop(0, group_size, head_body, 0)
        for h in range(group_size):
            m_out[:, h : h + 1] = m_scr[h][:, :1]
            l_out[:, h : h + 1] = l_scr[h][:, :1]


def local_attention(query_rows, cache_keys, cache_values, new_keys, new_values, keep, live, query_place, key_place):
    rows, width = query_rows.shape
    kv_local = new_keys.shape[1] // DH
    group_size = width // DH // kv_local
    slots = keep.shape[1]
    steps = slots // TPB
    q_new = new_keys.shape[0]

    def tile_map(j):
        def index_map(g, t, kt_ref, cnt_ref):
            return (kt_ref[g, jnp.minimum(t * TPB + j, cnt_ref[g] - 1)], g)

        return index_map

    tile_spec = [pl.BlockSpec((TILE, DH), tile_map(j)) for j in range(TPB)]
    grid_spec = pltpu.PrefetchScalarGridSpec(
        num_scalar_prefetch=2,
        grid=(kv_local, steps),
        in_specs=[pl.BlockSpec((rows, group_size * DH), lambda g, t, kt, cn: (0, g))]
        + tile_spec
        + tile_spec
        + [
            pl.BlockSpec((q_new, DH), lambda g, t, kt, cn: (0, g)),
            pl.BlockSpec((q_new, DH), lambda g, t, kt, cn: (0, g)),
            pl.BlockSpec((rows, 1), lambda g, t, kt, cn: (0, 0)),
            pl.BlockSpec((1, q_new), lambda g, t, kt, cn: (0, 0)),
        ],
        out_specs=[
            pl.BlockSpec((rows, group_size * DH), lambda g, t, kt, cn: (0, g)),
            pl.BlockSpec((None, rows, group_size), lambda g, t, kt, cn: (g, 0, 0)),
            pl.BlockSpec((None, rows, group_size), lambda g, t, kt, cn: (g, 0, 0)),
        ],
        scratch_shapes=[
            pltpu.VMEM((group_size, rows, DH), jnp.float32),
            pltpu.VMEM((group_size, rows, DH), jnp.float32),
        ],
    )
    keys_total = slots * TILE + q_new
    flops = 4 * rows * kv_local * group_size * keys_total * DH
    cost = pl.CostEstimate(
        flops=flops,
        transcendentals=rows * kv_local * group_size * keys_total,
        bytes_accessed=rows * width * 2 + rows * width * 4 + 2 * kv_local * slots * TILE * DH * 2,
    )
    return pl.pallas_call(
        functools.partial(attn_kernel, TPB, group_size),
        grid_spec=grid_spec,
        out_shape=[
            jax.ShapeDtypeStruct((rows, width), jnp.float32),
            jax.ShapeDtypeStruct((kv_local, rows, group_size), jnp.float32),
            jax.ShapeDtypeStruct((kv_local, rows, group_size), jnp.float32),
        ],
        compiler_params=pltpu.CompilerParams(
            dimension_semantics=("arbitrary", "arbitrary"), vmem_limit_bytes=56 * 1024 * 1024
        ),
        cost_estimate=cost,
    )(keep, live, query_rows, *([cache_keys] * TPB), *([cache_values] * TPB), new_keys, new_values, query_place, key_place)


def body(
    queries,
    new_keys,
    new_values,
    cache_keys,
    cache_values,
    keep_tiles,
    tile_count,
    owner_slot,
    out_weight,
):
    q_dev = queries.shape[0]
    kv_local = new_keys.shape[1] // DH
    q_local = queries.shape[1] // DH
    group_size = q_local // kv_local
    ctx_count = lax.axis_size("ctx")
    tp_count = lax.axis_size("tp")
    total_rows = q_dev * ctx_count
    my_index = lax.axis_index("ctx")
    key_place = owner_slot[my_index] * q_dev + jnp.arange(q_dev, dtype=jnp.int32)
    (query_blocks,) = push((queries,), "ctx", ctx_count, False, 0)
    query_rows = query_blocks.reshape(total_rows, queries.shape[1])
    row_ids = jnp.arange(total_rows, dtype=jnp.int32)
    query_place = owner_slot[row_ids // q_dev] * q_dev + row_ids % q_dev
    sums_all, maxima, totals = local_attention(
        query_rows,
        cache_keys,
        cache_values,
        new_keys,
        new_values,
        keep_tiles[0],
        tile_count[0],
        query_place.reshape(total_rows, 1),
        key_place.reshape(1, q_dev),
    )
    maxima_all = jnp.transpose(maxima, (1, 0, 2)).reshape(ctx_count, q_dev, q_local)
    totals_all = jnp.transpose(totals, (1, 0, 2)).reshape(ctx_count, q_dev, q_local)
    sums_all = sums_all.reshape(ctx_count, q_dev, q_local * DH)
    part_max, part_total, part_sum = push((maxima_all, totals_all, sums_all), "ctx", ctx_count, True, 1)
    top_max = jnp.max(part_max, axis=0)
    factor = jnp.exp(part_max - top_max[None])
    denominator = jnp.sum(part_total * factor, axis=0)
    numerator = jnp.sum(
        part_sum.reshape(ctx_count, q_dev, q_local, DH) * factor[..., None], axis=0
    )
    attn_rows = (
        (numerator / denominator[..., None]).reshape(q_dev, q_local * DH).astype(jnp.bfloat16)
    )
    (attn_blocks,) = push((attn_rows,), "ctx", ctx_count, False, 2)
    projected = jnp.dot(
        attn_blocks.reshape(total_rows, q_local * DH),
        out_weight,
        preferred_element_type=jnp.float32,
    )
    out_rows = total_rows // tp_count
    (proj_parts,) = push(
        (projected.reshape(tp_count, out_rows, projected.shape[1]),), "tp", tp_count, True, 3
    )
    return jnp.sum(proj_parts, axis=0)


def solution(mesh):
    return jax.shard_map(
        body,
        mesh=mesh,
        in_specs=(
            P("ctx", "tp"),
            P("ctx", "tp"),
            P("ctx", "tp"),
            P("ctx", "tp"),
            P("ctx", "tp"),
            P("ctx", "tp", None),
            P("ctx", "tp"),
            P(),
            P("tp", "ctx"),
        ),
        out_specs=P("tp", "ctx"),
        check_vma=False,
    )
```

```python
import functools

import jax
import jax.numpy as jnp
from jax import lax
from jax.experimental import pallas as pl
from jax.experimental.pallas import tpu as pltpu
from jax.sharding import PartitionSpec as P

DH = 128
TILE = 128
TB = 4
MESH = pl.DeviceIdType.MESH

NEG_INF = -jnp.inf


def push_kernel(axis, n, per_dest, count, *refs):
    x_refs = refs[:count]
    y_refs = refs[count : 2 * count]
    send_sem, recv_sem, local_sem = refs[2 * count :]
    me = lax.axis_index(axis)
    barrier = pltpu.get_barrier_semaphore()
    for k in range(1, n):
        peer = lax.rem(me + k, n)
        pl.semaphore_signal(barrier, inc=1, device_id={axis: peer}, device_id_type=MESH)
    pl.semaphore_wait(barrier, n - 1)
    copies = []
    for a in range(count):
        for k in range(1, n):
            peer = lax.rem(me + k, n)
            src = x_refs[a].at[peer] if per_dest else x_refs[a]
            copy = pltpu.make_async_remote_copy(
                src_ref=src,
                dst_ref=y_refs[a].at[me],
                send_sem=send_sem.at[a, k],
                recv_sem=recv_sem.at[a, k],
                device_id={axis: peer},
                device_id_type=MESH,
            )
            copy.start()
            copies.append(copy)
    locals_ = []
    for a in range(count):
        src = x_refs[a].at[me] if per_dest else x_refs[a]
        local = pltpu.make_async_copy(src, y_refs[a].at[me], local_sem.at[a])
        local.start()
        locals_.append(local)
    for local in locals_:
        local.wait()
    for copy in copies:
        copy.wait()


def push(xs, axis, n, per_dest, collective_id):
    count = len(xs)
    out_shape = []
    for x in xs:
        block = x.shape[1:] if per_dest else x.shape
        out_shape.append(jax.ShapeDtypeStruct((n,) + tuple(block), x.dtype))
    any_spec = pl.BlockSpec(memory_space=pl.ANY)
    return pl.pallas_call(
        functools.partial(push_kernel, axis, n, per_dest, count),
        out_shape=tuple(out_shape),
        in_specs=[any_spec] * count,
        out_specs=tuple([any_spec] * count),
        scratch_shapes=[
            pltpu.SemaphoreType.DMA((count, n)),
            pltpu.SemaphoreType.DMA((count, n)),
            pltpu.SemaphoreType.DMA((count,)),
        ],
        compiler_params=pltpu.CompilerParams(collective_id=collective_id, has_side_effects=True),
    )(*xs)


TPB = 8
LOG2E = 1.4426950408889634


def dot_nt(a, b):
    return lax.dot_general(a, b, (((1,), (1,)), ((), ())), preferred_element_type=jnp.float32)


def attn_kernel(tpb, group_size, kt_ref, cnt_ref, q_ref, *refs):
    k_refs = refs[:tpb]
    v_refs = refs[tpb : 2 * tpb]
    nk_ref, nv_ref, qp_ref, kp_ref = refs[2 * tpb : 2 * tpb + 4]
    sum_out, m_out, l_out = refs[2 * tpb + 4 : 2 * tpb + 7]
    m_scr, l_scr, acc_ref = refs[2 * tpb + 7 :]
    g = pl.program_id(0)
    t = pl.program_id(1)
    last = pl.num_programs(1) - 1
    live = cnt_ref[g]
    coef = DH ** (-0.5) * LOG2E

    @pl.when(t == 0)
    def _():
        m_scr[...] = jnp.full(m_scr.shape, NEG_INF, jnp.float32)
        l_scr[...] = jnp.zeros(l_scr.shape, jnp.float32)
        acc_ref[...] = jnp.zeros(acc_ref.shape, jnp.float32)

    def fold(h, keys, values, masks):
        cols = pl.ds(pl.multiple_of(h * DH, DH), DH)
        q = q_ref[:, cols]
        scores = []
        for j, k in enumerate(keys):
            s = dot_nt(q, k)
            if masks is not None:
                s = s + masks[j]
            scores.append(s)
        top = scores[0]
        for s in scores[1:]:
            top = jnp.maximum(top, s)
        m_prev = m_scr[h]
        m_new = jnp.maximum(m_prev, top.max(axis=1, keepdims=True))
        alpha = jnp.exp2((m_prev - m_new) * coef)
        shift = m_new[:, :1] * coef
        acc = acc_ref[:, cols] * alpha[:, :1]
        psum = None
        for s, v in zip(scores, values):
            p = jnp.exp2(s * coef - shift)
            psum = p if psum is None else psum + p
            acc = acc + jnp.dot(p.astype(jnp.bfloat16), v, preferred_element_type=jnp.float32)
        m_scr[h] = m_new
        l_scr[h] = l_scr[h] * alpha + psum.sum(axis=1, keepdims=True)
        acc_ref[:, cols] = acc

    def tiles_step(masked):
        keys = [k[...] for k in k_refs]
        values = [v[...] for v in v_refs]
        masks = None
        if masked:
            masks = [
                jnp.where(t * tpb + j < live, 0.0, NEG_INF).astype(jnp.float32) for j in range(tpb)
            ]

        def head_body(h, carry):
            fold(h, keys, values, masks)
            return carry

        lax.fori_loop(0, group_size, head_body, 0)

    @pl.when((t + 1) * tpb <= live)
    def _():
        tiles_step(False)

    @pl.when(jnp.logical_and(t * tpb < live, (t + 1) * tpb > live))
    def _():
        tiles_step(True)

    @pl.when(t == last)
    def _():
        causal = jnp.where(qp_ref[...] >= kp_ref[...], 0.0, NEG_INF).astype(jnp.float32)
        nk = nk_ref[...]
        nv = nv_ref[...]

        def head_body(h, carry):
            fold(h, [nk], [nv], [causal])
            return carry

        lax.fori_loop(0, group_size, head_body, 0)
        sum_out[...] = acc_ref[...].astype(sum_out.dtype)
        for h in range(group_size):
            m_out[:, h : h + 1] = m_scr[h][:, :1]
            l_out[:, h : h + 1] = l_scr[h][:, :1]


def local_attention(query_rows, cache_keys, cache_values, new_keys, new_values, keep, live, query_place, key_place):
    rows, width = query_rows.shape
    kv_local = new_keys.shape[1] // DH
    group_size = width // DH // kv_local
    slots = keep.shape[1]
    steps = slots // TPB
    q_new = new_keys.shape[0]

    def tile_map(j):
        def index_map(g, t, kt_ref, cnt_ref):
            return (kt_ref[g, jnp.minimum(t * TPB + j, cnt_ref[g] - 1)], g)

        return index_map

    tile_spec = [pl.BlockSpec((TILE, DH), tile_map(j)) for j in range(TPB)]
    grid_spec = pltpu.PrefetchScalarGridSpec(
        num_scalar_prefetch=2,
        grid=(kv_local, steps),
        in_specs=[pl.BlockSpec((rows, group_size * DH), lambda g, t, kt, cn: (0, g))]
        + tile_spec
        + tile_spec
        + [
            pl.BlockSpec((q_new, DH), lambda g, t, kt, cn: (0, g)),
            pl.BlockSpec((q_new, DH), lambda g, t, kt, cn: (0, g)),
            pl.BlockSpec((rows, 1), lambda g, t, kt, cn: (0, 0)),
            pl.BlockSpec((1, q_new), lambda g, t, kt, cn: (0, 0)),
        ],
        out_specs=[
            pl.BlockSpec((rows, group_size * DH), lambda g, t, kt, cn: (0, g)),
            pl.BlockSpec((None, rows, group_size), lambda g, t, kt, cn: (g, 0, 0)),
            pl.BlockSpec((None, rows, group_size), lambda g, t, kt, cn: (g, 0, 0)),
        ],
        scratch_shapes=[
            pltpu.VMEM((group_size, rows, DH), jnp.float32),
            pltpu.VMEM((group_size, rows, DH), jnp.float32),
            pltpu.VMEM((rows, group_size * DH), jnp.float32),
        ],
    )
    keys_total = slots * TILE + q_new
    flops = 4 * rows * kv_local * group_size * keys_total * DH
    cost = pl.CostEstimate(
        flops=flops,
        transcendentals=rows * kv_local * group_size * keys_total,
        bytes_accessed=rows * width * 2 + rows * width * 4 + 2 * kv_local * slots * TILE * DH * 2,
    )
    return pl.pallas_call(
        functools.partial(attn_kernel, TPB, group_size),
        grid_spec=grid_spec,
        out_shape=[
            jax.ShapeDtypeStruct((rows, width), jnp.bfloat16),
            jax.ShapeDtypeStruct((kv_local, rows, group_size), jnp.float32),
            jax.ShapeDtypeStruct((kv_local, rows, group_size), jnp.float32),
        ],
        compiler_params=pltpu.CompilerParams(
            dimension_semantics=("arbitrary", "arbitrary"), vmem_limit_bytes=56 * 1024 * 1024
        ),
        cost_estimate=cost,
    )(keep, live, query_rows, *([cache_keys] * TPB), *([cache_values] * TPB), new_keys, new_values, query_place, key_place)


def body(
    queries,
    new_keys,
    new_values,
    cache_keys,
    cache_values,
    keep_tiles,
    tile_count,
    owner_slot,
    out_weight,
):
    q_dev = queries.shape[0]
    kv_local = new_keys.shape[1] // DH
    q_local = queries.shape[1] // DH
    group_size = q_local // kv_local
    ctx_count = lax.axis_size("ctx")
    tp_count = lax.axis_size("tp")
    total_rows = q_dev * ctx_count
    my_index = lax.axis_index("ctx")
    key_place = owner_slot[my_index] * q_dev + jnp.arange(q_dev, dtype=jnp.int32)
    (query_blocks,) = push((queries,), "ctx", ctx_count, False, 0)
    query_rows = query_blocks.reshape(total_rows, queries.shape[1])
    row_ids = jnp.arange(total_rows, dtype=jnp.int32)
    query_place = owner_slot[row_ids // q_dev] * q_dev + row_ids % q_dev
    sums_all, maxima, totals = local_attention(
        query_rows,
        cache_keys,
        cache_values,
        new_keys,
        new_values,
        keep_tiles[0],
        tile_count[0],
        query_place.reshape(total_rows, 1),
        key_place.reshape(1, q_dev),
    )
    maxima_all = jnp.transpose(maxima, (1, 0, 2)).reshape(ctx_count, q_dev, q_local)
    totals_all = jnp.transpose(totals, (1, 0, 2)).reshape(ctx_count, q_dev, q_local)
    sums_all = sums_all.reshape(ctx_count, q_dev, q_local * DH)
    part_max, part_total, part_sum = push((maxima_all, totals_all, sums_all), "ctx", ctx_count, True, 1)
    top_max = jnp.max(part_max, axis=0)
    factor = jnp.exp2((part_max - top_max[None]) * (DH ** (-0.5) * LOG2E))
    denominator = jnp.sum(part_total * factor, axis=0)
    numerator = jnp.sum(
        part_sum.reshape(ctx_count, q_dev, q_local, DH).astype(jnp.float32) * factor[..., None],
        axis=0,
    )
    attn_rows = (
        (numerator / denominator[..., None]).reshape(q_dev, q_local * DH).astype(jnp.bfloat16)
    )
    (attn_blocks,) = push((attn_rows,), "ctx", ctx_count, False, 2)
    projected = jnp.dot(
        attn_blocks.reshape(total_rows, q_local * DH),
        out_weight,
        preferred_element_type=jnp.float32,
    )
    out_rows = total_rows // tp_count
    (proj_parts,) = push(
        (projected.reshape(tp_count, out_rows, projected.shape[1]),), "tp", tp_count, True, 3
    )
    return jnp.sum(proj_parts, axis=0)


def solution(mesh):
    return jax.shard_map(
        body,
        mesh=mesh,
        in_specs=(
            P("ctx", "tp"),
            P("ctx", "tp"),
            P("ctx", "tp"),
            P("ctx", "tp"),
            P("ctx", "tp"),
            P("ctx", "tp", None),
            P("ctx", "tp"),
            P(),
            P("tp", "ctx"),
        ),
        out_specs=P("tp", "ctx"),
        check_vma=False,
    )
```

```python
import functools

import jax
import jax.numpy as jnp
from jax import lax
from jax.experimental import pallas as pl
from jax.experimental.pallas import tpu as pltpu
from jax.sharding import PartitionSpec as P

DH = 128
TILE = 128
TB = 4
MESH = pl.DeviceIdType.MESH

NEG_INF = -jnp.inf


def push_kernel(axis, n, per_dest, count, *refs):
    x_refs = refs[:count]
    y_refs = refs[count : 2 * count]
    send_sem, recv_sem, local_sem = refs[2 * count :]
    me = lax.axis_index(axis)
    barrier = pltpu.get_barrier_semaphore()
    for k in range(1, n):
        peer = lax.rem(me + k, n)
        pl.semaphore_signal(barrier, inc=1, device_id={axis: peer}, device_id_type=MESH)
    pl.semaphore_wait(barrier, n - 1)
    copies = []
    for a in range(count):
        for k in range(1, n):
            peer = lax.rem(me + k, n)
            src = x_refs[a].at[peer] if per_dest else x_refs[a]
            copy = pltpu.make_async_remote_copy(
                src_ref=src,
                dst_ref=y_refs[a].at[me],
                send_sem=send_sem.at[a, k],
                recv_sem=recv_sem.at[a, k],
                device_id={axis: peer},
                device_id_type=MESH,
            )
            copy.start()
            copies.append(copy)
    locals_ = []
    for a in range(count):
        src = x_refs[a].at[me] if per_dest else x_refs[a]
        local = pltpu.make_async_copy(src, y_refs[a].at[me], local_sem.at[a])
        local.start()
        locals_.append(local)
    for local in locals_:
        local.wait()
    for copy in copies:
        copy.wait()


def push(xs, axis, n, per_dest, collective_id):
    count = len(xs)
    out_shape = []
    for x in xs:
        block = x.shape[1:] if per_dest else x.shape
        out_shape.append(jax.ShapeDtypeStruct((n,) + tuple(block), x.dtype))
    any_spec = pl.BlockSpec(memory_space=pl.ANY)
    return pl.pallas_call(
        functools.partial(push_kernel, axis, n, per_dest, count),
        out_shape=tuple(out_shape),
        in_specs=[any_spec] * count,
        out_specs=tuple([any_spec] * count),
        scratch_shapes=[
            pltpu.SemaphoreType.DMA((count, n)),
            pltpu.SemaphoreType.DMA((count, n)),
            pltpu.SemaphoreType.DMA((count,)),
        ],
        compiler_params=pltpu.CompilerParams(collective_id=collective_id, has_side_effects=True),
    )(*xs)


TPB = 8
LOG2E = 1.4426950408889634


def dot_nt(a, b):
    return lax.dot_general(a, b, (((1,), (1,)), ((), ())), preferred_element_type=jnp.float32)


def attn_kernel(tpb, group_size, kt_ref, cnt_ref, q_ref, *refs):
    k_refs = refs[:tpb]
    v_refs = refs[tpb : 2 * tpb]
    nk_ref, nv_ref, qp_ref, kp_ref = refs[2 * tpb : 2 * tpb + 4]
    sum_out, m_out, l_out = refs[2 * tpb + 4 : 2 * tpb + 7]
    m_scr, acc_ref = refs[2 * tpb + 7 :]
    g = pl.program_id(0)
    t = pl.program_id(1)
    last = pl.num_programs(1) - 1
    live = cnt_ref[g]
    coef = DH ** (-0.5) * LOG2E

    @pl.when(t == 0)
    def _():
        m_scr[...] = jnp.full(m_scr.shape, NEG_INF, jnp.float32)
        acc_ref[...] = jnp.zeros(acc_ref.shape, jnp.float32)

    def fold(h, keys, values_ext, mask):
        cols = pl.ds(pl.multiple_of(h * DH, DH), DH)
        s = dot_nt(q_ref[:, cols], keys)
        if mask is not None:
            s = s + mask
        m_prev = m_scr[h]
        m_new = jnp.maximum(m_prev, s.max(axis=1, keepdims=True))
        alpha = jnp.exp2((m_prev - m_new) * coef)
        p = jnp.exp2(s * coef - m_new[:, :1] * coef)
        m_scr[h] = m_new
        acc_ref[h] = acc_ref[h] * alpha[:, :1] + jnp.dot(
            p.astype(jnp.bfloat16), values_ext, preferred_element_type=jnp.float32
        )

    def with_ones(values):
        return jnp.concatenate([values, jnp.ones(values.shape, values.dtype)], axis=1)

    def tiles_step(masked):
        keys = jnp.concatenate([k[...] for k in k_refs], axis=0)
        values_ext = with_ones(jnp.concatenate([v[...] for v in v_refs], axis=0))
        mask = None
        if masked:
            slot = t * tpb + lax.broadcasted_iota(jnp.int32, (1, tpb * TILE), 1) // TILE
            mask = jnp.where(slot < live, 0.0, NEG_INF).astype(jnp.float32)

        def head_body(h, carry):
            fold(h, keys, values_ext, mask)
            return carry

        lax.fori_loop(0, group_size, head_body, 0)

    @pl.when((t + 1) * tpb <= live)
    def _():
        tiles_step(False)

    @pl.when(jnp.logical_and(t * tpb < live, (t + 1) * tpb > live))
    def _():
        tiles_step(True)

    @pl.when(t == last)
    def _():
        causal = jnp.where(qp_ref[...] >= kp_ref[...], 0.0, NEG_INF).astype(jnp.float32)
        nk = nk_ref[...]
        nv_ext = with_ones(nv_ref[...])

        def head_body(h, carry):
            fold(h, nk, nv_ext, causal)
            return carry

        lax.fori_loop(0, group_size, head_body, 0)
        for h in range(group_size):
            acc = acc_ref[h]
            sum_out[:, h * DH : (h + 1) * DH] = acc[:, :DH].astype(sum_out.dtype)
            m_out[:, h : h + 1] = m_scr[h][:, :1]
            l_out[:, h : h + 1] = acc[:, DH : DH + 1]


def local_attention(query_rows, cache_keys, cache_values, new_keys, new_values, keep, live, query_place, key_place):
    rows, width = query_rows.shape
    kv_local = new_keys.shape[1] // DH
    group_size = width // DH // kv_local
    slots = keep.shape[1]
    steps = slots // TPB
    q_new = new_keys.shape[0]

    def tile_map(j):
        def index_map(g, t, kt_ref, cnt_ref):
            return (kt_ref[g, jnp.minimum(t * TPB + j, cnt_ref[g] - 1)], g)

        return index_map

    tile_spec = [pl.BlockSpec((TILE, DH), tile_map(j)) for j in range(TPB)]
    grid_spec = pltpu.PrefetchScalarGridSpec(
        num_scalar_prefetch=2,
        grid=(kv_local, steps),
        in_specs=[pl.BlockSpec((rows, group_size * DH), lambda g, t, kt, cn: (0, g))]
        + tile_spec
        + tile_spec
        + [
            pl.BlockSpec((q_new, DH), lambda g, t, kt, cn: (0, g)),
            pl.BlockSpec((q_new, DH), lambda g, t, kt, cn: (0, g)),
            pl.BlockSpec((rows, 1), lambda g, t, kt, cn: (0, 0)),
            pl.BlockSpec((1, q_new), lambda g, t, kt, cn: (0, 0)),
        ],
        out_specs=[
            pl.BlockSpec((rows, group_size * DH), lambda g, t, kt, cn: (0, g)),
            pl.BlockSpec((None, rows, group_size), lambda g, t, kt, cn: (g, 0, 0)),
            pl.BlockSpec((None, rows, group_size), lambda g, t, kt, cn: (g, 0, 0)),
        ],
        scratch_shapes=[
            pltpu.VMEM((group_size, rows, DH), jnp.float32),
            pltpu.VMEM((group_size, rows, 2 * DH), jnp.float32),
        ],
    )
    keys_total = slots * TILE + q_new
    flops = 4 * rows * kv_local * group_size * keys_total * DH
    cost = pl.CostEstimate(
        flops=flops,
        transcendentals=rows * kv_local * group_size * keys_total,
        bytes_accessed=rows * width * 2 + rows * width * 4 + 2 * kv_local * slots * TILE * DH * 2,
    )
    return pl.pallas_call(
        functools.partial(attn_kernel, TPB, group_size),
        grid_spec=grid_spec,
        out_shape=[
            jax.ShapeDtypeStruct((rows, width), jnp.bfloat16),
            jax.ShapeDtypeStruct((kv_local, rows, group_size), jnp.float32),
            jax.ShapeDtypeStruct((kv_local, rows, group_size), jnp.float32),
        ],
        compiler_params=pltpu.CompilerParams(
            dimension_semantics=("arbitrary", "arbitrary"), vmem_limit_bytes=56 * 1024 * 1024
        ),
        cost_estimate=cost,
    )(keep, live, query_rows, *([cache_keys] * TPB), *([cache_values] * TPB), new_keys, new_values, query_place, key_place)


def body(
    queries,
    new_keys,
    new_values,
    cache_keys,
    cache_values,
    keep_tiles,
    tile_count,
    owner_slot,
    out_weight,
):
    q_dev = queries.shape[0]
    kv_local = new_keys.shape[1] // DH
    q_local = queries.shape[1] // DH
    group_size = q_local // kv_local
    ctx_count = lax.axis_size("ctx")
    tp_count = lax.axis_size("tp")
    total_rows = q_dev * ctx_count
    my_index = lax.axis_index("ctx")
    key_place = owner_slot[my_index] * q_dev + jnp.arange(q_dev, dtype=jnp.int32)
    (query_blocks,) = push((queries,), "ctx", ctx_count, False, 0)
    query_rows = query_blocks.reshape(total_rows, queries.shape[1])
    query_place = (
        owner_slot[:, None] * q_dev + jnp.arange(q_dev, dtype=jnp.int32)[None, :]
    ).reshape(total_rows)
    sums_all, maxima, totals = local_attention(
        query_rows,
        cache_keys,
        cache_values,
        new_keys,
        new_values,
        keep_tiles[0],
        tile_count[0],
        query_place.reshape(total_rows, 1),
        key_place.reshape(1, q_dev),
    )
    maxima_all = jnp.transpose(maxima, (1, 0, 2)).reshape(ctx_count, q_dev, q_local)
    totals_all = jnp.transpose(totals, (1, 0, 2)).reshape(ctx_count, q_dev, q_local)
    sums_all = sums_all.reshape(ctx_count, q_dev, q_local * DH)
    part_max, part_total, part_sum = push((maxima_all, totals_all, sums_all), "ctx", ctx_count, True, 1)
    top_max = jnp.max(part_max, axis=0)
    factor = jnp.exp2((part_max - top_max[None]) * (DH ** (-0.5) * LOG2E))
    denominator = jnp.sum(part_total * factor, axis=0)
    numerator = jnp.sum(
        part_sum.reshape(ctx_count, q_dev, q_local, DH).astype(jnp.float32) * factor[..., None],
        axis=0,
    )
    attn_rows = (
        (numerator / denominator[..., None]).reshape(q_dev, q_local * DH).astype(jnp.bfloat16)
    )
    (attn_blocks,) = push((attn_rows,), "ctx", ctx_count, False, 2)
    projected = jnp.dot(
        attn_blocks.reshape(total_rows, q_local * DH),
        out_weight,
        preferred_element_type=jnp.float32,
    )
    out_rows = total_rows // tp_count
    (proj_parts,) = push(
        (projected.reshape(tp_count, out_rows, projected.shape[1]),), "tp", tp_count, True, 3
    )
    return jnp.sum(proj_parts, axis=0)


def solution(mesh):
    return jax.shard_map(
        body,
        mesh=mesh,
        in_specs=(
            P("ctx", "tp"),
            P("ctx", "tp"),
            P("ctx", "tp"),
            P("ctx", "tp"),
            P("ctx", "tp"),
            P("ctx", "tp", None),
            P("ctx", "tp"),
            P(),
            P("tp", "ctx"),
        ),
        out_specs=P("tp", "ctx"),
        check_vma=False,
    )
```

```python
import functools

import jax
import jax.numpy as jnp
from jax import lax
from jax.experimental import pallas as pl
from jax.experimental.pallas import tpu as pltpu
from jax.sharding import PartitionSpec as P

DH = 128
TILE = 128
TB = 4
MESH = pl.DeviceIdType.MESH

NEG_INF = -jnp.inf


def push_kernel(axis, n, per_dest, count, *refs):
    x_refs = refs[:count]
    y_refs = refs[count : 2 * count]
    send_sem, recv_sem, local_sem = refs[2 * count :]
    me = lax.axis_index(axis)
    barrier = pltpu.get_barrier_semaphore()
    for k in range(1, n):
        peer = lax.rem(me + k, n)
        pl.semaphore_signal(barrier, inc=1, device_id={axis: peer}, device_id_type=MESH)
    pl.semaphore_wait(barrier, n - 1)
    copies = []
    for a in range(count):
        for k in range(1, n):
            peer = lax.rem(me + k, n)
            src = x_refs[a].at[peer] if per_dest else x_refs[a]
            copy = pltpu.make_async_remote_copy(
                src_ref=src,
                dst_ref=y_refs[a].at[me],
                send_sem=send_sem.at[a, k],
                recv_sem=recv_sem.at[a, k],
                device_id={axis: peer},
                device_id_type=MESH,
            )
            copy.start()
            copies.append(copy)
    locals_ = []
    for a in range(count):
        src = x_refs[a].at[me] if per_dest else x_refs[a]
        local = pltpu.make_async_copy(src, y_refs[a].at[me], local_sem.at[a])
        local.start()
        locals_.append(local)
    for local in locals_:
        local.wait()
    for copy in copies:
        copy.wait()


def push(xs, axis, n, per_dest, collective_id):
    count = len(xs)
    out_shape = []
    for x in xs:
        block = x.shape[1:] if per_dest else x.shape
        out_shape.append(jax.ShapeDtypeStruct((n,) + tuple(block), x.dtype))
    any_spec = pl.BlockSpec(memory_space=pl.ANY)
    return pl.pallas_call(
        functools.partial(push_kernel, axis, n, per_dest, count),
        out_shape=tuple(out_shape),
        in_specs=[any_spec] * count,
        out_specs=tuple([any_spec] * count),
        scratch_shapes=[
            pltpu.SemaphoreType.DMA((count, n)),
            pltpu.SemaphoreType.DMA((count, n)),
            pltpu.SemaphoreType.DMA((count,)),
        ],
        compiler_params=pltpu.CompilerParams(collective_id=collective_id, has_side_effects=True),
    )(*xs)


TPB = 8
LOG2E = 1.4426950408889634


def dot_nt(a, b):
    return lax.dot_general(a, b, (((1,), (1,)), ((), ())), preferred_element_type=jnp.float32)


def attn_kernel(tpb, group_size, kt_ref, cnt_ref, q_ref, *refs):
    k_refs = refs[:tpb]
    v_refs = refs[tpb : 2 * tpb]
    nk_ref, nv_ref, qp_ref, kp_ref = refs[2 * tpb : 2 * tpb + 4]
    sum_out, m_out, l_out = refs[2 * tpb + 4 : 2 * tpb + 7]
    m_scr, acc_ref = refs[2 * tpb + 7 :]
    g = pl.program_id(0)
    t = pl.program_id(1)
    last = pl.num_programs(1) - 1
    live = cnt_ref[g]
    coef = DH ** (-0.5) * LOG2E

    @pl.when(t == 0)
    def _():
        m_scr[...] = jnp.full(m_scr.shape, NEG_INF, jnp.float32)
        acc_ref[...] = jnp.zeros(acc_ref.shape, jnp.float32)

    def fold(h, keys, values_ext, mask):
        cols = pl.ds(pl.multiple_of(h * DH, DH), DH)
        s = dot_nt(q_ref[:, cols], keys)
        if mask is not None:
            s = s + mask
        m_prev = m_scr[h]
        m_new = jnp.maximum(m_prev, s.max(axis=1, keepdims=True))
        alpha = jnp.exp2((m_prev - m_new) * coef)
        p = jnp.exp2(s * coef - m_new[:, :1] * coef)
        m_scr[h] = m_new
        acc_ref[h] = acc_ref[h] * alpha[:, :1] + jnp.dot(
            p.astype(jnp.bfloat16), values_ext, preferred_element_type=jnp.float32
        )

    def with_ones(values):
        return jnp.concatenate([values, jnp.ones(values.shape, values.dtype)], axis=1)

    def tiles_step(masked):
        keys = jnp.concatenate([k[...] for k in k_refs], axis=0)
        values_ext = with_ones(jnp.concatenate([v[...] for v in v_refs], axis=0))
        mask = None
        if masked:
            slot = t * tpb + lax.broadcasted_iota(jnp.int32, (1, tpb * TILE), 1) // TILE
            mask = jnp.where(slot < live, 0.0, NEG_INF).astype(jnp.float32)

        def head_body(h, carry):
            fold(h, keys, values_ext, mask)
            return carry

        lax.fori_loop(0, group_size, head_body, 0)

    @pl.when((t + 1) * tpb <= live)
    def _():
        tiles_step(False)

    @pl.when(jnp.logical_and(t * tpb < live, (t + 1) * tpb > live))
    def _():
        tiles_step(True)

    @pl.when(t == last)
    def _():
        causal = jnp.where(qp_ref[...] >= kp_ref[...], 0.0, NEG_INF).astype(jnp.float32)
        nk = nk_ref[...]
        nv_ext = with_ones(nv_ref[...])

        def head_body(h, carry):
            fold(h, nk, nv_ext, causal)
            return carry

        lax.fori_loop(0, group_size, head_body, 0)
        for h in range(group_size):
            acc = acc_ref[h]
            sum_out[:, h * DH : (h + 1) * DH] = acc[:, :DH].astype(sum_out.dtype)
            m_out[:, h : h + 1] = m_scr[h][:, :1]
            l_out[:, h : h + 1] = acc[:, DH : DH + 1]


def local_attention(query_rows, cache_keys, cache_values, new_keys, new_values, keep, live, query_place, key_place):
    rows, width = query_rows.shape
    kv_local = new_keys.shape[1] // DH
    group_size = width // DH // kv_local
    slots = keep.shape[1]
    steps = slots // TPB
    q_new = new_keys.shape[0]

    def tile_map(j):
        def index_map(g, t, kt_ref, cnt_ref):
            return (kt_ref[g, jnp.minimum(t * TPB + j, cnt_ref[g] - 1)], g)

        return index_map

    tile_spec = [pl.BlockSpec((TILE, DH), tile_map(j)) for j in range(TPB)]
    grid_spec = pltpu.PrefetchScalarGridSpec(
        num_scalar_prefetch=2,
        grid=(kv_local, steps),
        in_specs=[pl.BlockSpec((rows, group_size * DH), lambda g, t, kt, cn: (0, g))]
        + tile_spec
        + tile_spec
        + [
            pl.BlockSpec((q_new, DH), lambda g, t, kt, cn: (0, g)),
            pl.BlockSpec((q_new, DH), lambda g, t, kt, cn: (0, g)),
            pl.BlockSpec((rows, 1), lambda g, t, kt, cn: (0, 0)),
            pl.BlockSpec((1, q_new), lambda g, t, kt, cn: (0, 0)),
        ],
        out_specs=[
            pl.BlockSpec((rows, group_size * DH), lambda g, t, kt, cn: (0, g)),
            pl.BlockSpec((None, rows, group_size), lambda g, t, kt, cn: (g, 0, 0)),
            pl.BlockSpec((None, rows, group_size), lambda g, t, kt, cn: (g, 0, 0)),
        ],
        scratch_shapes=[
            pltpu.VMEM((group_size, rows, DH), jnp.float32),
            pltpu.VMEM((group_size, rows, 2 * DH), jnp.float32),
        ],
    )
    keys_total = slots * TILE + q_new
    flops = 4 * rows * kv_local * group_size * keys_total * DH
    cost = pl.CostEstimate(
        flops=flops,
        transcendentals=rows * kv_local * group_size * keys_total,
        bytes_accessed=rows * width * 2 + rows * width * 4 + 2 * kv_local * slots * TILE * DH * 2,
    )
    return pl.pallas_call(
        functools.partial(attn_kernel, TPB, group_size),
        grid_spec=grid_spec,
        out_shape=[
            jax.ShapeDtypeStruct((rows, width), jnp.bfloat16),
            jax.ShapeDtypeStruct((kv_local, rows, group_size), jnp.float32),
            jax.ShapeDtypeStruct((kv_local, rows, group_size), jnp.float32),
        ],
        compiler_params=pltpu.CompilerParams(
            dimension_semantics=("arbitrary", "arbitrary"), vmem_limit_bytes=56 * 1024 * 1024
        ),
        cost_estimate=cost,
    )(keep, live, query_rows, *([cache_keys] * TPB), *([cache_values] * TPB), new_keys, new_values, query_place, key_place)


def combine_kernel(heads, part_ref, fac_ref, den_ref, out_ref):
    senders = part_ref.shape[0]

    def sender_body(i, acc):
        blk = part_ref[i].astype(jnp.float32)
        fac = fac_ref[i]
        return tuple(
            acc[h] + blk[:, h * DH : (h + 1) * DH] * fac[:, h : h + 1] for h in range(heads)
        )

    rows = out_ref.shape[0]
    start = tuple(jnp.zeros((rows, DH), jnp.float32) for _ in range(heads))
    acc = lax.fori_loop(0, senders, sender_body, start)
    den = den_ref[...]
    for h in range(heads):
        out_ref[:, h * DH : (h + 1) * DH] = (acc[h] / den[:, h : h + 1]).astype(out_ref.dtype)


def combine(part_sum, factor, denominator):
    senders, rows, width = part_sum.shape
    heads = width // DH
    vmem = pl.BlockSpec(memory_space=pltpu.VMEM)
    return pl.pallas_call(
        functools.partial(combine_kernel, heads),
        out_shape=jax.ShapeDtypeStruct((rows, width), jnp.bfloat16),
        in_specs=[vmem, vmem, vmem],
        out_specs=vmem,
        compiler_params=pltpu.CompilerParams(vmem_limit_bytes=32 * 1024 * 1024),
    )(part_sum, factor, denominator)


def body(
    queries,
    new_keys,
    new_values,
    cache_keys,
    cache_values,
    keep_tiles,
    tile_count,
    owner_slot,
    out_weight,
):
    q_dev = queries.shape[0]
    kv_local = new_keys.shape[1] // DH
    q_local = queries.shape[1] // DH
    group_size = q_local // kv_local
    ctx_count = lax.axis_size("ctx")
    tp_count = lax.axis_size("tp")
    total_rows = q_dev * ctx_count
    my_index = lax.axis_index("ctx")
    key_place = owner_slot[my_index] * q_dev + jnp.arange(q_dev, dtype=jnp.int32)
    (query_blocks,) = push((queries,), "ctx", ctx_count, False, 0)
    query_rows = query_blocks.reshape(total_rows, queries.shape[1])
    query_place = (
        owner_slot[:, None] * q_dev + jnp.arange(q_dev, dtype=jnp.int32)[None, :]
    ).reshape(total_rows)
    sums_all, maxima, totals = local_attention(
        query_rows,
        cache_keys,
        cache_values,
        new_keys,
        new_values,
        keep_tiles[0],
        tile_count[0],
        query_place.reshape(total_rows, 1),
        key_place.reshape(1, q_dev),
    )
    maxima_all = jnp.transpose(maxima, (1, 0, 2)).reshape(ctx_count, q_dev, q_local)
    totals_all = jnp.transpose(totals, (1, 0, 2)).reshape(ctx_count, q_dev, q_local)
    sums_all = sums_all.reshape(ctx_count, q_dev, q_local * DH)
    part_max, part_total, part_sum = push((maxima_all, totals_all, sums_all), "ctx", ctx_count, True, 1)
    top_max = jnp.max(part_max, axis=0)
    factor = jnp.exp2((part_max - top_max[None]) * (DH ** (-0.5) * LOG2E))
    denominator = jnp.sum(part_total * factor, axis=0)
    attn_rows = combine(part_sum, factor, denominator)
    (attn_blocks,) = push((attn_rows,), "ctx", ctx_count, False, 2)
    projected = jnp.dot(
        attn_blocks.reshape(total_rows, q_local * DH),
        out_weight,
        preferred_element_type=jnp.float32,
    )
    out_rows = total_rows // tp_count
    (proj_parts,) = push(
        (projected.reshape(tp_count, out_rows, projected.shape[1]),), "tp", tp_count, True, 3
    )
    return jnp.sum(proj_parts, axis=0)


def solution(mesh):
    return jax.shard_map(
        body,
        mesh=mesh,
        in_specs=(
            P("ctx", "tp"),
            P("ctx", "tp"),
            P("ctx", "tp"),
            P("ctx", "tp"),
            P("ctx", "tp"),
            P("ctx", "tp", None),
            P("ctx", "tp"),
            P(),
            P("tp", "ctx"),
        ),
        out_specs=P("tp", "ctx"),
        check_vma=False,
    )
```

```python
import functools

import jax
import jax.numpy as jnp
from jax import lax
from jax.experimental import pallas as pl
from jax.experimental.pallas import tpu as pltpu
from jax.sharding import PartitionSpec as P

DH = 128
TILE = 128
TB = 4
MESH = pl.DeviceIdType.MESH

NEG_INF = -jnp.inf


def push_kernel(axis, n, per_dest, count, *refs):
    x_refs = refs[:count]
    y_refs = refs[count : 2 * count]
    send_sem, recv_sem, local_sem = refs[2 * count :]
    me = lax.axis_index(axis)
    barrier = pltpu.get_barrier_semaphore()
    for k in range(1, n):
        peer = lax.rem(me + k, n)
        pl.semaphore_signal(barrier, inc=1, device_id={axis: peer}, device_id_type=MESH)
    pl.semaphore_wait(barrier, n - 1)
    copies = []
    for a in range(count):
        for k in range(1, n):
            peer = lax.rem(me + k, n)
            src = x_refs[a].at[peer] if per_dest else x_refs[a]
            copy = pltpu.make_async_remote_copy(
                src_ref=src,
                dst_ref=y_refs[a].at[me],
                send_sem=send_sem.at[a, k],
                recv_sem=recv_sem.at[a, k],
                device_id={axis: peer},
                device_id_type=MESH,
            )
            copy.start()
            copies.append(copy)
    locals_ = []
    for a in range(count):
        src = x_refs[a].at[me] if per_dest else x_refs[a]
        local = pltpu.make_async_copy(src, y_refs[a].at[me], local_sem.at[a])
        local.start()
        locals_.append(local)
    for local in locals_:
        local.wait()
    for copy in copies:
        copy.wait()


def push(xs, axis, n, per_dest, collective_id):
    count = len(xs)
    out_shape = []
    for x in xs:
        block = x.shape[1:] if per_dest else x.shape
        out_shape.append(jax.ShapeDtypeStruct((n,) + tuple(block), x.dtype))
    any_spec = pl.BlockSpec(memory_space=pl.ANY)
    return pl.pallas_call(
        functools.partial(push_kernel, axis, n, per_dest, count),
        out_shape=tuple(out_shape),
        in_specs=[any_spec] * count,
        out_specs=tuple([any_spec] * count),
        scratch_shapes=[
            pltpu.SemaphoreType.DMA((count, n)),
            pltpu.SemaphoreType.DMA((count, n)),
            pltpu.SemaphoreType.DMA((count,)),
        ],
        compiler_params=pltpu.CompilerParams(collective_id=collective_id, has_side_effects=True),
    )(*xs)


TPB = 8
LOG2E = 1.4426950408889634
RC = 32


def dot_nt(a, b):
    return lax.dot_general(a, b, (((1,), (1,)), ((), ())), preferred_element_type=jnp.float32)


def attn_kernel(tpb, group_size, kt_ref, cnt_ref, q_ref, *refs):
    k_refs = refs[:tpb]
    v_refs = refs[tpb : 2 * tpb]
    nk_ref, nv_ref, qp_ref, kp_ref = refs[2 * tpb : 2 * tpb + 4]
    sum_out, m_out, l_out = refs[2 * tpb + 4 : 2 * tpb + 7]
    m_scr, acc_ref, s_scr, p_scr, alpha_scr = refs[2 * tpb + 7 :]
    g = pl.program_id(0)
    t = pl.program_id(1)
    last = pl.num_programs(1) - 1
    live = cnt_ref[g]
    coef = DH ** (-0.5) * LOG2E

    @pl.when(t == 0)
    def _():
        m_scr[...] = jnp.full(m_scr.shape, NEG_INF, jnp.float32)
        acc_ref[...] = jnp.zeros(acc_ref.shape, jnp.float32)

    def fold(h, keys, values_ext, mask):
        cols = pl.ds(pl.multiple_of(h * DH, DH), DH)
        s = dot_nt(q_ref[:, cols], keys)
        if mask is not None:
            s = s + mask
        m_prev = m_scr[h]
        m_new = jnp.maximum(m_prev, s.max(axis=1, keepdims=True))
        alpha = jnp.exp2((m_prev - m_new) * coef)
        p = jnp.exp2(s * coef - m_new[:, :1] * coef)
        m_scr[h] = m_new
        acc_ref[h] = acc_ref[h] * alpha[:, :1] + jnp.dot(
            p.astype(jnp.bfloat16), values_ext, preferred_element_type=jnp.float32
        )

    def fold_chunked(h, keys, values_ext, mask):
        cols = pl.ds(pl.multiple_of(h * DH, DH), DH)
        s_scr[...] = dot_nt(q_ref[:, cols], keys)
        rows = s_scr.shape[0]

        def chunk(r, carry):
            rs = pl.ds(pl.multiple_of(r * RC, RC), RC)
            s = s_scr[rs, :]
            if mask is not None:
                s = s + mask
            m_prev = m_scr[h, rs, :]
            m_new = jnp.maximum(m_prev, s.max(axis=1, keepdims=True))
            alpha_scr[rs, :] = jnp.exp2((m_prev - m_new) * coef)
            p_scr[rs, :] = jnp.exp2(s * coef - m_new[:, :1] * coef).astype(jnp.bfloat16)
            m_scr[h, rs, :] = m_new
            return carry

        lax.fori_loop(0, rows // RC, chunk, 0)
        acc_ref[h] = acc_ref[h] * alpha_scr[:, :1] + jnp.dot(
            p_scr[...], values_ext, preferred_element_type=jnp.float32
        )

    def with_ones(values):
        return jnp.concatenate([values, jnp.ones(values.shape, values.dtype)], axis=1)

    def tiles_step(masked):
        keys = jnp.concatenate([k[...] for k in k_refs], axis=0)
        values_ext = with_ones(jnp.concatenate([v[...] for v in v_refs], axis=0))
        mask = None
        if masked:
            slot = t * tpb + lax.broadcasted_iota(jnp.int32, (1, tpb * TILE), 1) // TILE
            mask = jnp.where(slot < live, 0.0, NEG_INF).astype(jnp.float32)

        def head_body(h, carry):
            fold_chunked(h, keys, values_ext, mask)
            return carry

        lax.fori_loop(0, group_size, head_body, 0)

    @pl.when((t + 1) * tpb <= live)
    def _():
        tiles_step(False)

    @pl.when(jnp.logical_and(t * tpb < live, (t + 1) * tpb > live))
    def _():
        tiles_step(True)

    @pl.when(t == last)
    def _():
        causal = jnp.where(qp_ref[...] >= kp_ref[...], 0.0, NEG_INF).astype(jnp.float32)
        nk = nk_ref[...]
        nv_ext = with_ones(nv_ref[...])

        def head_body(h, carry):
            fold(h, nk, nv_ext, causal)
            return carry

        lax.fori_loop(0, group_size, head_body, 0)
        for h in range(group_size):
            acc = acc_ref[h]
            sum_out[:, h * DH : (h + 1) * DH] = acc[:, :DH].astype(sum_out.dtype)
            m_out[:, h : h + 1] = m_scr[h][:, :1]
            l_out[:, h : h + 1] = acc[:, DH : DH + 1]


def local_attention(query_rows, cache_keys, cache_values, new_keys, new_values, keep, live, query_place, key_place):
    rows, width = query_rows.shape
    kv_local = new_keys.shape[1] // DH
    group_size = width // DH // kv_local
    slots = keep.shape[1]
    steps = slots // TPB
    q_new = new_keys.shape[0]

    def tile_map(j):
        def index_map(g, t, kt_ref, cnt_ref):
            return (kt_ref[g, jnp.minimum(t * TPB + j, cnt_ref[g] - 1)], g)

        return index_map

    tile_spec = [pl.BlockSpec((TILE, DH), tile_map(j)) for j in range(TPB)]
    grid_spec = pltpu.PrefetchScalarGridSpec(
        num_scalar_prefetch=2,
        grid=(kv_local, steps),
        in_specs=[pl.BlockSpec((rows, group_size * DH), lambda g, t, kt, cn: (0, g))]
        + tile_spec
        + tile_spec
        + [
            pl.BlockSpec((q_new, DH), lambda g, t, kt, cn: (0, g)),
            pl.BlockSpec((q_new, DH), lambda g, t, kt, cn: (0, g)),
            pl.BlockSpec((rows, 1), lambda g, t, kt, cn: (0, 0)),
            pl.BlockSpec((1, q_new), lambda g, t, kt, cn: (0, 0)),
        ],
        out_specs=[
            pl.BlockSpec((rows, group_size * DH), lambda g, t, kt, cn: (0, g)),
            pl.BlockSpec((None, rows, group_size), lambda g, t, kt, cn: (g, 0, 0)),
            pl.BlockSpec((None, rows, group_size), lambda g, t, kt, cn: (g, 0, 0)),
        ],
        scratch_shapes=[
            pltpu.VMEM((group_size, rows, DH), jnp.float32),
            pltpu.VMEM((group_size, rows, 2 * DH), jnp.float32),
            pltpu.VMEM((rows, TPB * TILE), jnp.float32),
            pltpu.VMEM((rows, TPB * TILE), jnp.bfloat16),
            pltpu.VMEM((rows, DH), jnp.float32),
        ],
    )
    keys_total = slots * TILE + q_new
    flops = 4 * rows * kv_local * group_size * keys_total * DH
    cost = pl.CostEstimate(
        flops=flops,
        transcendentals=rows * kv_local * group_size * keys_total,
        bytes_accessed=rows * width * 2 + rows * width * 4 + 2 * kv_local * slots * TILE * DH * 2,
    )
    return pl.pallas_call(
        functools.partial(attn_kernel, TPB, group_size),
        grid_spec=grid_spec,
        out_shape=[
            jax.ShapeDtypeStruct((rows, width), jnp.bfloat16),
            jax.ShapeDtypeStruct((kv_local, rows, group_size), jnp.float32),
            jax.ShapeDtypeStruct((kv_local, rows, group_size), jnp.float32),
        ],
        compiler_params=pltpu.CompilerParams(
            dimension_semantics=("arbitrary", "arbitrary"), vmem_limit_bytes=56 * 1024 * 1024
        ),
        cost_estimate=cost,
    )(keep, live, query_rows, *([cache_keys] * TPB), *([cache_values] * TPB), new_keys, new_values, query_place, key_place)


def combine_kernel(heads, part_ref, fac_ref, den_ref, out_ref):
    senders = part_ref.shape[0]

    def sender_body(i, acc):
        blk = part_ref[i].astype(jnp.float32)
        fac = fac_ref[i]
        return tuple(
            acc[h] + blk[:, h * DH : (h + 1) * DH] * fac[:, h : h + 1] for h in range(heads)
        )

    rows = out_ref.shape[0]
    start = tuple(jnp.zeros((rows, DH), jnp.float32) for _ in range(heads))
    acc = lax.fori_loop(0, senders, sender_body, start)
    den = den_ref[...]
    for h in range(heads):
        out_ref[:, h * DH : (h + 1) * DH] = (acc[h] / den[:, h : h + 1]).astype(out_ref.dtype)


def combine(part_sum, factor, denominator):
    senders, rows, width = part_sum.shape
    heads = width // DH
    vmem = pl.BlockSpec(memory_space=pltpu.VMEM)
    return pl.pallas_call(
        functools.partial(combine_kernel, heads),
        out_shape=jax.ShapeDtypeStruct((rows, width), jnp.bfloat16),
        in_specs=[vmem, vmem, vmem],
        out_specs=vmem,
        compiler_params=pltpu.CompilerParams(vmem_limit_bytes=32 * 1024 * 1024),
    )(part_sum, factor, denominator)


def body(
    queries,
    new_keys,
    new_values,
    cache_keys,
    cache_values,
    keep_tiles,
    tile_count,
    owner_slot,
    out_weight,
):
    q_dev = queries.shape[0]
    kv_local = new_keys.shape[1] // DH
    q_local = queries.shape[1] // DH
    group_size = q_local // kv_local
    ctx_count = lax.axis_size("ctx")
    tp_count = lax.axis_size("tp")
    total_rows = q_dev * ctx_count
    my_index = lax.axis_index("ctx")
    key_place = owner_slot[my_index] * q_dev + jnp.arange(q_dev, dtype=jnp.int32)
    (query_blocks,) = push((queries,), "ctx", ctx_count, False, 0)
    query_rows = query_blocks.reshape(total_rows, queries.shape[1])
    query_place = (
        owner_slot[:, None] * q_dev + jnp.arange(q_dev, dtype=jnp.int32)[None, :]
    ).reshape(total_rows)
    sums_all, maxima, totals = local_attention(
        query_rows,
        cache_keys,
        cache_values,
        new_keys,
        new_values,
        keep_tiles[0],
        tile_count[0],
        query_place.reshape(total_rows, 1),
        key_place.reshape(1, q_dev),
    )
    maxima_all = jnp.transpose(maxima, (1, 0, 2)).reshape(ctx_count, q_dev, q_local)
    totals_all = jnp.transpose(totals, (1, 0, 2)).reshape(ctx_count, q_dev, q_local)
    sums_all = sums_all.reshape(ctx_count, q_dev, q_local * DH)
    part_max, part_total, part_sum = push((maxima_all, totals_all, sums_all), "ctx", ctx_count, True, 1)
    top_max = jnp.max(part_max, axis=0)
    factor = jnp.exp2((part_max - top_max[None]) * (DH ** (-0.5) * LOG2E))
    denominator = jnp.sum(part_total * factor, axis=0)
    attn_rows = combine(part_sum, factor, denominator)
    (attn_blocks,) = push((attn_rows,), "ctx", ctx_count, False, 2)
    projected = jnp.dot(
        attn_blocks.reshape(total_rows, q_local * DH),
        out_weight,
        preferred_element_type=jnp.float32,
    )
    out_rows = total_rows // tp_count
    (proj_parts,) = push(
        (projected.reshape(tp_count, out_rows, projected.shape[1]),), "tp", tp_count, True, 3
    )
    return jnp.sum(proj_parts, axis=0)


def solution(mesh):
    return jax.shard_map(
        body,
        mesh=mesh,
        in_specs=(
            P("ctx", "tp"),
            P("ctx", "tp"),
            P("ctx", "tp"),
            P("ctx", "tp"),
            P("ctx", "tp"),
            P("ctx", "tp", None),
            P("ctx", "tp"),
            P(),
            P("tp", "ctx"),
        ),
        out_specs=P("tp", "ctx"),
        check_vma=False,
    )
```

```python
import functools

import jax
import jax.numpy as jnp
from jax import lax
from jax.experimental import pallas as pl
from jax.experimental.pallas import tpu as pltpu
from jax.sharding import PartitionSpec as P

DH = 128
TILE = 128
TB = 4
MESH = pl.DeviceIdType.MESH

NEG_INF = -jnp.inf


def push_kernel(axis, n, per_dest, count, *refs):
    x_refs = refs[:count]
    y_refs = refs[count : 2 * count]
    send_sem, recv_sem, local_sem = refs[2 * count :]
    me = lax.axis_index(axis)
    barrier = pltpu.get_barrier_semaphore()
    for k in range(1, n):
        peer = lax.rem(me + k, n)
        pl.semaphore_signal(barrier, inc=1, device_id={axis: peer}, device_id_type=MESH)
    pl.semaphore_wait(barrier, n - 1)
    copies = []
    for a in range(count):
        for k in range(1, n):
            peer = lax.rem(me + k, n)
            src = x_refs[a].at[peer] if per_dest else x_refs[a]
            copy = pltpu.make_async_remote_copy(
                src_ref=src,
                dst_ref=y_refs[a].at[me],
                send_sem=send_sem.at[a, k],
                recv_sem=recv_sem.at[a, k],
                device_id={axis: peer},
                device_id_type=MESH,
            )
            copy.start()
            copies.append(copy)
    locals_ = []
    for a in range(count):
        src = x_refs[a].at[me] if per_dest else x_refs[a]
        local = pltpu.make_async_copy(src, y_refs[a].at[me], local_sem.at[a])
        local.start()
        locals_.append(local)
    for local in locals_:
        local.wait()
    for copy in copies:
        copy.wait()


def push(xs, axis, n, per_dest, collective_id):
    count = len(xs)
    out_shape = []
    for x in xs:
        block = x.shape[1:] if per_dest else x.shape
        out_shape.append(jax.ShapeDtypeStruct((n,) + tuple(block), x.dtype))
    any_spec = pl.BlockSpec(memory_space=pl.ANY)
    return pl.pallas_call(
        functools.partial(push_kernel, axis, n, per_dest, count),
        out_shape=tuple(out_shape),
        in_specs=[any_spec] * count,
        out_specs=tuple([any_spec] * count),
        scratch_shapes=[
            pltpu.SemaphoreType.DMA((count, n)),
            pltpu.SemaphoreType.DMA((count, n)),
            pltpu.SemaphoreType.DMA((count,)),
        ],
        compiler_params=pltpu.CompilerParams(collective_id=collective_id, has_side_effects=True),
    )(*xs)


TPB = 8
LOG2E = 1.4426950408889634


def dot_nt(a, b):
    return jnp.dot(a, b, preferred_element_type=jnp.float32)


def attn_kernel(tpb, group_size, kt_ref, cnt_ref, q_ref, *refs):
    k_refs = refs[:tpb]
    v_refs = refs[tpb : 2 * tpb]
    nk_ref, nv_ref, qp_ref, kp_ref = refs[2 * tpb : 2 * tpb + 4]
    sum_out, m_out, l_out = refs[2 * tpb + 4 : 2 * tpb + 7]
    m_scr, acc_ref = refs[2 * tpb + 7 :]
    g = pl.program_id(0)
    t = pl.program_id(1)
    last = pl.num_programs(1) - 1
    live = cnt_ref[g]
    coef = DH ** (-0.5) * LOG2E

    @pl.when(t == 0)
    def _():
        m_scr[...] = jnp.full(m_scr.shape, NEG_INF, jnp.float32)
        acc_ref[...] = jnp.zeros(acc_ref.shape, jnp.float32)

    def fold(h, keys, values_ext, mask):
        cols = pl.ds(pl.multiple_of(h * DH, DH), DH)
        s = dot_nt(q_ref[:, cols], keys)
        if mask is not None:
            s = s + mask
        m_prev = m_scr[h]
        m_new = jnp.maximum(m_prev, s.max(axis=1, keepdims=True))
        alpha = jnp.exp2((m_prev - m_new) * coef)
        p = jnp.exp2(s * coef - m_new[:, :1] * coef)
        m_scr[h] = m_new
        acc_ref[h] = acc_ref[h] * alpha[:, :1] + jnp.dot(
            p.astype(jnp.bfloat16), values_ext, preferred_element_type=jnp.float32
        )

    def with_ones(values):
        return jnp.concatenate([values, jnp.ones(values.shape, values.dtype)], axis=1)

    def tiles_step(masked):
        keys = jnp.concatenate([k[...] for k in k_refs], axis=1)
        values_ext = with_ones(jnp.concatenate([v[...] for v in v_refs], axis=0))
        mask = None
        if masked:
            slot = t * tpb + lax.broadcasted_iota(jnp.int32, (1, tpb * TILE), 1) // TILE
            mask = jnp.where(slot < live, 0.0, NEG_INF).astype(jnp.float32)

        def head_body(h, carry):
            fold(h, keys, values_ext, mask)
            return carry

        lax.fori_loop(0, group_size, head_body, 0)

    @pl.when((t + 1) * tpb <= live)
    def _():
        tiles_step(False)

    @pl.when(jnp.logical_and(t * tpb < live, (t + 1) * tpb > live))
    def _():
        tiles_step(True)

    @pl.when(t == last)
    def _():
        causal = jnp.where(qp_ref[...] >= kp_ref[...], 0.0, NEG_INF).astype(jnp.float32)
        nk = nk_ref[...]
        nv_ext = with_ones(nv_ref[...])

        def head_body(h, carry):
            fold(h, nk, nv_ext, causal)
            return carry

        lax.fori_loop(0, group_size, head_body, 0)
        for h in range(group_size):
            acc = acc_ref[h]
            sum_out[:, h * DH : (h + 1) * DH] = acc[:, :DH].astype(sum_out.dtype)
            m_out[:, h : h + 1] = m_scr[h][:, :1]
            l_out[:, h : h + 1] = acc[:, DH : DH + 1]


def local_attention(query_rows, cache_keys, cache_values, new_keys, new_values, keep, live, query_place, key_place):
    rows, width = query_rows.shape
    kv_local = new_keys.shape[1] // DH
    group_size = width // DH // kv_local
    slots = keep.shape[1]
    steps = slots // TPB
    q_new = new_keys.shape[0]

    def tile_map(j):
        def index_map(g, t, kt_ref, cnt_ref):
            return (kt_ref[g, jnp.minimum(t * TPB + j, cnt_ref[g] - 1)], g)

        return index_map

    tile_spec = [pl.BlockSpec((TILE, DH), tile_map(j)) for j in range(TPB)]

    def tile_map_t(j):
        def index_map(g, t, kt_ref, cnt_ref):
            return (g, kt_ref[g, jnp.minimum(t * TPB + j, cnt_ref[g] - 1)])

        return index_map

    tile_spec_t = [pl.BlockSpec((DH, TILE), tile_map_t(j)) for j in range(TPB)]
    grid_spec = pltpu.PrefetchScalarGridSpec(
        num_scalar_prefetch=2,
        grid=(kv_local, steps),
        in_specs=[pl.BlockSpec((rows, group_size * DH), lambda g, t, kt, cn: (0, g))]
        + tile_spec_t
        + tile_spec
        + [
            pl.BlockSpec((DH, q_new), lambda g, t, kt, cn: (g, 0)),
            pl.BlockSpec((q_new, DH), lambda g, t, kt, cn: (0, g)),
            pl.BlockSpec((rows, 1), lambda g, t, kt, cn: (0, 0)),
            pl.BlockSpec((1, q_new), lambda g, t, kt, cn: (0, 0)),
        ],
        out_specs=[
            pl.BlockSpec((rows, group_size * DH), lambda g, t, kt, cn: (0, g)),
            pl.BlockSpec((None, rows, group_size), lambda g, t, kt, cn: (g, 0, 0)),
            pl.BlockSpec((None, rows, group_size), lambda g, t, kt, cn: (g, 0, 0)),
        ],
        scratch_shapes=[
            pltpu.VMEM((group_size, rows, DH), jnp.float32),
            pltpu.VMEM((group_size, rows, 2 * DH), jnp.float32),
        ],
    )
    keys_total = slots * TILE + q_new
    flops = 4 * rows * kv_local * group_size * keys_total * DH
    cost = pl.CostEstimate(
        flops=flops,
        transcendentals=rows * kv_local * group_size * keys_total,
        bytes_accessed=rows * width * 2 + rows * width * 4 + 2 * kv_local * slots * TILE * DH * 2,
    )
    return pl.pallas_call(
        functools.partial(attn_kernel, TPB, group_size),
        grid_spec=grid_spec,
        out_shape=[
            jax.ShapeDtypeStruct((rows, width), jnp.bfloat16),
            jax.ShapeDtypeStruct((kv_local, rows, group_size), jnp.float32),
            jax.ShapeDtypeStruct((kv_local, rows, group_size), jnp.float32),
        ],
        compiler_params=pltpu.CompilerParams(
            dimension_semantics=("arbitrary", "arbitrary"), vmem_limit_bytes=56 * 1024 * 1024
        ),
        cost_estimate=cost,
    )(keep, live, query_rows, *([cache_keys.T] * TPB), *([cache_values] * TPB), new_keys.T, new_values, query_place, key_place)


def combine_kernel(heads, part_ref, fac_ref, den_ref, out_ref):
    senders = part_ref.shape[0]

    def sender_body(i, acc):
        blk = part_ref[i].astype(jnp.float32)
        fac = fac_ref[i]
        return tuple(
            acc[h] + blk[:, h * DH : (h + 1) * DH] * fac[:, h : h + 1] for h in range(heads)
        )

    rows = out_ref.shape[0]
    start = tuple(jnp.zeros((rows, DH), jnp.float32) for _ in range(heads))
    acc = lax.fori_loop(0, senders, sender_body, start)
    den = den_ref[...]
    for h in range(heads):
        out_ref[:, h * DH : (h + 1) * DH] = (acc[h] / den[:, h : h + 1]).astype(out_ref.dtype)


def combine(part_sum, factor, denominator):
    senders, rows, width = part_sum.shape
    heads = width // DH
    vmem = pl.BlockSpec(memory_space=pltpu.VMEM)
    return pl.pallas_call(
        functools.partial(combine_kernel, heads),
        out_shape=jax.ShapeDtypeStruct((rows, width), jnp.bfloat16),
        in_specs=[vmem, vmem, vmem],
        out_specs=vmem,
        compiler_params=pltpu.CompilerParams(vmem_limit_bytes=32 * 1024 * 1024),
    )(part_sum, factor, denominator)


def body(
    queries,
    new_keys,
    new_values,
    cache_keys,
    cache_values,
    keep_tiles,
    tile_count,
    owner_slot,
    out_weight,
):
    q_dev = queries.shape[0]
    kv_local = new_keys.shape[1] // DH
    q_local = queries.shape[1] // DH
    group_size = q_local // kv_local
    ctx_count = lax.axis_size("ctx")
    tp_count = lax.axis_size("tp")
    total_rows = q_dev * ctx_count
    my_index = lax.axis_index("ctx")
    key_place = owner_slot[my_index] * q_dev + jnp.arange(q_dev, dtype=jnp.int32)
    (query_blocks,) = push((queries,), "ctx", ctx_count, False, 0)
    query_rows = query_blocks.reshape(total_rows, queries.shape[1])
    query_place = (
        owner_slot[:, None] * q_dev + jnp.arange(q_dev, dtype=jnp.int32)[None, :]
    ).reshape(total_rows)
    sums_all, maxima, totals = local_attention(
        query_rows,
        cache_keys,
        cache_values,
        new_keys,
        new_values,
        keep_tiles[0],
        tile_count[0],
        query_place.reshape(total_rows, 1),
        key_place.reshape(1, q_dev),
    )
    maxima_all = jnp.transpose(maxima, (1, 0, 2)).reshape(ctx_count, q_dev, q_local)
    totals_all = jnp.transpose(totals, (1, 0, 2)).reshape(ctx_count, q_dev, q_local)
    sums_all = sums_all.reshape(ctx_count, q_dev, q_local * DH)
    part_max, part_total, part_sum = push((maxima_all, totals_all, sums_all), "ctx", ctx_count, True, 1)
    top_max = jnp.max(part_max, axis=0)
    factor = jnp.exp2((part_max - top_max[None]) * (DH ** (-0.5) * LOG2E))
    denominator = jnp.sum(part_total * factor, axis=0)
    attn_rows = combine(part_sum, factor, denominator)
    (attn_blocks,) = push((attn_rows,), "ctx", ctx_count, False, 2)
    projected = jnp.dot(
        attn_blocks.reshape(total_rows, q_local * DH),
        out_weight,
        preferred_element_type=jnp.float32,
    )
    out_rows = total_rows // tp_count
    (proj_parts,) = push(
        (projected.reshape(tp_count, out_rows, projected.shape[1]),), "tp", tp_count, True, 3
    )
    return jnp.sum(proj_parts, axis=0)


def solution(mesh):
    return jax.shard_map(
        body,
        mesh=mesh,
        in_specs=(
            P("ctx", "tp"),
            P("ctx", "tp"),
            P("ctx", "tp"),
            P("ctx", "tp"),
            P("ctx", "tp"),
            P("ctx", "tp", None),
            P("ctx", "tp"),
            P(),
            P("tp", "ctx"),
        ),
        out_specs=P("tp", "ctx"),
        check_vma=False,
    )
```

```python
import functools

import jax
import jax.numpy as jnp
from jax import lax
from jax.experimental import pallas as pl
from jax.experimental.pallas import tpu as pltpu
from jax.sharding import PartitionSpec as P

DH = 128
TILE = 128
TB = 4
MESH = pl.DeviceIdType.MESH

NEG_INF = -jnp.inf


def push_kernel(axis, n, per_dest, count, *refs):
    x_refs = refs[:count]
    y_refs = refs[count : 2 * count]
    send_sem, recv_sem, local_sem = refs[2 * count :]
    me = lax.axis_index(axis)
    barrier = pltpu.get_barrier_semaphore()
    for k in range(1, n):
        peer = lax.rem(me + k, n)
        pl.semaphore_signal(barrier, inc=1, device_id={axis: peer}, device_id_type=MESH)
    pl.semaphore_wait(barrier, n - 1)
    copies = []
    for a in range(count):
        for k in range(1, n):
            peer = lax.rem(me + k, n)
            src = x_refs[a].at[peer] if per_dest else x_refs[a]
            copy = pltpu.make_async_remote_copy(
                src_ref=src,
                dst_ref=y_refs[a].at[me],
                send_sem=send_sem.at[a, k],
                recv_sem=recv_sem.at[a, k],
                device_id={axis: peer},
                device_id_type=MESH,
            )
            copy.start()
            copies.append(copy)
    locals_ = []
    for a in range(count):
        src = x_refs[a].at[me] if per_dest else x_refs[a]
        local = pltpu.make_async_copy(src, y_refs[a].at[me], local_sem.at[a])
        local.start()
        locals_.append(local)
    for local in locals_:
        local.wait()
    for copy in copies:
        copy.wait()


def push(xs, axis, n, per_dest, collective_id):
    count = len(xs)
    out_shape = []
    for x in xs:
        block = x.shape[1:] if per_dest else x.shape
        out_shape.append(jax.ShapeDtypeStruct((n,) + tuple(block), x.dtype))
    any_spec = pl.BlockSpec(memory_space=pl.ANY)
    return pl.pallas_call(
        functools.partial(push_kernel, axis, n, per_dest, count),
        out_shape=tuple(out_shape),
        in_specs=[any_spec] * count,
        out_specs=tuple([any_spec] * count),
        scratch_shapes=[
            pltpu.SemaphoreType.DMA((count, n)),
            pltpu.SemaphoreType.DMA((count, n)),
            pltpu.SemaphoreType.DMA((count,)),
        ],
        compiler_params=pltpu.CompilerParams(collective_id=collective_id, has_side_effects=True),
    )(*xs)


TPB = 8
LOG2E = 1.4426950408889634


def dot_nt(a, b):
    return jnp.dot(a, b, preferred_element_type=jnp.float32)


def attn_kernel(tpb, group_size, kt_ref, cnt_ref, q_ref, *refs):
    k_refs = refs[:tpb]
    v_refs = refs[tpb : 2 * tpb]
    nk_ref, nv_ref, qp_ref, kp_ref = refs[2 * tpb : 2 * tpb + 4]
    sum_out, m_out, l_out = refs[2 * tpb + 4 : 2 * tpb + 7]
    m_scr, acc_ref = refs[2 * tpb + 7 :]
    g = pl.program_id(0)
    t = pl.program_id(1)
    last = pl.num_programs(1) - 1
    live = cnt_ref[g]
    coef = DH ** (-0.5) * LOG2E

    @pl.when(t == 0)
    def _():
        m_scr[...] = jnp.full(m_scr.shape, NEG_INF, jnp.float32)
        acc_ref[...] = jnp.zeros(acc_ref.shape, jnp.float32)

    def fold(h, keys, values_ext, mask):
        cols = pl.ds(pl.multiple_of(h * DH, DH), DH)
        s = dot_nt(q_ref[:, cols], keys)
        if mask is not None:
            s = s + mask
        m_prev = m_scr[h]
        m_new = jnp.maximum(m_prev, s.max(axis=1, keepdims=True))
        alpha = jnp.exp2((m_prev - m_new) * coef)
        p = jnp.exp2(s * coef - m_new[:, :1] * coef)
        m_scr[h] = m_new
        acc_ref[h] = acc_ref[h] * alpha[:, :1] + jnp.dot(
            p.astype(jnp.bfloat16), values_ext, preferred_element_type=jnp.float32
        )

    def with_ones(values):
        return jnp.concatenate([values, jnp.ones(values.shape, values.dtype)], axis=1)

    def tiles_step(masked):
        keys = jnp.concatenate([k[...] for k in k_refs], axis=1)
        values_ext = with_ones(jnp.concatenate([v[...] for v in v_refs], axis=0))
        mask = None
        if masked:
            slot = t * tpb + lax.broadcasted_iota(jnp.int32, (1, tpb * TILE), 1) // TILE
            mask = jnp.where(slot < live, 0.0, NEG_INF).astype(jnp.float32)

        def head_body(h, carry):
            fold(h, keys, values_ext, mask)
            return carry

        lax.fori_loop(0, group_size, head_body, 0)

    @pl.when((t + 1) * tpb <= live)
    def _():
        tiles_step(False)

    @pl.when(jnp.logical_and(t * tpb < live, (t + 1) * tpb > live))
    def _():
        tiles_step(True)

    @pl.when(t == last)
    def _():
        causal = jnp.where(qp_ref[...] >= kp_ref[...], 0.0, NEG_INF).astype(jnp.float32)
        nk = nk_ref[...]
        nv_ext = with_ones(nv_ref[...])

        def head_body(h, carry):
            fold(h, nk, nv_ext, causal)
            return carry

        lax.fori_loop(0, group_size, head_body, 0)
        for h in range(group_size):
            acc = acc_ref[h]
            sum_out[:, h * DH : (h + 1) * DH] = acc[:, :DH].astype(sum_out.dtype)
            m_out[:, h : h + 1] = m_scr[h][:, :1]
            l_out[:, h : h + 1] = acc[:, DH : DH + 1]


def local_attention(query_rows, cache_keys, cache_values, new_keys, new_values, keep, live, query_place, key_place):
    rows, width = query_rows.shape
    kv_local = new_keys.shape[1] // DH
    group_size = width // DH // kv_local
    slots = keep.shape[1]
    steps = slots // TPB
    q_new = new_keys.shape[0]

    def tile_map(j):
        def index_map(g, t, kt_ref, cnt_ref):
            return (kt_ref[g, jnp.minimum(t * TPB + j, cnt_ref[g] - 1)], g)

        return index_map

    tile_spec = [pl.BlockSpec((TILE, DH), tile_map(j)) for j in range(TPB)]

    def tile_map_t(j):
        def index_map(g, t, kt_ref, cnt_ref):
            return (g, kt_ref[g, jnp.minimum(t * TPB + j, cnt_ref[g] - 1)])

        return index_map

    tile_spec_t = [pl.BlockSpec((DH, TILE), tile_map_t(j)) for j in range(TPB)]
    grid_spec = pltpu.PrefetchScalarGridSpec(
        num_scalar_prefetch=2,
        grid=(kv_local, steps),
        in_specs=[pl.BlockSpec((rows, group_size * DH), lambda g, t, kt, cn: (0, g))]
        + tile_spec_t
        + tile_spec
        + [
            pl.BlockSpec((DH, q_new), lambda g, t, kt, cn: (g, 0)),
            pl.BlockSpec((q_new, DH), lambda g, t, kt, cn: (0, g)),
            pl.BlockSpec((rows, 1), lambda g, t, kt, cn: (0, 0)),
            pl.BlockSpec((1, q_new), lambda g, t, kt, cn: (0, 0)),
        ],
        out_specs=[
            pl.BlockSpec((rows, group_size * DH), lambda g, t, kt, cn: (0, g)),
            pl.BlockSpec((None, rows, group_size), lambda g, t, kt, cn: (g, 0, 0)),
            pl.BlockSpec((None, rows, group_size), lambda g, t, kt, cn: (g, 0, 0)),
        ],
        scratch_shapes=[
            pltpu.VMEM((group_size, rows, DH), jnp.float32),
            pltpu.VMEM((group_size, rows, 2 * DH), jnp.float32),
        ],
    )
    keys_total = slots * TILE + q_new
    flops = 4 * rows * kv_local * group_size * keys_total * DH
    cost = pl.CostEstimate(
        flops=flops,
        transcendentals=rows * kv_local * group_size * keys_total,
        bytes_accessed=rows * width * 2 + rows * width * 4 + 2 * kv_local * slots * TILE * DH * 2,
    )
    return pl.pallas_call(
        functools.partial(attn_kernel, TPB, group_size),
        grid_spec=grid_spec,
        out_shape=[
            jax.ShapeDtypeStruct((rows, width), jnp.bfloat16),
            jax.ShapeDtypeStruct((kv_local, rows, group_size), jnp.float32),
            jax.ShapeDtypeStruct((kv_local, rows, group_size), jnp.float32),
        ],
        compiler_params=pltpu.CompilerParams(
            dimension_semantics=("arbitrary", "arbitrary"), vmem_limit_bytes=56 * 1024 * 1024
        ),
        cost_estimate=cost,
    )(keep, live, query_rows, *([cache_keys.T] * TPB), *([cache_values] * TPB), new_keys.T, new_values, query_place, key_place)


def dense_fold(q_ref, h, keys_t, values_ext, mask, m_scr, acc_ref):
    coef = DH ** (-0.5) * LOG2E
    cols = pl.ds(pl.multiple_of(h * DH, DH), DH)
    s = jnp.dot(q_ref[:, cols], keys_t, preferred_element_type=jnp.float32) + mask
    m_prev = m_scr[h]
    m_new = jnp.maximum(m_prev, s.max(axis=1, keepdims=True))
    alpha = jnp.exp2((m_prev - m_new) * coef)
    p = jnp.exp2(s * coef - m_new[:, :1] * coef)
    m_scr[h] = m_new
    acc_ref[h] = acc_ref[h] * alpha[:, :1] + jnp.dot(
        p.astype(jnp.bfloat16), values_ext, preferred_element_type=jnp.float32
    )


def attn_push_kernel(n, group_size, *refs):
    q_ref, kt_ref, v_ref, bias_ref, nkt_ref, nv_ref, qp_ref, kp_ref = refs[:8]
    srcs = refs[8:11]
    sum_out, m_out, l_out = refs[11:14]
    dsts = refs[14:17]
    m_scr, acc_ref, send_sem, recv_sem, local_sem = refs[17:]
    t = pl.program_id(0)
    last = pl.num_programs(0) - 1
    me = lax.axis_index("ctx")

    def remote_copies():
        out = []
        for a in range(3):
            for k in range(1, n):
                peer = lax.rem(me + k, n)
                out.append(
                    pltpu.make_async_remote_copy(
                        src_ref=srcs[a].at[peer],
                        dst_ref=dsts[a].at[me],
                        send_sem=send_sem.at[a, k],
                        recv_sem=recv_sem.at[a, k],
                        device_id={"ctx": peer},
                        device_id_type=MESH,
                    )
                )
        return out

    def local_copies():
        return [
            pltpu.make_async_copy(srcs[a].at[me], dsts[a].at[me], local_sem.at[a]) for a in range(3)
        ]

    def with_ones(values):
        return jnp.concatenate([values, jnp.ones(values.shape, values.dtype)], axis=1)

    @pl.when(t == 0)
    def _():
        barrier = pltpu.get_barrier_semaphore()
        for k in range(1, n):
            peer = lax.rem(me + k, n)
            pl.semaphore_signal(barrier, inc=1, device_id={"ctx": peer}, device_id_type=MESH)
        pl.semaphore_wait(barrier, n - 1)
        for c in remote_copies():
            c.start()
        for c in local_copies():
            c.start()
        m_scr[...] = jnp.full(m_scr.shape, NEG_INF, jnp.float32)
        acc_ref[...] = jnp.zeros(acc_ref.shape, jnp.float32)

    keys_t = kt_ref[...]
    values_ext = with_ones(v_ref[...])
    mask = bias_ref[...]

    def head_body(h, carry):
        dense_fold(q_ref, h, keys_t, values_ext, mask, m_scr, acc_ref)
        return carry

    lax.fori_loop(0, group_size, head_body, 0)

    @pl.when(t == last)
    def _():
        causal = jnp.where(qp_ref[...] >= kp_ref[...], 0.0, NEG_INF).astype(jnp.float32)
        nkt = nkt_ref[...]
        nv_ext = with_ones(nv_ref[...])

        def new_body(h, carry):
            dense_fold(q_ref, h, nkt, nv_ext, causal, m_scr, acc_ref)
            return carry

        lax.fori_loop(0, group_size, new_body, 0)
        for h in range(group_size):
            acc = acc_ref[h]
            sum_out[:, h * DH : (h + 1) * DH] = acc[:, :DH].astype(sum_out.dtype)
            m_out[:, h : h + 1] = m_scr[h][:, :1]
            l_out[:, h : h + 1] = acc[:, DH : DH + 1]
        for c in local_copies():
            c.wait()
        for c in remote_copies():
            c.wait()


def attention_with_push(query_rows, keys_t, values, bias, new_keys_t, new_values, query_place, key_place, sends, n):
    rows, width = query_rows.shape
    group_size = width // DH
    total_keys = keys_t.shape[1]
    step_keys = TPB * TILE
    steps = total_keys // step_keys
    q_new = new_values.shape[0]
    any_spec = pl.BlockSpec(memory_space=pl.ANY)
    recv_shapes = [
        jax.ShapeDtypeStruct((n,) + tuple(x.shape[1:]), x.dtype) for x in sends
    ]
    flops = 4 * rows * group_size * (total_keys + q_new) * DH
    cost = pl.CostEstimate(
        flops=flops,
        transcendentals=rows * group_size * (total_keys + q_new),
        bytes_accessed=rows * width * 4 + 2 * total_keys * DH * 2,
    )
    return pl.pallas_call(
        functools.partial(attn_push_kernel, n, group_size),
        grid=(steps,),
        in_specs=[
            pl.BlockSpec((rows, width), lambda t: (0, 0)),
            pl.BlockSpec((DH, step_keys), lambda t: (0, t)),
            pl.BlockSpec((step_keys, DH), lambda t: (t, 0)),
            pl.BlockSpec((1, step_keys), lambda t: (0, t)),
            pl.BlockSpec((DH, q_new), lambda t: (0, 0)),
            pl.BlockSpec((q_new, DH), lambda t: (0, 0)),
            pl.BlockSpec((rows, 1), lambda t: (0, 0)),
            pl.BlockSpec((1, q_new), lambda t: (0, 0)),
        ]
        + [any_spec] * 3,
        out_specs=[
            pl.BlockSpec((rows, width), lambda t: (0, 0)),
            pl.BlockSpec((rows, group_size), lambda t: (0, 0)),
            pl.BlockSpec((rows, group_size), lambda t: (0, 0)),
        ]
        + [any_spec] * 3,
        out_shape=[
            jax.ShapeDtypeStruct((rows, width), jnp.bfloat16),
            jax.ShapeDtypeStruct((rows, group_size), jnp.float32),
            jax.ShapeDtypeStruct((rows, group_size), jnp.float32),
        ]
        + recv_shapes,
        scratch_shapes=[
            pltpu.VMEM((group_size, rows, DH), jnp.float32),
            pltpu.VMEM((group_size, rows, 2 * DH), jnp.float32),
            pltpu.SemaphoreType.DMA((3, n)),
            pltpu.SemaphoreType.DMA((3, n)),
            pltpu.SemaphoreType.DMA((3,)),
        ],
        compiler_params=pltpu.CompilerParams(
            collective_id=4, has_side_effects=True, vmem_limit_bytes=56 * 1024 * 1024
        ),
        cost_estimate=cost,
    )(query_rows, keys_t, values, bias, new_keys_t, new_values, query_place, key_place, *sends)


def combine_kernel(heads, part_ref, fac_ref, den_ref, out_ref):
    senders = part_ref.shape[0]
    width = part_ref.shape[3]
    half = width // DH

    def sender_body(i, acc):
        fac = fac_ref[i]
        out = []
        for h in range(heads):
            j, c = divmod(h, half)
            blk = part_ref[i, j][:, c * DH : (c + 1) * DH].astype(jnp.float32)
            out.append(acc[h] + blk * fac[:, h : h + 1])
        return tuple(out)

    rows = out_ref.shape[0]
    start = tuple(jnp.zeros((rows, DH), jnp.float32) for _ in range(heads))
    acc = lax.fori_loop(0, senders, sender_body, start)
    den = den_ref[...]
    for h in range(heads):
        out_ref[:, h * DH : (h + 1) * DH] = (acc[h] / den[:, h : h + 1]).astype(out_ref.dtype)


def combine(part_sum, factor, denominator):
    senders, groups, rows, width = part_sum.shape
    heads = groups * width // DH
    vmem = pl.BlockSpec(memory_space=pltpu.VMEM)
    return pl.pallas_call(
        functools.partial(combine_kernel, heads),
        out_shape=jax.ShapeDtypeStruct((rows, heads * DH), jnp.bfloat16),
        in_specs=[vmem, vmem, vmem],
        out_specs=vmem,
        compiler_params=pltpu.CompilerParams(vmem_limit_bytes=32 * 1024 * 1024),
    )(part_sum, factor, denominator)


def body(
    queries,
    new_keys,
    new_values,
    cache_keys,
    cache_values,
    keep_tiles,
    tile_count,
    owner_slot,
    out_weight,
):
    q_dev = queries.shape[0]
    kv_local = new_keys.shape[1] // DH
    q_local = queries.shape[1] // DH
    group_size = q_local // kv_local
    ctx_count = lax.axis_size("ctx")
    tp_count = lax.axis_size("tp")
    total_rows = q_dev * ctx_count
    my_index = lax.axis_index("ctx")
    key_place = owner_slot[my_index] * q_dev + jnp.arange(q_dev, dtype=jnp.int32)
    (query_blocks,) = push((queries,), "ctx", ctx_count, False, 0)
    query_rows = query_blocks.reshape(total_rows, queries.shape[1])
    query_place = (
        owner_slot[:, None] * q_dev + jnp.arange(q_dev, dtype=jnp.int32)[None, :]
    ).reshape(total_rows)
    width = group_size * DH
    sums0, maxima0, totals0 = local_attention(
        query_rows[:, :width],
        cache_keys[:, :DH],
        cache_values[:, :DH],
        new_keys[:, :DH],
        new_values[:, :DH],
        keep_tiles[0, :1],
        tile_count[0, :1],
        query_place.reshape(total_rows, 1),
        key_place.reshape(1, q_dev),
    )
    slots = keep_tiles.shape[2]
    tiles_k = cache_keys[:, DH : 2 * DH].reshape(-1, TILE, DH)
    tiles_v = cache_values[:, DH : 2 * DH].reshape(-1, TILE, DH)
    kept_k = jnp.take(tiles_k, keep_tiles[0, 1], axis=0).reshape(slots * TILE, DH)
    kept_v = jnp.take(tiles_v, keep_tiles[0, 1], axis=0).reshape(slots * TILE, DH)
    slot_ids = jnp.arange(slots * TILE, dtype=jnp.int32) // TILE
    bias = jnp.where(slot_ids < tile_count[0, 1], 0.0, NEG_INF).astype(jnp.float32)
    sends0 = (
        sums0.reshape(ctx_count, q_dev, width),
        maxima0.reshape(ctx_count, q_dev, group_size),
        totals0.reshape(ctx_count, q_dev, group_size),
    )
    sums1, maxima1, totals1, recv_s0, recv_m0, recv_l0 = attention_with_push(
        query_rows[:, width:],
        kept_k.T,
        kept_v,
        bias.reshape(1, slots * TILE),
        new_keys[:, DH:].T,
        new_values[:, DH:],
        query_place.reshape(total_rows, 1),
        key_place.reshape(1, q_dev),
        sends0,
        ctx_count,
    )
    recv_s1, recv_m1, recv_l1 = push(
        (
            sums1.reshape(ctx_count, q_dev, width),
            maxima1.reshape(ctx_count, q_dev, group_size),
            totals1.reshape(ctx_count, q_dev, group_size),
        ),
        "ctx",
        ctx_count,
        True,
        1,
    )
    part_max = jnp.concatenate([recv_m0, recv_m1], axis=2)
    part_total = jnp.concatenate([recv_l0, recv_l1], axis=2)
    part_sum = jnp.stack([recv_s0, recv_s1], axis=1)
    top_max = jnp.max(part_max, axis=0)
    factor = jnp.exp2((part_max - top_max[None]) * (DH ** (-0.5) * LOG2E))
    denominator = jnp.sum(part_total * factor, axis=0)
    attn_rows = combine(part_sum, factor, denominator)
    (attn_blocks,) = push((attn_rows,), "ctx", ctx_count, False, 2)
    projected = jnp.dot(
        attn_blocks.reshape(total_rows, q_local * DH),
        out_weight,
        preferred_element_type=jnp.float32,
    )
    out_rows = total_rows // tp_count
    (proj_parts,) = push(
        (projected.reshape(tp_count, out_rows, projected.shape[1]),), "tp", tp_count, True, 3
    )
    return jnp.sum(proj_parts, axis=0)


def solution(mesh):
    return jax.shard_map(
        body,
        mesh=mesh,
        in_specs=(
            P("ctx", "tp"),
            P("ctx", "tp"),
            P("ctx", "tp"),
            P("ctx", "tp"),
            P("ctx", "tp"),
            P("ctx", "tp", None),
            P("ctx", "tp"),
            P(),
            P("tp", "ctx"),
        ),
        out_specs=P("tp", "ctx"),
        check_vma=False,
    )
```

```python
import functools

import jax
import jax.numpy as jnp
from jax import lax
from jax.experimental import pallas as pl
from jax.experimental.pallas import tpu as pltpu
from jax.sharding import PartitionSpec as P

DH = 128
TILE = 128
TB = 4
MESH = pl.DeviceIdType.MESH

NEG_INF = -jnp.inf


def push_kernel(axis, n, per_dest, count, *refs):
    x_refs = refs[:count]
    y_refs = refs[count : 2 * count]
    send_sem, recv_sem, local_sem = refs[2 * count :]
    me = lax.axis_index(axis)
    barrier = pltpu.get_barrier_semaphore()
    for k in range(1, n):
        peer = lax.rem(me + k, n)
        pl.semaphore_signal(barrier, inc=1, device_id={axis: peer}, device_id_type=MESH)
    pl.semaphore_wait(barrier, n - 1)
    copies = []
    for a in range(count):
        for k in range(1, n):
            peer = lax.rem(me + k, n)
            src = x_refs[a].at[peer] if per_dest else x_refs[a]
            copy = pltpu.make_async_remote_copy(
                src_ref=src,
                dst_ref=y_refs[a].at[me],
                send_sem=send_sem.at[a, k],
                recv_sem=recv_sem.at[a, k],
                device_id={axis: peer},
                device_id_type=MESH,
            )
            copy.start()
            copies.append(copy)
    locals_ = []
    for a in range(count):
        src = x_refs[a].at[me] if per_dest else x_refs[a]
        local = pltpu.make_async_copy(src, y_refs[a].at[me], local_sem.at[a])
        local.start()
        locals_.append(local)
    for local in locals_:
        local.wait()
    for copy in copies:
        copy.wait()


def push(xs, axis, n, per_dest, collective_id):
    count = len(xs)
    out_shape = []
    for x in xs:
        block = x.shape[1:] if per_dest else x.shape
        out_shape.append(jax.ShapeDtypeStruct((n,) + tuple(block), x.dtype))
    any_spec = pl.BlockSpec(memory_space=pl.ANY)
    return pl.pallas_call(
        functools.partial(push_kernel, axis, n, per_dest, count),
        out_shape=tuple(out_shape),
        in_specs=[any_spec] * count,
        out_specs=tuple([any_spec] * count),
        scratch_shapes=[
            pltpu.SemaphoreType.DMA((count, n)),
            pltpu.SemaphoreType.DMA((count, n)),
            pltpu.SemaphoreType.DMA((count,)),
        ],
        compiler_params=pltpu.CompilerParams(collective_id=collective_id, has_side_effects=True),
    )(*xs)


TPB = 8
LOG2E = 1.4426950408889634


def dot_nt(a, b):
    return jnp.dot(a, b, preferred_element_type=jnp.float32)


def attn_kernel(tpb, group_size, kt_ref, cnt_ref, q_ref, *refs):
    k_refs = refs[:tpb]
    v_refs = refs[tpb : 2 * tpb]
    nk_ref, nv_ref, qp_ref, kp_ref = refs[2 * tpb : 2 * tpb + 4]
    sum_out, m_out, l_out = refs[2 * tpb + 4 : 2 * tpb + 7]
    m_scr, acc_ref = refs[2 * tpb + 7 :]
    g = pl.program_id(0)
    t = pl.program_id(1)
    last = pl.num_programs(1) - 1
    live = cnt_ref[g]
    coef = DH ** (-0.5) * LOG2E

    @pl.when(t == 0)
    def _():
        m_scr[...] = jnp.full(m_scr.shape, NEG_INF, jnp.float32)
        acc_ref[...] = jnp.zeros(acc_ref.shape, jnp.float32)

    def fold(h, keys, values_ext, mask):
        cols = pl.ds(pl.multiple_of(h * DH, DH), DH)
        s = dot_nt(q_ref[:, cols], keys)
        if mask is not None:
            s = s + mask
        m_prev = m_scr[h]
        m_new = jnp.maximum(m_prev, s.max(axis=1, keepdims=True))
        alpha = jnp.exp2((m_prev - m_new) * coef)
        p = jnp.exp2(s * coef - m_new[:, :1] * coef)
        m_scr[h] = m_new
        acc_ref[h] = acc_ref[h] * alpha[:, :1] + jnp.dot(
            p.astype(jnp.bfloat16), values_ext, preferred_element_type=jnp.float32
        )

    def with_ones(values):
        return jnp.concatenate([values, jnp.ones(values.shape, values.dtype)], axis=1)

    def tiles_step(masked):
        keys = jnp.concatenate([k[...] for k in k_refs], axis=1)
        values_ext = with_ones(jnp.concatenate([v[...] for v in v_refs], axis=0))
        mask = None
        if masked:
            slot = t * tpb + lax.broadcasted_iota(jnp.int32, (1, tpb * TILE), 1) // TILE
            mask = jnp.where(slot < live, 0.0, NEG_INF).astype(jnp.float32)

        def head_body(h, carry):
            fold(h, keys, values_ext, mask)
            return carry

        lax.fori_loop(0, group_size, head_body, 0)

    @pl.when((t + 1) * tpb <= live)
    def _():
        tiles_step(False)

    @pl.when(jnp.logical_and(t * tpb < live, (t + 1) * tpb > live))
    def _():
        tiles_step(True)

    @pl.when(t == last)
    def _():
        causal = jnp.where(qp_ref[...] >= kp_ref[...], 0.0, NEG_INF).astype(jnp.float32)
        nk = nk_ref[...]
        nv_ext = with_ones(nv_ref[...])

        def head_body(h, carry):
            fold(h, nk, nv_ext, causal)
            return carry

        lax.fori_loop(0, group_size, head_body, 0)
        for h in range(group_size):
            acc = acc_ref[h]
            sum_out[:, h * DH : (h + 1) * DH] = acc[:, :DH].astype(sum_out.dtype)
            m_out[:, h : h + 1] = m_scr[h][:, :1]
            l_out[:, h : h + 1] = acc[:, DH : DH + 1]


def local_attention(query_rows, cache_keys, cache_values, new_keys, new_values, keep, live, query_place, key_place):
    rows, width = query_rows.shape
    kv_local = new_keys.shape[1] // DH
    group_size = width // DH // kv_local
    slots = keep.shape[1]
    steps = slots // TPB
    q_new = new_keys.shape[0]

    def tile_map(j):
        def index_map(g, t, kt_ref, cnt_ref):
            return (kt_ref[g, jnp.minimum(t * TPB + j, cnt_ref[g] - 1)], g)

        return index_map

    tile_spec = [pl.BlockSpec((TILE, DH), tile_map(j)) for j in range(TPB)]

    def tile_map_t(j):
        def index_map(g, t, kt_ref, cnt_ref):
            return (g, kt_ref[g, jnp.minimum(t * TPB + j, cnt_ref[g] - 1)])

        return index_map

    tile_spec_t = [pl.BlockSpec((DH, TILE), tile_map_t(j)) for j in range(TPB)]
    grid_spec = pltpu.PrefetchScalarGridSpec(
        num_scalar_prefetch=2,
        grid=(kv_local, steps),
        in_specs=[pl.BlockSpec((rows, group_size * DH), lambda g, t, kt, cn: (0, g))]
        + tile_spec_t
        + tile_spec
        + [
            pl.BlockSpec((DH, q_new), lambda g, t, kt, cn: (g, 0)),
            pl.BlockSpec((q_new, DH), lambda g, t, kt, cn: (0, g)),
            pl.BlockSpec((rows, 1), lambda g, t, kt, cn: (0, 0)),
            pl.BlockSpec((1, q_new), lambda g, t, kt, cn: (0, 0)),
        ],
        out_specs=[
            pl.BlockSpec((rows, group_size * DH), lambda g, t, kt, cn: (0, g)),
            pl.BlockSpec((None, rows, group_size), lambda g, t, kt, cn: (g, 0, 0)),
            pl.BlockSpec((None, rows, group_size), lambda g, t, kt, cn: (g, 0, 0)),
        ],
        scratch_shapes=[
            pltpu.VMEM((group_size, rows, DH), jnp.float32),
            pltpu.VMEM((group_size, rows, 2 * DH), jnp.float32),
        ],
    )
    keys_total = slots * TILE + q_new
    flops = 4 * rows * kv_local * group_size * keys_total * DH
    cost = pl.CostEstimate(
        flops=flops,
        transcendentals=rows * kv_local * group_size * keys_total,
        bytes_accessed=rows * width * 2 + rows * width * 4 + 2 * kv_local * slots * TILE * DH * 2,
    )
    return pl.pallas_call(
        functools.partial(attn_kernel, TPB, group_size),
        grid_spec=grid_spec,
        out_shape=[
            jax.ShapeDtypeStruct((rows, width), jnp.bfloat16),
            jax.ShapeDtypeStruct((kv_local, rows, group_size), jnp.float32),
            jax.ShapeDtypeStruct((kv_local, rows, group_size), jnp.float32),
        ],
        compiler_params=pltpu.CompilerParams(
            dimension_semantics=("arbitrary", "arbitrary"), vmem_limit_bytes=56 * 1024 * 1024
        ),
        cost_estimate=cost,
    )(keep, live, query_rows, *([cache_keys.T] * TPB), *([cache_values] * TPB), new_keys.T, new_values, query_place, key_place)


def dense_fold(q_ref, h, keys_t, values_ext, mask, m_scr, acc_ref):
    coef = DH ** (-0.5) * LOG2E
    cols = pl.ds(pl.multiple_of(h * DH, DH), DH)
    s = jnp.dot(q_ref[:, cols], keys_t, preferred_element_type=jnp.float32) + mask
    m_prev = m_scr[h]
    m_new = jnp.maximum(m_prev, s.max(axis=1, keepdims=True))
    alpha = jnp.exp2((m_prev - m_new) * coef)
    p = jnp.exp2(s * coef - m_new[:, :1] * coef)
    m_scr[h] = m_new
    acc_ref[h] = acc_ref[h] * alpha[:, :1] + jnp.dot(
        p.astype(jnp.bfloat16), values_ext, preferred_element_type=jnp.float32
    )


def attn_push_kernel(n, group_size, per_dest, count, *refs):
    q_ref, kt_ref, v_ref, bias_ref, nkt_ref, nv_ref, qp_ref, kp_ref = refs[:8]
    srcs = refs[8 : 8 + count]
    sum_out, m_out, l_out = refs[8 + count : 11 + count]
    dsts = refs[11 + count : 11 + 2 * count]
    m_scr, acc_ref, send_sem, recv_sem, local_sem = refs[11 + 2 * count :]
    t = pl.program_id(0)
    last = pl.num_programs(0) - 1
    me = lax.axis_index("ctx")

    def remote_copies():
        out = []
        for a in range(count):
            for k in range(1, n):
                peer = lax.rem(me + k, n)
                out.append(
                    pltpu.make_async_remote_copy(
                        src_ref=srcs[a].at[peer] if per_dest else srcs[a],
                        dst_ref=dsts[a].at[me],
                        send_sem=send_sem.at[a, k],
                        recv_sem=recv_sem.at[a, k],
                        device_id={"ctx": peer},
                        device_id_type=MESH,
                    )
                )
        return out

    def local_copies():
        return [
            pltpu.make_async_copy(
                srcs[a].at[me] if per_dest else srcs[a], dsts[a].at[me], local_sem.at[a]
            )
            for a in range(count)
        ]

    def with_ones(values):
        return jnp.concatenate([values, jnp.ones(values.shape, values.dtype)], axis=1)

    @pl.when(t == 0)
    def _():
        barrier = pltpu.get_barrier_semaphore()
        for k in range(1, n):
            peer = lax.rem(me + k, n)
            pl.semaphore_signal(barrier, inc=1, device_id={"ctx": peer}, device_id_type=MESH)
        pl.semaphore_wait(barrier, n - 1)
        for c in remote_copies():
            c.start()
        for c in local_copies():
            c.start()
        m_scr[...] = jnp.full(m_scr.shape, NEG_INF, jnp.float32)
        acc_ref[...] = jnp.zeros(acc_ref.shape, jnp.float32)

    keys_t = kt_ref[...]
    values_ext = with_ones(v_ref[...])
    mask = bias_ref[...]

    def head_body(h, carry):
        dense_fold(q_ref, h, keys_t, values_ext, mask, m_scr, acc_ref)
        return carry

    lax.fori_loop(0, group_size, head_body, 0)

    @pl.when(t == last)
    def _():
        causal = jnp.where(qp_ref[...] >= kp_ref[...], 0.0, NEG_INF).astype(jnp.float32)
        nkt = nkt_ref[...]
        nv_ext = with_ones(nv_ref[...])

        def new_body(h, carry):
            dense_fold(q_ref, h, nkt, nv_ext, causal, m_scr, acc_ref)
            return carry

        lax.fori_loop(0, group_size, new_body, 0)
        for h in range(group_size):
            acc = acc_ref[h]
            sum_out[:, h * DH : (h + 1) * DH] = acc[:, :DH].astype(sum_out.dtype)
            m_out[:, h : h + 1] = m_scr[h][:, :1]
            l_out[:, h : h + 1] = acc[:, DH : DH + 1]
        for c in local_copies():
            c.wait()
        for c in remote_copies():
            c.wait()


def attention_with_push(query_rows, keys_t, values, bias, new_keys_t, new_values, query_place, key_place, sends, n, per_dest, collective_id):
    rows, width = query_rows.shape
    group_size = width // DH
    total_keys = keys_t.shape[1]
    step_keys = TPB * TILE
    steps = total_keys // step_keys
    q_new = new_values.shape[0]
    any_spec = pl.BlockSpec(memory_space=pl.ANY)
    count = len(sends)
    recv_shapes = [
        jax.ShapeDtypeStruct((n,) + tuple(x.shape[1:] if per_dest else x.shape), x.dtype)
        for x in sends
    ]
    flops = 4 * rows * group_size * (total_keys + q_new) * DH
    cost = pl.CostEstimate(
        flops=flops,
        transcendentals=rows * group_size * (total_keys + q_new),
        bytes_accessed=rows * width * 4 + 2 * total_keys * DH * 2,
    )
    return pl.pallas_call(
        functools.partial(attn_push_kernel, n, group_size, per_dest, count),
        grid=(steps,),
        in_specs=[
            pl.BlockSpec((rows, width), lambda t: (0, 0)),
            pl.BlockSpec((DH, step_keys), lambda t: (0, t)),
            pl.BlockSpec((step_keys, DH), lambda t: (t, 0)),
            pl.BlockSpec((1, step_keys), lambda t: (0, t)),
            pl.BlockSpec((DH, q_new), lambda t: (0, 0)),
            pl.BlockSpec((q_new, DH), lambda t: (0, 0)),
            pl.BlockSpec((rows, 1), lambda t: (0, 0)),
            pl.BlockSpec((1, q_new), lambda t: (0, 0)),
        ]
        + [any_spec] * count,
        out_specs=[
            pl.BlockSpec((rows, width), lambda t: (0, 0)),
            pl.BlockSpec((rows, group_size), lambda t: (0, 0)),
            pl.BlockSpec((rows, group_size), lambda t: (0, 0)),
        ]
        + [any_spec] * count,
        out_shape=[
            jax.ShapeDtypeStruct((rows, width), jnp.bfloat16),
            jax.ShapeDtypeStruct((rows, group_size), jnp.float32),
            jax.ShapeDtypeStruct((rows, group_size), jnp.float32),
        ]
        + recv_shapes,
        scratch_shapes=[
            pltpu.VMEM((group_size, rows, DH), jnp.float32),
            pltpu.VMEM((group_size, rows, 2 * DH), jnp.float32),
            pltpu.SemaphoreType.DMA((count, n)),
            pltpu.SemaphoreType.DMA((count, n)),
            pltpu.SemaphoreType.DMA((count,)),
        ],
        compiler_params=pltpu.CompilerParams(
            collective_id=collective_id, has_side_effects=True, vmem_limit_bytes=56 * 1024 * 1024
        ),
        cost_estimate=cost,
    )(query_rows, keys_t, values, bias, new_keys_t, new_values, query_place, key_place, *sends)


def combine_kernel(heads, part_ref, fac_ref, den_ref, out_ref):
    senders = part_ref.shape[0]
    width = part_ref.shape[3]
    half = width // DH

    def sender_body(i, acc):
        fac = fac_ref[i]
        out = []
        for h in range(heads):
            j, c = divmod(h, half)
            blk = part_ref[i, j][:, c * DH : (c + 1) * DH].astype(jnp.float32)
            out.append(acc[h] + blk * fac[:, h : h + 1])
        return tuple(out)

    rows = out_ref.shape[0]
    start = tuple(jnp.zeros((rows, DH), jnp.float32) for _ in range(heads))
    acc = lax.fori_loop(0, senders, sender_body, start)
    den = den_ref[...]
    for h in range(heads):
        out_ref[:, h * DH : (h + 1) * DH] = (acc[h] / den[:, h : h + 1]).astype(out_ref.dtype)


def combine(part_sum, factor, denominator):
    senders, groups, rows, width = part_sum.shape
    heads = groups * width // DH
    vmem = pl.BlockSpec(memory_space=pltpu.VMEM)
    return pl.pallas_call(
        functools.partial(combine_kernel, heads),
        out_shape=jax.ShapeDtypeStruct((rows, heads * DH), jnp.bfloat16),
        in_specs=[vmem, vmem, vmem],
        out_specs=vmem,
        compiler_params=pltpu.CompilerParams(vmem_limit_bytes=32 * 1024 * 1024),
    )(part_sum, factor, denominator)


def body(
    queries,
    new_keys,
    new_values,
    cache_keys,
    cache_values,
    keep_tiles,
    tile_count,
    owner_slot,
    out_weight,
):
    q_dev = queries.shape[0]
    kv_local = new_keys.shape[1] // DH
    q_local = queries.shape[1] // DH
    group_size = q_local // kv_local
    ctx_count = lax.axis_size("ctx")
    tp_count = lax.axis_size("tp")
    total_rows = q_dev * ctx_count
    my_index = lax.axis_index("ctx")
    key_place = owner_slot[my_index] * q_dev + jnp.arange(q_dev, dtype=jnp.int32)
    width = group_size * DH
    (q0_blocks,) = push((queries[:, :width],), "ctx", ctx_count, False, 0)
    query_place = (
        owner_slot[:, None] * q_dev + jnp.arange(q_dev, dtype=jnp.int32)[None, :]
    ).reshape(total_rows, 1)
    key_place = key_place.reshape(1, q_dev)
    slots = keep_tiles.shape[2]
    slot_ids = jnp.arange(slots * TILE, dtype=jnp.int32) // TILE

    def dense_head(g):
        cols = slice(g * DH, (g + 1) * DH)
        tiles_k = cache_keys[:, cols].reshape(-1, TILE, DH)
        tiles_v = cache_values[:, cols].reshape(-1, TILE, DH)
        kept_k = jnp.take(tiles_k, keep_tiles[0, g], axis=0).reshape(slots * TILE, DH)
        kept_v = jnp.take(tiles_v, keep_tiles[0, g], axis=0).reshape(slots * TILE, DH)
        bias = jnp.where(slot_ids < tile_count[0, g], 0.0, NEG_INF).astype(jnp.float32)
        return kept_k.T, kept_v, bias.reshape(1, slots * TILE), new_keys[:, cols].T, new_values[:, cols]

    sums0, maxima0, totals0, q1_blocks = attention_with_push(
        q0_blocks.reshape(total_rows, width),
        *dense_head(0),
        query_place,
        key_place,
        (queries[:, width:],),
        ctx_count,
        False,
        5,
    )
    sends0 = (
        sums0.reshape(ctx_count, q_dev, width),
        maxima0.reshape(ctx_count, q_dev, group_size),
        totals0.reshape(ctx_count, q_dev, group_size),
    )
    sums1, maxima1, totals1, recv_s0, recv_m0, recv_l0 = attention_with_push(
        q1_blocks.reshape(total_rows, width),
        *dense_head(1),
        query_place,
        key_place,
        sends0,
        ctx_count,
        True,
        4,
    )
    recv_s1, recv_m1, recv_l1 = push(
        (
            sums1.reshape(ctx_count, q_dev, width),
            maxima1.reshape(ctx_count, q_dev, group_size),
            totals1.reshape(ctx_count, q_dev, group_size),
        ),
        "ctx",
        ctx_count,
        True,
        1,
    )
    part_max = jnp.concatenate([recv_m0, recv_m1], axis=2)
    part_total = jnp.concatenate([recv_l0, recv_l1], axis=2)
    part_sum = jnp.stack([recv_s0, recv_s1], axis=1)
    top_max = jnp.max(part_max, axis=0)
    factor = jnp.exp2((part_max - top_max[None]) * (DH ** (-0.5) * LOG2E))
    denominator = jnp.sum(part_total * factor, axis=0)
    attn_rows = combine(part_sum, factor, denominator)
    (attn_blocks,) = push((attn_rows,), "ctx", ctx_count, False, 2)
    projected = jnp.dot(
        attn_blocks.reshape(total_rows, q_local * DH),
        out_weight,
        preferred_element_type=jnp.float32,
    )
    out_rows = total_rows // tp_count
    (proj_parts,) = push(
        (projected.reshape(tp_count, out_rows, projected.shape[1]),), "tp", tp_count, True, 3
    )
    return jnp.sum(proj_parts, axis=0)


def solution(mesh):
    return jax.shard_map(
        body,
        mesh=mesh,
        in_specs=(
            P("ctx", "tp"),
            P("ctx", "tp"),
            P("ctx", "tp"),
            P("ctx", "tp"),
            P("ctx", "tp"),
            P("ctx", "tp", None),
            P("ctx", "tp"),
            P(),
            P("tp", "ctx"),
        ),
        out_specs=P("tp", "ctx"),
        check_vma=False,
    )
```

```python
import functools

import jax
import jax.numpy as jnp
from jax import lax
from jax.experimental import pallas as pl
from jax.experimental.pallas import tpu as pltpu
from jax.sharding import PartitionSpec as P

DH = 128
TILE = 128
TB = 4
MESH = pl.DeviceIdType.MESH

NEG_INF = -jnp.inf


def push_kernel(axis, n, per_dest, count, *refs):
    x_refs = refs[:count]
    y_refs = refs[count : 2 * count]
    send_sem, recv_sem, local_sem = refs[2 * count :]
    me = lax.axis_index(axis)
    barrier = pltpu.get_barrier_semaphore()
    for k in range(1, n):
        peer = lax.rem(me + k, n)
        pl.semaphore_signal(barrier, inc=1, device_id={axis: peer}, device_id_type=MESH)
    pl.semaphore_wait(barrier, n - 1)
    copies = []
    for a in range(count):
        for k in range(1, n):
            peer = lax.rem(me + k, n)
            src = x_refs[a].at[peer] if per_dest else x_refs[a]
            copy = pltpu.make_async_remote_copy(
                src_ref=src,
                dst_ref=y_refs[a].at[me],
                send_sem=send_sem.at[a, k],
                recv_sem=recv_sem.at[a, k],
                device_id={axis: peer},
                device_id_type=MESH,
            )
            copy.start()
            copies.append(copy)
    locals_ = []
    for a in range(count):
        src = x_refs[a].at[me] if per_dest else x_refs[a]
        local = pltpu.make_async_copy(src, y_refs[a].at[me], local_sem.at[a])
        local.start()
        locals_.append(local)
    for local in locals_:
        local.wait()
    for copy in copies:
        copy.wait()


def push(xs, axis, n, per_dest, collective_id):
    count = len(xs)
    out_shape = []
    for x in xs:
        block = x.shape[1:] if per_dest else x.shape
        out_shape.append(jax.ShapeDtypeStruct((n,) + tuple(block), x.dtype))
    any_spec = pl.BlockSpec(memory_space=pl.ANY)
    return pl.pallas_call(
        functools.partial(push_kernel, axis, n, per_dest, count),
        out_shape=tuple(out_shape),
        in_specs=[any_spec] * count,
        out_specs=tuple([any_spec] * count),
        scratch_shapes=[
            pltpu.SemaphoreType.DMA((count, n)),
            pltpu.SemaphoreType.DMA((count, n)),
            pltpu.SemaphoreType.DMA((count,)),
        ],
        compiler_params=pltpu.CompilerParams(collective_id=collective_id, has_side_effects=True),
    )(*xs)


TPB = 8
LOG2E = 1.4426950408889634


def dot_nt(a, b):
    return jnp.dot(a, b, preferred_element_type=jnp.float32)


def attn_kernel(tpb, group_size, kt_ref, cnt_ref, q_ref, *refs):
    k_refs = refs[:tpb]
    v_refs = refs[tpb : 2 * tpb]
    nk_ref, nv_ref, qp_ref, kp_ref = refs[2 * tpb : 2 * tpb + 4]
    sum_out, m_out, l_out = refs[2 * tpb + 4 : 2 * tpb + 7]
    m_scr, acc_ref = refs[2 * tpb + 7 :]
    g = pl.program_id(0)
    t = pl.program_id(1)
    last = pl.num_programs(1) - 1
    live = cnt_ref[g]
    coef = DH ** (-0.5) * LOG2E

    @pl.when(t == 0)
    def _():
        m_scr[...] = jnp.full(m_scr.shape, NEG_INF, jnp.float32)
        acc_ref[...] = jnp.zeros(acc_ref.shape, jnp.float32)

    def fold(h, keys, values_ext, mask):
        cols = pl.ds(pl.multiple_of(h * DH, DH), DH)
        s = dot_nt(q_ref[:, cols], keys)
        if mask is not None:
            s = s + mask
        m_prev = m_scr[h]
        m_new = jnp.maximum(m_prev, s.max(axis=1, keepdims=True))
        alpha = jnp.exp2((m_prev - m_new) * coef)
        p = jnp.exp2(s * coef - m_new[:, :1] * coef)
        m_scr[h] = m_new
        acc_ref[h] = acc_ref[h] * alpha[:, :1] + jnp.dot(
            p.astype(jnp.bfloat16), values_ext, preferred_element_type=jnp.float32
        )

    def with_ones(values):
        return jnp.concatenate([values, jnp.ones(values.shape, values.dtype)], axis=1)

    def tiles_step(masked):
        keys = jnp.concatenate([k[...] for k in k_refs], axis=1)
        values_ext = with_ones(jnp.concatenate([v[...] for v in v_refs], axis=0))
        mask = None
        if masked:
            slot = t * tpb + lax.broadcasted_iota(jnp.int32, (1, tpb * TILE), 1) // TILE
            mask = jnp.where(slot < live, 0.0, NEG_INF).astype(jnp.float32)

        def head_body(h, carry):
            fold(h, keys, values_ext, mask)
            return carry

        lax.fori_loop(0, group_size, head_body, 0)

    @pl.when((t + 1) * tpb <= live)
    def _():
        tiles_step(False)

    @pl.when(jnp.logical_and(t * tpb < live, (t + 1) * tpb > live))
    def _():
        tiles_step(True)

    @pl.when(t == last)
    def _():
        causal = jnp.where(qp_ref[...] >= kp_ref[...], 0.0, NEG_INF).astype(jnp.float32)
        nk = nk_ref[...]
        nv_ext = with_ones(nv_ref[...])

        def head_body(h, carry):
            fold(h, nk, nv_ext, causal)
            return carry

        lax.fori_loop(0, group_size, head_body, 0)
        for h in range(group_size):
            acc = acc_ref[h]
            sum_out[:, h * DH : (h + 1) * DH] = acc[:, :DH].astype(sum_out.dtype)
            m_out[:, h : h + 1] = m_scr[h][:, :1]
            l_out[:, h : h + 1] = acc[:, DH : DH + 1]


def local_attention(query_rows, cache_keys, cache_values, new_keys, new_values, keep, live, query_place, key_place):
    rows, width = query_rows.shape
    kv_local = new_keys.shape[1] // DH
    group_size = width // DH // kv_local
    slots = keep.shape[1]
    steps = slots // TPB
    q_new = new_keys.shape[0]

    def tile_map(j):
        def index_map(g, t, kt_ref, cnt_ref):
            return (kt_ref[g, jnp.minimum(t * TPB + j, cnt_ref[g] - 1)], g)

        return index_map

    tile_spec = [pl.BlockSpec((TILE, DH), tile_map(j)) for j in range(TPB)]

    def tile_map_t(j):
        def index_map(g, t, kt_ref, cnt_ref):
            return (g, kt_ref[g, jnp.minimum(t * TPB + j, cnt_ref[g] - 1)])

        return index_map

    tile_spec_t = [pl.BlockSpec((DH, TILE), tile_map_t(j)) for j in range(TPB)]
    grid_spec = pltpu.PrefetchScalarGridSpec(
        num_scalar_prefetch=2,
        grid=(kv_local, steps),
        in_specs=[pl.BlockSpec((rows, group_size * DH), lambda g, t, kt, cn: (0, g))]
        + tile_spec_t
        + tile_spec
        + [
            pl.BlockSpec((DH, q_new), lambda g, t, kt, cn: (g, 0)),
            pl.BlockSpec((q_new, DH), lambda g, t, kt, cn: (0, g)),
            pl.BlockSpec((rows, 1), lambda g, t, kt, cn: (0, 0)),
            pl.BlockSpec((1, q_new), lambda g, t, kt, cn: (0, 0)),
        ],
        out_specs=[
            pl.BlockSpec((rows, group_size * DH), lambda g, t, kt, cn: (0, g)),
            pl.BlockSpec((None, rows, group_size), lambda g, t, kt, cn: (g, 0, 0)),
            pl.BlockSpec((None, rows, group_size), lambda g, t, kt, cn: (g, 0, 0)),
        ],
        scratch_shapes=[
            pltpu.VMEM((group_size, rows, DH), jnp.float32),
            pltpu.VMEM((group_size, rows, 2 * DH), jnp.float32),
        ],
    )
    keys_total = slots * TILE + q_new
    flops = 4 * rows * kv_local * group_size * keys_total * DH
    cost = pl.CostEstimate(
        flops=flops,
        transcendentals=rows * kv_local * group_size * keys_total,
        bytes_accessed=rows * width * 2 + rows * width * 4 + 2 * kv_local * slots * TILE * DH * 2,
    )
    return pl.pallas_call(
        functools.partial(attn_kernel, TPB, group_size),
        grid_spec=grid_spec,
        out_shape=[
            jax.ShapeDtypeStruct((rows, width), jnp.bfloat16),
            jax.ShapeDtypeStruct((kv_local, rows, group_size), jnp.float32),
            jax.ShapeDtypeStruct((kv_local, rows, group_size), jnp.float32),
        ],
        compiler_params=pltpu.CompilerParams(
            dimension_semantics=("arbitrary", "arbitrary"), vmem_limit_bytes=56 * 1024 * 1024
        ),
        cost_estimate=cost,
    )(keep, live, query_rows, *([cache_keys.T] * TPB), *([cache_values] * TPB), new_keys.T, new_values, query_place, key_place)


def dense_fold(q_ref, h, keys_t, values_ext, mask, m_scr, acc_ref):
    coef = DH ** (-0.5) * LOG2E
    cols = pl.ds(pl.multiple_of(h * DH, DH), DH)
    s = jnp.dot(q_ref[:, cols], keys_t, preferred_element_type=jnp.float32) + mask
    m_prev = m_scr[h]
    m_new = jnp.maximum(m_prev, s.max(axis=1, keepdims=True))
    alpha = jnp.exp2((m_prev - m_new) * coef)
    p = jnp.exp2(s * coef - m_new[:, :1] * coef)
    m_scr[h] = m_new
    acc_ref[h] = acc_ref[h] * alpha[:, :1] + jnp.dot(
        p.astype(jnp.bfloat16), values_ext, preferred_element_type=jnp.float32
    )


def attn_push_kernel(n, group_size, per_dest, count, *refs):
    q_ref, kt_ref, v_ref, bias_ref, nkt_ref, nv_ref, qp_ref, kp_ref = refs[:8]
    srcs = refs[8 : 8 + count]
    sum_out, m_out, l_out = refs[8 + count : 11 + count]
    dsts = refs[11 + count : 11 + 2 * count]
    m_scr, acc_ref, send_sem, recv_sem, local_sem = refs[11 + 2 * count :]
    t = pl.program_id(0)
    last = pl.num_programs(0) - 1
    me = lax.axis_index("ctx")

    def remote_copies():
        out = []
        for a in range(count):
            for k in range(1, n):
                peer = lax.rem(me + k, n)
                out.append(
                    pltpu.make_async_remote_copy(
                        src_ref=srcs[a].at[peer] if per_dest[a] else srcs[a],
                        dst_ref=dsts[a].at[me],
                        send_sem=send_sem.at[a, k],
                        recv_sem=recv_sem.at[a, k],
                        device_id={"ctx": peer},
                        device_id_type=MESH,
                    )
                )
        return out

    def local_copies():
        return [
            pltpu.make_async_copy(
                srcs[a].at[me] if per_dest[a] else srcs[a], dsts[a].at[me], local_sem.at[a]
            )
            for a in range(count)
        ]

    def with_ones(values):
        return jnp.concatenate([values, jnp.ones(values.shape, values.dtype)], axis=1)

    @pl.when(t == 0)
    def _():
        barrier = pltpu.get_barrier_semaphore()
        for k in range(1, n):
            peer = lax.rem(me + k, n)
            pl.semaphore_signal(barrier, inc=1, device_id={"ctx": peer}, device_id_type=MESH)
        pl.semaphore_wait(barrier, n - 1)
        for c in remote_copies():
            c.start()
        for c in local_copies():
            c.start()
        m_scr[...] = jnp.full(m_scr.shape, NEG_INF, jnp.float32)
        acc_ref[...] = jnp.zeros(acc_ref.shape, jnp.float32)

    keys_t = kt_ref[...]
    values_ext = with_ones(v_ref[...])
    mask = bias_ref[...]

    def head_body(h, carry):
        dense_fold(q_ref, h, keys_t, values_ext, mask, m_scr, acc_ref)
        return carry

    lax.fori_loop(0, group_size, head_body, 0)

    @pl.when(t == last)
    def _():
        causal = jnp.where(qp_ref[...] >= kp_ref[...], 0.0, NEG_INF).astype(jnp.float32)
        nkt = nkt_ref[...]
        nv_ext = with_ones(nv_ref[...])

        def new_body(h, carry):
            dense_fold(q_ref, h, nkt, nv_ext, causal, m_scr, acc_ref)
            return carry

        lax.fori_loop(0, group_size, new_body, 0)
        for h in range(group_size):
            acc = acc_ref[h]
            sum_out[:, h * DH : (h + 1) * DH] = acc[:, :DH].astype(sum_out.dtype)
            m_out[:, h : h + 1] = m_scr[h][:, :1]
            l_out[:, h : h + 1] = acc[:, DH : DH + 1]
        for c in local_copies():
            c.wait()
        for c in remote_copies():
            c.wait()


def attention_with_push(query_rows, keys_t, values, bias, new_keys_t, new_values, query_place, key_place, sends, n, per_dest, collective_id):
    rows, width = query_rows.shape
    group_size = width // DH
    total_keys = keys_t.shape[1]
    step_keys = TPB * TILE
    steps = total_keys // step_keys
    q_new = new_values.shape[0]
    any_spec = pl.BlockSpec(memory_space=pl.ANY)
    count = len(sends)
    recv_shapes = [
        jax.ShapeDtypeStruct((n,) + tuple(x.shape[1:] if d else x.shape), x.dtype)
        for x, d in zip(sends, per_dest)
    ]
    flops = 4 * rows * group_size * (total_keys + q_new) * DH
    cost = pl.CostEstimate(
        flops=flops,
        transcendentals=rows * group_size * (total_keys + q_new),
        bytes_accessed=rows * width * 4 + 2 * total_keys * DH * 2,
    )
    return pl.pallas_call(
        functools.partial(attn_push_kernel, n, group_size, per_dest, count),
        grid=(steps,),
        in_specs=[
            pl.BlockSpec((rows, width), lambda t: (0, 0)),
            pl.BlockSpec((DH, step_keys), lambda t: (0, t)),
            pl.BlockSpec((step_keys, DH), lambda t: (t, 0)),
            pl.BlockSpec((1, step_keys), lambda t: (0, t)),
            pl.BlockSpec((DH, q_new), lambda t: (0, 0)),
            pl.BlockSpec((q_new, DH), lambda t: (0, 0)),
            pl.BlockSpec((rows, 1), lambda t: (0, 0)),
            pl.BlockSpec((1, q_new), lambda t: (0, 0)),
        ]
        + [any_spec] * count,
        out_specs=[
            pl.BlockSpec((rows, width), lambda t: (0, 0)),
            pl.BlockSpec((rows, group_size), lambda t: (0, 0)),
            pl.BlockSpec((rows, group_size), lambda t: (0, 0)),
        ]
        + [any_spec] * count,
        out_shape=[
            jax.ShapeDtypeStruct((rows, width), jnp.bfloat16),
            jax.ShapeDtypeStruct((rows, group_size), jnp.float32),
            jax.ShapeDtypeStruct((rows, group_size), jnp.float32),
        ]
        + recv_shapes,
        scratch_shapes=[
            pltpu.VMEM((group_size, rows, DH), jnp.float32),
            pltpu.VMEM((group_size, rows, 2 * DH), jnp.float32),
            pltpu.SemaphoreType.DMA((count, n)),
            pltpu.SemaphoreType.DMA((count, n)),
            pltpu.SemaphoreType.DMA((count,)),
        ],
        compiler_params=pltpu.CompilerParams(
            collective_id=collective_id, has_side_effects=True, vmem_limit_bytes=56 * 1024 * 1024
        ),
        cost_estimate=cost,
    )(query_rows, keys_t, values, bias, new_keys_t, new_values, query_place, key_place, *sends)


def combine_kernel(heads, part_ref, fac_ref, den_ref, out_ref):
    senders = part_ref.shape[0]
    width = part_ref.shape[3]
    half = width // DH

    def sender_body(i, acc):
        fac = fac_ref[i]
        out = []
        for h in range(heads):
            j, c = divmod(h, half)
            blk = part_ref[i, j][:, c * DH : (c + 1) * DH].astype(jnp.float32)
            out.append(acc[h] + blk * fac[:, h : h + 1])
        return tuple(out)

    rows = out_ref.shape[0]
    start = tuple(jnp.zeros((rows, DH), jnp.float32) for _ in range(heads))
    acc = lax.fori_loop(0, senders, sender_body, start)
    den = den_ref[...]
    for h in range(heads):
        out_ref[:, h * DH : (h + 1) * DH] = (acc[h] / den[:, h : h + 1]).astype(out_ref.dtype)


def combine(part_sum, factor, denominator):
    senders, groups, rows, width = part_sum.shape
    heads = groups * width // DH
    vmem = pl.BlockSpec(memory_space=pltpu.VMEM)
    return pl.pallas_call(
        functools.partial(combine_kernel, heads),
        out_shape=jax.ShapeDtypeStruct((rows, heads * DH), jnp.bfloat16),
        in_specs=[vmem, vmem, vmem],
        out_specs=vmem,
        compiler_params=pltpu.CompilerParams(vmem_limit_bytes=32 * 1024 * 1024),
    )(part_sum, factor, denominator)


def body(
    queries,
    new_keys,
    new_values,
    cache_keys,
    cache_values,
    keep_tiles,
    tile_count,
    owner_slot,
    out_weight,
):
    q_dev = queries.shape[0]
    kv_local = new_keys.shape[1] // DH
    q_local = queries.shape[1] // DH
    group_size = q_local // kv_local
    ctx_count = lax.axis_size("ctx")
    tp_count = lax.axis_size("tp")
    total_rows = q_dev * ctx_count
    my_index = lax.axis_index("ctx")
    key_place = owner_slot[my_index] * q_dev + jnp.arange(q_dev, dtype=jnp.int32)
    pieces = 4
    piece_heads = q_local // pieces
    width = piece_heads * DH
    (q_blocks,) = push((queries[:, :width],), "ctx", ctx_count, False, 0)
    query_place = (
        owner_slot[:, None] * q_dev + jnp.arange(q_dev, dtype=jnp.int32)[None, :]
    ).reshape(total_rows, 1)
    key_place = key_place.reshape(1, q_dev)
    slots = keep_tiles.shape[2]
    slot_ids = jnp.arange(slots * TILE, dtype=jnp.int32) // TILE

    def dense_head(g):
        cols = slice(g * DH, (g + 1) * DH)
        tiles_k = cache_keys[:, cols].reshape(-1, TILE, DH)
        tiles_v = cache_values[:, cols].reshape(-1, TILE, DH)
        kept_k = jnp.take(tiles_k, keep_tiles[0, g], axis=0).reshape(slots * TILE, DH)
        kept_v = jnp.take(tiles_v, keep_tiles[0, g], axis=0).reshape(slots * TILE, DH)
        bias = jnp.where(slot_ids < tile_count[0, g], 0.0, NEG_INF).astype(jnp.float32)
        return kept_k.T, kept_v, bias.reshape(1, slots * TILE), new_keys[:, cols].T, new_values[:, cols]

    head_data = [dense_head(g) for g in range(kv_local)]
    received = []
    previous = None
    for i in range(pieces):
        sends = []
        flags = []
        if i + 1 < pieces:
            sends.append(queries[:, (i + 1) * width : (i + 2) * width])
            flags.append(False)
        if previous is not None:
            sends.extend(previous)
            flags.extend([True, True, True])
        outs = attention_with_push(
            q_blocks.reshape(total_rows, width),
            *head_data[i * kv_local // pieces],
            query_place,
            key_place,
            tuple(sends),
            ctx_count,
            tuple(flags),
            4 + i,
        )
        sums_i, maxima_i, totals_i = outs[:3]
        rest = list(outs[3:])
        if i + 1 < pieces:
            q_blocks = rest.pop(0)
        if previous is not None:
            received.append(tuple(rest))
        previous = (
            sums_i.reshape(ctx_count, q_dev, width),
            maxima_i.reshape(ctx_count, q_dev, piece_heads),
            totals_i.reshape(ctx_count, q_dev, piece_heads),
        )
    received.append(push(previous, "ctx", ctx_count, True, 1))
    part_max = jnp.concatenate([r[1] for r in received], axis=2)
    part_total = jnp.concatenate([r[2] for r in received], axis=2)
    part_sum = jnp.stack([r[0] for r in received], axis=1)
    top_max = jnp.max(part_max, axis=0)
    factor = jnp.exp2((part_max - top_max[None]) * (DH ** (-0.5) * LOG2E))
    denominator = jnp.sum(part_total * factor, axis=0)
    attn_rows = combine(part_sum, factor, denominator)
    (attn_blocks,) = push((attn_rows,), "ctx", ctx_count, False, 2)
    projected = jnp.dot(
        attn_blocks.reshape(total_rows, q_local * DH),
        out_weight,
        preferred_element_type=jnp.float32,
    )
    out_rows = total_rows // tp_count
    (proj_parts,) = push(
        (projected.reshape(tp_count, out_rows, projected.shape[1]),), "tp", tp_count, True, 3
    )
    return jnp.sum(proj_parts, axis=0)


def solution(mesh):
    return jax.shard_map(
        body,
        mesh=mesh,
        in_specs=(
            P("ctx", "tp"),
            P("ctx", "tp"),
            P("ctx", "tp"),
            P("ctx", "tp"),
            P("ctx", "tp"),
            P("ctx", "tp", None),
            P("ctx", "tp"),
            P(),
            P("tp", "ctx"),
        ),
        out_specs=P("tp", "ctx"),
        check_vma=False,
    )
```

```python
import functools

import jax
import jax.numpy as jnp
from jax import lax
from jax.experimental import pallas as pl
from jax.experimental.pallas import tpu as pltpu
from jax.sharding import PartitionSpec as P

DH = 128
TILE = 128
TB = 4
MESH = pl.DeviceIdType.MESH

NEG_INF = -jnp.inf


def push_kernel(axis, n, per_dest, count, *refs):
    x_refs = refs[:count]
    y_refs = refs[count : 2 * count]
    send_sem, recv_sem, local_sem = refs[2 * count :]
    me = lax.axis_index(axis)
    barrier = pltpu.get_barrier_semaphore()
    for k in range(1, n):
        peer = lax.rem(me + k, n)
        pl.semaphore_signal(barrier, inc=1, device_id={axis: peer}, device_id_type=MESH)
    pl.semaphore_wait(barrier, n - 1)
    copies = []
    for a in range(count):
        for k in range(1, n):
            peer = lax.rem(me + k, n)
            src = x_refs[a].at[peer] if per_dest else x_refs[a]
            copy = pltpu.make_async_remote_copy(
                src_ref=src,
                dst_ref=y_refs[a].at[me],
                send_sem=send_sem.at[a, k],
                recv_sem=recv_sem.at[a, k],
                device_id={axis: peer},
                device_id_type=MESH,
            )
            copy.start()
            copies.append(copy)
    locals_ = []
    for a in range(count):
        src = x_refs[a].at[me] if per_dest else x_refs[a]
        local = pltpu.make_async_copy(src, y_refs[a].at[me], local_sem.at[a])
        local.start()
        locals_.append(local)
    for local in locals_:
        local.wait()
    for copy in copies:
        copy.wait()


def push(xs, axis, n, per_dest, collective_id):
    count = len(xs)
    out_shape = []
    for x in xs:
        block = x.shape[1:] if per_dest else x.shape
        out_shape.append(jax.ShapeDtypeStruct((n,) + tuple(block), x.dtype))
    any_spec = pl.BlockSpec(memory_space=pl.ANY)
    return pl.pallas_call(
        functools.partial(push_kernel, axis, n, per_dest, count),
        out_shape=tuple(out_shape),
        in_specs=[any_spec] * count,
        out_specs=tuple([any_spec] * count),
        scratch_shapes=[
            pltpu.SemaphoreType.DMA((count, n)),
            pltpu.SemaphoreType.DMA((count, n)),
            pltpu.SemaphoreType.DMA((count,)),
        ],
        compiler_params=pltpu.CompilerParams(collective_id=collective_id, has_side_effects=True),
    )(*xs)


TPB = 8
LOG2E = 1.4426950408889634


def dot_nt(a, b):
    return jnp.dot(a, b, preferred_element_type=jnp.float32)


def attn_kernel(tpb, group_size, kt_ref, cnt_ref, q_ref, *refs):
    k_refs = refs[:tpb]
    v_refs = refs[tpb : 2 * tpb]
    nk_ref, nv_ref, qp_ref, kp_ref = refs[2 * tpb : 2 * tpb + 4]
    sum_out, m_out, l_out = refs[2 * tpb + 4 : 2 * tpb + 7]
    m_scr, acc_ref = refs[2 * tpb + 7 :]
    g = pl.program_id(0)
    t = pl.program_id(1)
    last = pl.num_programs(1) - 1
    live = cnt_ref[g]
    coef = DH ** (-0.5) * LOG2E

    @pl.when(t == 0)
    def _():
        m_scr[...] = jnp.full(m_scr.shape, NEG_INF, jnp.float32)
        acc_ref[...] = jnp.zeros(acc_ref.shape, jnp.float32)

    def fold(h, keys, values_ext, mask):
        cols = pl.ds(pl.multiple_of(h * DH, DH), DH)
        s = dot_nt(q_ref[:, cols], keys)
        if mask is not None:
            s = s + mask
        m_prev = m_scr[h]
        m_new = jnp.maximum(m_prev, s.max(axis=1, keepdims=True))
        alpha = jnp.exp2((m_prev - m_new) * coef)
        p = jnp.exp2(s * coef - m_new[:, :1] * coef)
        m_scr[h] = m_new
        acc_ref[h] = acc_ref[h] * alpha[:, :1] + jnp.dot(
            p.astype(jnp.bfloat16), values_ext, preferred_element_type=jnp.float32
        )

    def with_ones(values):
        return jnp.concatenate([values, jnp.ones(values.shape, values.dtype)], axis=1)

    def tiles_step(masked):
        keys = jnp.concatenate([k[...] for k in k_refs], axis=1)
        values_ext = with_ones(jnp.concatenate([v[...] for v in v_refs], axis=0))
        mask = None
        if masked:
            slot = t * tpb + lax.broadcasted_iota(jnp.int32, (1, tpb * TILE), 1) // TILE
            mask = jnp.where(slot < live, 0.0, NEG_INF).astype(jnp.float32)

        def head_body(h, carry):
            fold(h, keys, values_ext, mask)
            return carry

        lax.fori_loop(0, group_size, head_body, 0)

    @pl.when((t + 1) * tpb <= live)
    def _():
        tiles_step(False)

    @pl.when(jnp.logical_and(t * tpb < live, (t + 1) * tpb > live))
    def _():
        tiles_step(True)

    @pl.when(t == last)
    def _():
        causal = jnp.where(qp_ref[...] >= kp_ref[...], 0.0, NEG_INF).astype(jnp.float32)
        nk = nk_ref[...]
        nv_ext = with_ones(nv_ref[...])

        def head_body(h, carry):
            fold(h, nk, nv_ext, causal)
            return carry

        lax.fori_loop(0, group_size, head_body, 0)
        for h in range(group_size):
            acc = acc_ref[h]
            sum_out[:, h * DH : (h + 1) * DH] = acc[:, :DH].astype(sum_out.dtype)
            m_out[:, h : h + 1] = m_scr[h][:, :1]
            l_out[:, h : h + 1] = acc[:, DH : DH + 1]


def local_attention(query_rows, cache_keys, cache_values, new_keys, new_values, keep, live, query_place, key_place):
    rows, width = query_rows.shape
    kv_local = new_keys.shape[1] // DH
    group_size = width // DH // kv_local
    slots = keep.shape[1]
    steps = slots // TPB
    q_new = new_keys.shape[0]

    def tile_map(j):
        def index_map(g, t, kt_ref, cnt_ref):
            return (kt_ref[g, jnp.minimum(t * TPB + j, cnt_ref[g] - 1)], g)

        return index_map

    tile_spec = [pl.BlockSpec((TILE, DH), tile_map(j)) for j in range(TPB)]

    def tile_map_t(j):
        def index_map(g, t, kt_ref, cnt_ref):
            return (g, kt_ref[g, jnp.minimum(t * TPB + j, cnt_ref[g] - 1)])

        return index_map

    tile_spec_t = [pl.BlockSpec((DH, TILE), tile_map_t(j)) for j in range(TPB)]
    grid_spec = pltpu.PrefetchScalarGridSpec(
        num_scalar_prefetch=2,
        grid=(kv_local, steps),
        in_specs=[pl.BlockSpec((rows, group_size * DH), lambda g, t, kt, cn: (0, g))]
        + tile_spec_t
        + tile_spec
        + [
            pl.BlockSpec((DH, q_new), lambda g, t, kt, cn: (g, 0)),
            pl.BlockSpec((q_new, DH), lambda g, t, kt, cn: (0, g)),
            pl.BlockSpec((rows, 1), lambda g, t, kt, cn: (0, 0)),
            pl.BlockSpec((1, q_new), lambda g, t, kt, cn: (0, 0)),
        ],
        out_specs=[
            pl.BlockSpec((rows, group_size * DH), lambda g, t, kt, cn: (0, g)),
            pl.BlockSpec((None, rows, group_size), lambda g, t, kt, cn: (g, 0, 0)),
            pl.BlockSpec((None, rows, group_size), lambda g, t, kt, cn: (g, 0, 0)),
        ],
        scratch_shapes=[
            pltpu.VMEM((group_size, rows, DH), jnp.float32),
            pltpu.VMEM((group_size, rows, 2 * DH), jnp.float32),
        ],
    )
    keys_total = slots * TILE + q_new
    flops = 4 * rows * kv_local * group_size * keys_total * DH
    cost = pl.CostEstimate(
        flops=flops,
        transcendentals=rows * kv_local * group_size * keys_total,
        bytes_accessed=rows * width * 2 + rows * width * 4 + 2 * kv_local * slots * TILE * DH * 2,
    )
    return pl.pallas_call(
        functools.partial(attn_kernel, TPB, group_size),
        grid_spec=grid_spec,
        out_shape=[
            jax.ShapeDtypeStruct((rows, width), jnp.bfloat16),
            jax.ShapeDtypeStruct((kv_local, rows, group_size), jnp.float32),
            jax.ShapeDtypeStruct((kv_local, rows, group_size), jnp.float32),
        ],
        compiler_params=pltpu.CompilerParams(
            dimension_semantics=("arbitrary", "arbitrary"), vmem_limit_bytes=56 * 1024 * 1024
        ),
        cost_estimate=cost,
    )(keep, live, query_rows, *([cache_keys.T] * TPB), *([cache_values] * TPB), new_keys.T, new_values, query_place, key_place)


def dense_fold(q_ref, h, keys_t, values_ext, mask, m_scr, acc_ref):
    coef = DH ** (-0.5) * LOG2E
    cols = pl.ds(pl.multiple_of(h * DH, DH), DH)
    s = jnp.dot(q_ref[:, cols], keys_t, preferred_element_type=jnp.float32) + mask
    m_prev = m_scr[h]
    m_new = jnp.maximum(m_prev, s.max(axis=1, keepdims=True))
    alpha = jnp.exp2((m_prev - m_new) * coef)
    p = jnp.exp2(s * coef - m_new[:, :1] * coef)
    m_scr[h] = m_new
    acc_ref[h] = acc_ref[h] * alpha[:, :1] + jnp.dot(
        p.astype(jnp.bfloat16), values_ext, preferred_element_type=jnp.float32
    )


def attn_push_kernel(n, group_size, per_dest, count, *refs):
    q_ref, kt_ref, v_ref, bias_ref, nkt_ref, nv_ref, qp_ref, kp_ref = refs[:8]
    srcs = refs[8 : 8 + count]
    sum_out, m_out, l_out = refs[8 + count : 11 + count]
    dsts = refs[11 + count : 11 + 2 * count]
    m_scr, acc_ref, send_sem, recv_sem, local_sem = refs[11 + 2 * count :]
    t = pl.program_id(0)
    last = pl.num_programs(0) - 1
    me = lax.axis_index("ctx")

    def remote_copies():
        out = []
        for a in range(count):
            for k in range(1, n):
                peer = lax.rem(me + k, n)
                out.append(
                    pltpu.make_async_remote_copy(
                        src_ref=srcs[a].at[peer] if per_dest[a] else srcs[a],
                        dst_ref=dsts[a].at[me],
                        send_sem=send_sem.at[a, k],
                        recv_sem=recv_sem.at[a, k],
                        device_id={"ctx": peer},
                        device_id_type=MESH,
                    )
                )
        return out

    def local_copies():
        return [
            pltpu.make_async_copy(
                srcs[a].at[me] if per_dest[a] else srcs[a], dsts[a].at[me], local_sem.at[a]
            )
            for a in range(count)
        ]

    def with_ones(values):
        return jnp.concatenate([values, jnp.ones(values.shape, values.dtype)], axis=1)

    @pl.when(t == 0)
    def _():
        barrier = pltpu.get_barrier_semaphore()
        for k in range(1, n):
            peer = lax.rem(me + k, n)
            pl.semaphore_signal(barrier, inc=1, device_id={"ctx": peer}, device_id_type=MESH)
        pl.semaphore_wait(barrier, n - 1)
        for c in remote_copies():
            c.start()
        for c in local_copies():
            c.start()
        m_scr[...] = jnp.full(m_scr.shape, NEG_INF, jnp.float32)
        acc_ref[...] = jnp.zeros(acc_ref.shape, jnp.float32)

    keys_t = kt_ref[...]
    values_ext = with_ones(v_ref[...])
    mask = bias_ref[...]

    def head_body(h, carry):
        dense_fold(q_ref, h, keys_t, values_ext, mask, m_scr, acc_ref)
        return carry

    lax.fori_loop(0, group_size, head_body, 0)

    @pl.when(t == last)
    def _():
        causal = jnp.where(qp_ref[...] >= kp_ref[...], 0.0, NEG_INF).astype(jnp.float32)
        nkt = nkt_ref[...]
        nv_ext = with_ones(nv_ref[...])

        def new_body(h, carry):
            dense_fold(q_ref, h, nkt, nv_ext, causal, m_scr, acc_ref)
            return carry

        lax.fori_loop(0, group_size, new_body, 0)
        for h in range(group_size):
            acc = acc_ref[h]
            sum_out[:, h * DH : (h + 1) * DH] = acc[:, :DH].astype(sum_out.dtype)
            m_out[:, h : h + 1] = m_scr[h][:, :1]
            l_out[:, h : h + 1] = acc[:, DH : DH + 1]
        for c in local_copies():
            c.wait()
        for c in remote_copies():
            c.wait()


def attention_with_push(query_rows, keys_t, values, bias, new_keys_t, new_values, query_place, key_place, sends, n, per_dest, collective_id):
    rows, width = query_rows.shape
    group_size = width // DH
    total_keys = keys_t.shape[1]
    step_keys = TPB * TILE
    steps = total_keys // step_keys
    q_new = new_values.shape[0]
    any_spec = pl.BlockSpec(memory_space=pl.ANY)
    count = len(sends)
    recv_shapes = [
        jax.ShapeDtypeStruct((n,) + tuple(x.shape[1:] if d else x.shape), x.dtype)
        for x, d in zip(sends, per_dest)
    ]
    flops = 4 * rows * group_size * (total_keys + q_new) * DH
    cost = pl.CostEstimate(
        flops=flops,
        transcendentals=rows * group_size * (total_keys + q_new),
        bytes_accessed=rows * width * 4 + 2 * total_keys * DH * 2,
    )
    return pl.pallas_call(
        functools.partial(attn_push_kernel, n, group_size, per_dest, count),
        grid=(steps,),
        in_specs=[
            pl.BlockSpec((rows, width), lambda t: (0, 0)),
            pl.BlockSpec((DH, step_keys), lambda t: (0, t)),
            pl.BlockSpec((step_keys, DH), lambda t: (t, 0)),
            pl.BlockSpec((1, step_keys), lambda t: (0, t)),
            pl.BlockSpec((DH, q_new), lambda t: (0, 0)),
            pl.BlockSpec((q_new, DH), lambda t: (0, 0)),
            pl.BlockSpec((rows, 1), lambda t: (0, 0)),
            pl.BlockSpec((1, q_new), lambda t: (0, 0)),
        ]
        + [any_spec] * count,
        out_specs=[
            pl.BlockSpec((rows, width), lambda t: (0, 0)),
            pl.BlockSpec((rows, group_size), lambda t: (0, 0)),
            pl.BlockSpec((rows, group_size), lambda t: (0, 0)),
        ]
        + [any_spec] * count,
        out_shape=[
            jax.ShapeDtypeStruct((rows, width), jnp.bfloat16),
            jax.ShapeDtypeStruct((rows, group_size), jnp.float32),
            jax.ShapeDtypeStruct((rows, group_size), jnp.float32),
        ]
        + recv_shapes,
        scratch_shapes=[
            pltpu.VMEM((group_size, rows, DH), jnp.float32),
            pltpu.VMEM((group_size, rows, 2 * DH), jnp.float32),
            pltpu.SemaphoreType.DMA((count, n)),
            pltpu.SemaphoreType.DMA((count, n)),
            pltpu.SemaphoreType.DMA((count,)),
        ],
        compiler_params=pltpu.CompilerParams(
            collective_id=collective_id, has_side_effects=True, vmem_limit_bytes=56 * 1024 * 1024
        ),
        cost_estimate=cost,
    )(query_rows, keys_t, values, bias, new_keys_t, new_values, query_place, key_place, *sends)


def combine_kernel(heads, part_ref, fac_ref, den_ref, out_ref):
    senders = part_ref.shape[0]
    width = part_ref.shape[3]
    half = width // DH

    def sender_body(i, acc):
        fac = fac_ref[i]
        out = []
        for h in range(heads):
            j, c = divmod(h, half)
            blk = part_ref[i, j][:, c * DH : (c + 1) * DH].astype(jnp.float32)
            out.append(acc[h] + blk * fac[:, h : h + 1])
        return tuple(out)

    rows = out_ref.shape[0]
    start = tuple(jnp.zeros((rows, DH), jnp.float32) for _ in range(heads))
    acc = lax.fori_loop(0, senders, sender_body, start)
    den = den_ref[...]
    for h in range(heads):
        out_ref[:, h * DH : (h + 1) * DH] = (acc[h] / den[:, h : h + 1]).astype(out_ref.dtype)


def combine(part_sum, factor, denominator):
    senders, groups, rows, width = part_sum.shape
    heads = groups * width // DH
    vmem = pl.BlockSpec(memory_space=pltpu.VMEM)
    return pl.pallas_call(
        functools.partial(combine_kernel, heads),
        out_shape=jax.ShapeDtypeStruct((rows, heads * DH), jnp.bfloat16),
        in_specs=[vmem, vmem, vmem],
        out_specs=vmem,
        compiler_params=pltpu.CompilerParams(vmem_limit_bytes=32 * 1024 * 1024),
    )(part_sum, factor, denominator)


def body(
    queries,
    new_keys,
    new_values,
    cache_keys,
    cache_values,
    keep_tiles,
    tile_count,
    owner_slot,
    out_weight,
):
    q_dev = queries.shape[0]
    kv_local = new_keys.shape[1] // DH
    q_local = queries.shape[1] // DH
    group_size = q_local // kv_local
    ctx_count = lax.axis_size("ctx")
    tp_count = lax.axis_size("tp")
    total_rows = q_dev * ctx_count
    my_index = lax.axis_index("ctx")
    key_place = owner_slot[my_index] * q_dev + jnp.arange(q_dev, dtype=jnp.int32)
    pieces = 4
    piece_heads = q_local // pieces
    width = piece_heads * DH
    (q_blocks,) = push((queries[:, :width],), "ctx", ctx_count, False, 0)
    query_place = (
        owner_slot[:, None] * q_dev + jnp.arange(q_dev, dtype=jnp.int32)[None, :]
    ).reshape(total_rows, 1)
    key_place = key_place.reshape(1, q_dev)
    slots = keep_tiles.shape[2]
    slot_ids = jnp.arange(slots * TILE, dtype=jnp.int32) // TILE

    def dense_head(g):
        cols = slice(g * DH, (g + 1) * DH)
        tiles_k = cache_keys[:, cols].reshape(-1, TILE, DH)
        tiles_v = cache_values[:, cols].reshape(-1, TILE, DH)
        kept_k = jnp.take(tiles_k, keep_tiles[0, g], axis=0).reshape(slots * TILE, DH)
        kept_v = jnp.take(tiles_v, keep_tiles[0, g], axis=0).reshape(slots * TILE, DH)
        bias = jnp.where(slot_ids < tile_count[0, g], 0.0, NEG_INF).astype(jnp.float32)
        return kept_k.T, kept_v, bias.reshape(1, slots * TILE), new_keys[:, cols].T, new_values[:, cols]

    head_data = [dense_head(g) for g in range(kv_local)]
    coef = DH ** (-0.5) * LOG2E

    def combine_piece(parts):
        part_sum, part_max, part_total = parts
        top_max = jnp.max(part_max, axis=0)
        factor = jnp.exp2((part_max - top_max[None]) * coef)
        denominator = jnp.sum(part_total * factor, axis=0)
        return combine(part_sum[:, None], factor, denominator)

    attn_pieces = []
    attn_blocks = []
    previous = None
    for i in range(pieces):
        sends = []
        flags = []
        if i + 1 < pieces:
            sends.append(queries[:, (i + 1) * width : (i + 2) * width])
            flags.append(False)
        if previous is not None:
            sends.extend(previous)
            flags.extend([True, True, True])
        if i >= 2:
            sends.append(attn_pieces[i - 2])
            flags.append(False)
        outs = attention_with_push(
            q_blocks.reshape(total_rows, width),
            *head_data[i * kv_local // pieces],
            query_place,
            key_place,
            tuple(sends),
            ctx_count,
            tuple(flags),
            4 + i,
        )
        sums_i, maxima_i, totals_i = outs[:3]
        rest = list(outs[3:])
        if i + 1 < pieces:
            q_blocks = rest.pop(0)
        if previous is not None:
            got = (rest.pop(0), rest.pop(0), rest.pop(0))
            attn_pieces.append(combine_piece(got))
        if i >= 2:
            attn_blocks.append(rest.pop(0))
        previous = (
            sums_i.reshape(ctx_count, q_dev, width),
            maxima_i.reshape(ctx_count, q_dev, piece_heads),
            totals_i.reshape(ctx_count, q_dev, piece_heads),
        )
    attn_pieces.append(combine_piece(push(previous, "ctx", ctx_count, True, 1)))
    attn_blocks.extend(push(tuple(attn_pieces[pieces - 2 :]), "ctx", ctx_count, False, 2))
    projected = None
    for j, blocks in enumerate(attn_blocks):
        term = jnp.dot(
            blocks.reshape(total_rows, width),
            out_weight[j * width : (j + 1) * width],
            preferred_element_type=jnp.float32,
        )
        projected = term if projected is None else projected + term
    out_rows = total_rows // tp_count
    (proj_parts,) = push(
        (projected.reshape(tp_count, out_rows, projected.shape[1]),), "tp", tp_count, True, 3
    )
    return jnp.sum(proj_parts, axis=0)


def solution(mesh):
    return jax.shard_map(
        body,
        mesh=mesh,
        in_specs=(
            P("ctx", "tp"),
            P("ctx", "tp"),
            P("ctx", "tp"),
            P("ctx", "tp"),
            P("ctx", "tp"),
            P("ctx", "tp", None),
            P("ctx", "tp"),
            P(),
            P("tp", "ctx"),
        ),
        out_specs=P("tp", "ctx"),
        check_vma=False,
    )
```

```python
import functools

import jax
import jax.numpy as jnp
from jax import lax
from jax.experimental import pallas as pl
from jax.experimental.pallas import tpu as pltpu
from jax.sharding import PartitionSpec as P

DH = 128
TILE = 128
TB = 4
MESH = pl.DeviceIdType.MESH

NEG_INF = -jnp.inf


def push_kernel(axis, n, per_dest, count, *refs):
    x_refs = refs[:count]
    y_refs = refs[count : 2 * count]
    send_sem, recv_sem, local_sem = refs[2 * count :]
    me = lax.axis_index(axis)
    barrier = pltpu.get_barrier_semaphore()
    for k in range(1, n):
        peer = lax.rem(me + k, n)
        pl.semaphore_signal(barrier, inc=1, device_id={axis: peer}, device_id_type=MESH)
    pl.semaphore_wait(barrier, n - 1)
    copies = []
    for a in range(count):
        for k in range(1, n):
            peer = lax.rem(me + k, n)
            src = x_refs[a].at[peer] if per_dest else x_refs[a]
            copy = pltpu.make_async_remote_copy(
                src_ref=src,
                dst_ref=y_refs[a].at[me],
                send_sem=send_sem.at[a, k],
                recv_sem=recv_sem.at[a, k],
                device_id={axis: peer},
                device_id_type=MESH,
            )
            copy.start()
            copies.append(copy)
    locals_ = []
    for a in range(count):
        src = x_refs[a].at[me] if per_dest else x_refs[a]
        local = pltpu.make_async_copy(src, y_refs[a].at[me], local_sem.at[a])
        local.start()
        locals_.append(local)
    for local in locals_:
        local.wait()
    for copy in copies:
        copy.wait()


def push(xs, axis, n, per_dest, collective_id):
    count = len(xs)
    out_shape = []
    for x in xs:
        block = x.shape[1:] if per_dest else x.shape
        out_shape.append(jax.ShapeDtypeStruct((n,) + tuple(block), x.dtype))
    any_spec = pl.BlockSpec(memory_space=pl.ANY)
    return pl.pallas_call(
        functools.partial(push_kernel, axis, n, per_dest, count),
        out_shape=tuple(out_shape),
        in_specs=[any_spec] * count,
        out_specs=tuple([any_spec] * count),
        scratch_shapes=[
            pltpu.SemaphoreType.DMA((count, n)),
            pltpu.SemaphoreType.DMA((count, n)),
            pltpu.SemaphoreType.DMA((count,)),
        ],
        compiler_params=pltpu.CompilerParams(collective_id=collective_id, has_side_effects=True),
    )(*xs)


TPB = 8
LOG2E = 1.4426950408889634
SPLITS = (2, 3, 3, 3, 3, 2)


def dot_nt(a, b):
    return jnp.dot(a, b, preferred_element_type=jnp.float32)


def attn_kernel(tpb, group_size, kt_ref, cnt_ref, q_ref, *refs):
    k_refs = refs[:tpb]
    v_refs = refs[tpb : 2 * tpb]
    nk_ref, nv_ref, qp_ref, kp_ref = refs[2 * tpb : 2 * tpb + 4]
    sum_out, m_out, l_out = refs[2 * tpb + 4 : 2 * tpb + 7]
    m_scr, acc_ref = refs[2 * tpb + 7 :]
    g = pl.program_id(0)
    t = pl.program_id(1)
    last = pl.num_programs(1) - 1
    live = cnt_ref[g]
    coef = DH ** (-0.5) * LOG2E

    @pl.when(t == 0)
    def _():
        m_scr[...] = jnp.full(m_scr.shape, NEG_INF, jnp.float32)
        acc_ref[...] = jnp.zeros(acc_ref.shape, jnp.float32)

    def fold(h, keys, values_ext, mask):
        cols = pl.ds(pl.multiple_of(h * DH, DH), DH)
        s = dot_nt(q_ref[:, cols], keys)
        if mask is not None:
            s = s + mask
        m_prev = m_scr[h]
        m_new = jnp.maximum(m_prev, s.max(axis=1, keepdims=True))
        alpha = jnp.exp2((m_prev - m_new) * coef)
        p = jnp.exp2(s * coef - m_new[:, :1] * coef)
        m_scr[h] = m_new
        acc_ref[h] = acc_ref[h] * alpha[:, :1] + jnp.dot(
            p.astype(jnp.bfloat16), values_ext, preferred_element_type=jnp.float32
        )

    def with_ones(values):
        return jnp.concatenate([values, jnp.ones(values.shape, values.dtype)], axis=1)

    def tiles_step(masked):
        keys = jnp.concatenate([k[...] for k in k_refs], axis=1)
        values_ext = with_ones(jnp.concatenate([v[...] for v in v_refs], axis=0))
        mask = None
        if masked:
            slot = t * tpb + lax.broadcasted_iota(jnp.int32, (1, tpb * TILE), 1) // TILE
            mask = jnp.where(slot < live, 0.0, NEG_INF).astype(jnp.float32)

        def head_body(h, carry):
            fold(h, keys, values_ext, mask)
            return carry

        lax.fori_loop(0, group_size, head_body, 0)

    @pl.when((t + 1) * tpb <= live)
    def _():
        tiles_step(False)

    @pl.when(jnp.logical_and(t * tpb < live, (t + 1) * tpb > live))
    def _():
        tiles_step(True)

    @pl.when(t == last)
    def _():
        causal = jnp.where(qp_ref[...] >= kp_ref[...], 0.0, NEG_INF).astype(jnp.float32)
        nk = nk_ref[...]
        nv_ext = with_ones(nv_ref[...])

        def head_body(h, carry):
            fold(h, nk, nv_ext, causal)
            return carry

        lax.fori_loop(0, group_size, head_body, 0)
        for h in range(group_size):
            acc = acc_ref[h]
            sum_out[:, h * DH : (h + 1) * DH] = acc[:, :DH].astype(sum_out.dtype)
            m_out[:, h : h + 1] = m_scr[h][:, :1]
            l_out[:, h : h + 1] = acc[:, DH : DH + 1]


def local_attention(query_rows, cache_keys, cache_values, new_keys, new_values, keep, live, query_place, key_place):
    rows, width = query_rows.shape
    kv_local = new_keys.shape[1] // DH
    group_size = width // DH // kv_local
    slots = keep.shape[1]
    steps = slots // TPB
    q_new = new_keys.shape[0]

    def tile_map(j):
        def index_map(g, t, kt_ref, cnt_ref):
            return (kt_ref[g, jnp.minimum(t * TPB + j, cnt_ref[g] - 1)], g)

        return index_map

    tile_spec = [pl.BlockSpec((TILE, DH), tile_map(j)) for j in range(TPB)]

    def tile_map_t(j):
        def index_map(g, t, kt_ref, cnt_ref):
            return (g, kt_ref[g, jnp.minimum(t * TPB + j, cnt_ref[g] - 1)])

        return index_map

    tile_spec_t = [pl.BlockSpec((DH, TILE), tile_map_t(j)) for j in range(TPB)]
    grid_spec = pltpu.PrefetchScalarGridSpec(
        num_scalar_prefetch=2,
        grid=(kv_local, steps),
        in_specs=[pl.BlockSpec((rows, group_size * DH), lambda g, t, kt, cn: (0, g))]
        + tile_spec_t
        + tile_spec
        + [
            pl.BlockSpec((DH, q_new), lambda g, t, kt, cn: (g, 0)),
            pl.BlockSpec((q_new, DH), lambda g, t, kt, cn: (0, g)),
            pl.BlockSpec((rows, 1), lambda g, t, kt, cn: (0, 0)),
            pl.BlockSpec((1, q_new), lambda g, t, kt, cn: (0, 0)),
        ],
        out_specs=[
            pl.BlockSpec((rows, group_size * DH), lambda g, t, kt, cn: (0, g)),
            pl.BlockSpec((None, rows, group_size), lambda g, t, kt, cn: (g, 0, 0)),
            pl.BlockSpec((None, rows, group_size), lambda g, t, kt, cn: (g, 0, 0)),
        ],
        scratch_shapes=[
            pltpu.VMEM((group_size, rows, DH), jnp.float32),
            pltpu.VMEM((group_size, rows, 2 * DH), jnp.float32),
        ],
    )
    keys_total = slots * TILE + q_new
    flops = 4 * rows * kv_local * group_size * keys_total * DH
    cost = pl.CostEstimate(
        flops=flops,
        transcendentals=rows * kv_local * group_size * keys_total,
        bytes_accessed=rows * width * 2 + rows * width * 4 + 2 * kv_local * slots * TILE * DH * 2,
    )
    return pl.pallas_call(
        functools.partial(attn_kernel, TPB, group_size),
        grid_spec=grid_spec,
        out_shape=[
            jax.ShapeDtypeStruct((rows, width), jnp.bfloat16),
            jax.ShapeDtypeStruct((kv_local, rows, group_size), jnp.float32),
            jax.ShapeDtypeStruct((kv_local, rows, group_size), jnp.float32),
        ],
        compiler_params=pltpu.CompilerParams(
            dimension_semantics=("arbitrary", "arbitrary"), vmem_limit_bytes=56 * 1024 * 1024
        ),
        cost_estimate=cost,
    )(keep, live, query_rows, *([cache_keys.T] * TPB), *([cache_values] * TPB), new_keys.T, new_values, query_place, key_place)


def dense_fold(q_ref, h, keys_t, values_ext, mask, m_scr, acc_ref):
    coef = DH ** (-0.5) * LOG2E
    cols = pl.ds(pl.multiple_of(h * DH, DH), DH)
    s = jnp.dot(q_ref[:, cols], keys_t, preferred_element_type=jnp.float32) + mask
    m_prev = m_scr[h]
    m_new = jnp.maximum(m_prev, s.max(axis=1, keepdims=True))
    alpha = jnp.exp2((m_prev - m_new) * coef)
    p = jnp.exp2(s * coef - m_new[:, :1] * coef)
    m_scr[h] = m_new
    acc_ref[h] = acc_ref[h] * alpha[:, :1] + jnp.dot(
        p.astype(jnp.bfloat16), values_ext, preferred_element_type=jnp.float32
    )


def attn_push_kernel(n, group_size, per_dest, count, *refs):
    q_ref, kt_ref, v_ref, bias_ref, nkt_ref, nv_ref, qp_ref, kp_ref = refs[:8]
    srcs = refs[8 : 8 + count]
    sum_out, m_out, l_out = refs[8 + count : 11 + count]
    dsts = refs[11 + count : 11 + 2 * count]
    m_scr, acc_ref, send_sem, recv_sem, local_sem = refs[11 + 2 * count :]
    t = pl.program_id(0)
    last = pl.num_programs(0) - 1
    me = lax.axis_index("ctx")

    def remote_copies():
        out = []
        for a in range(count):
            for k in range(1, n):
                peer = lax.rem(me + k, n)
                out.append(
                    pltpu.make_async_remote_copy(
                        src_ref=srcs[a].at[peer] if per_dest[a] else srcs[a],
                        dst_ref=dsts[a].at[me],
                        send_sem=send_sem.at[a, k],
                        recv_sem=recv_sem.at[a, k],
                        device_id={"ctx": peer},
                        device_id_type=MESH,
                    )
                )
        return out

    def local_copies():
        return [
            pltpu.make_async_copy(
                srcs[a].at[me] if per_dest[a] else srcs[a], dsts[a].at[me], local_sem.at[a]
            )
            for a in range(count)
        ]

    def with_ones(values):
        return jnp.concatenate([values, jnp.ones(values.shape, values.dtype)], axis=1)

    @pl.when(t == 0)
    def _():
        barrier = pltpu.get_barrier_semaphore()
        for k in range(1, n):
            peer = lax.rem(me + k, n)
            pl.semaphore_signal(barrier, inc=1, device_id={"ctx": peer}, device_id_type=MESH)
        pl.semaphore_wait(barrier, n - 1)
        for c in remote_copies():
            c.start()
        for c in local_copies():
            c.start()
        m_scr[...] = jnp.full(m_scr.shape, NEG_INF, jnp.float32)
        acc_ref[...] = jnp.zeros(acc_ref.shape, jnp.float32)

    keys_t = kt_ref[...]
    values_ext = with_ones(v_ref[...])
    mask = bias_ref[...]

    def head_body(h, carry):
        dense_fold(q_ref, h, keys_t, values_ext, mask, m_scr, acc_ref)
        return carry

    lax.fori_loop(0, group_size, head_body, 0)

    @pl.when(t == last)
    def _():
        causal = jnp.where(qp_ref[...] >= kp_ref[...], 0.0, NEG_INF).astype(jnp.float32)
        nkt = nkt_ref[...]
        nv_ext = with_ones(nv_ref[...])

        def new_body(h, carry):
            dense_fold(q_ref, h, nkt, nv_ext, causal, m_scr, acc_ref)
            return carry

        lax.fori_loop(0, group_size, new_body, 0)
        for h in range(group_size):
            acc = acc_ref[h]
            sum_out[:, h * DH : (h + 1) * DH] = acc[:, :DH].astype(sum_out.dtype)
            m_out[:, h : h + 1] = m_scr[h][:, :1]
            l_out[:, h : h + 1] = acc[:, DH : DH + 1]
        for c in local_copies():
            c.wait()
        for c in remote_copies():
            c.wait()


def attention_with_push(query_rows, keys_t, values, bias, new_keys_t, new_values, query_place, key_place, sends, n, per_dest, collective_id):
    rows, width = query_rows.shape
    group_size = width // DH
    total_keys = keys_t.shape[1]
    step_keys = TPB * TILE
    steps = total_keys // step_keys
    q_new = new_values.shape[0]
    any_spec = pl.BlockSpec(memory_space=pl.ANY)
    count = len(sends)
    recv_shapes = [
        jax.ShapeDtypeStruct((n,) + tuple(x.shape[1:] if d else x.shape), x.dtype)
        for x, d in zip(sends, per_dest)
    ]
    flops = 4 * rows * group_size * (total_keys + q_new) * DH
    cost = pl.CostEstimate(
        flops=flops,
        transcendentals=rows * group_size * (total_keys + q_new),
        bytes_accessed=rows * width * 4 + 2 * total_keys * DH * 2,
    )
    return pl.pallas_call(
        functools.partial(attn_push_kernel, n, group_size, per_dest, count),
        grid=(steps,),
        in_specs=[
            pl.BlockSpec((rows, width), lambda t: (0, 0)),
            pl.BlockSpec((DH, step_keys), lambda t: (0, t)),
            pl.BlockSpec((step_keys, DH), lambda t: (t, 0)),
            pl.BlockSpec((1, step_keys), lambda t: (0, t)),
            pl.BlockSpec((DH, q_new), lambda t: (0, 0)),
            pl.BlockSpec((q_new, DH), lambda t: (0, 0)),
            pl.BlockSpec((rows, 1), lambda t: (0, 0)),
            pl.BlockSpec((1, q_new), lambda t: (0, 0)),
        ]
        + [any_spec] * count,
        out_specs=[
            pl.BlockSpec((rows, width), lambda t: (0, 0)),
            pl.BlockSpec((rows, group_size), lambda t: (0, 0)),
            pl.BlockSpec((rows, group_size), lambda t: (0, 0)),
        ]
        + [any_spec] * count,
        out_shape=[
            jax.ShapeDtypeStruct((rows, width), jnp.bfloat16),
            jax.ShapeDtypeStruct((rows, group_size), jnp.float32),
            jax.ShapeDtypeStruct((rows, group_size), jnp.float32),
        ]
        + recv_shapes,
        scratch_shapes=[
            pltpu.VMEM((group_size, rows, DH), jnp.float32),
            pltpu.VMEM((group_size, rows, 2 * DH), jnp.float32),
            pltpu.SemaphoreType.DMA((count, n)),
            pltpu.SemaphoreType.DMA((count, n)),
            pltpu.SemaphoreType.DMA((count,)),
        ],
        compiler_params=pltpu.CompilerParams(
            collective_id=collective_id, has_side_effects=True, vmem_limit_bytes=56 * 1024 * 1024
        ),
        cost_estimate=cost,
    )(query_rows, keys_t, values, bias, new_keys_t, new_values, query_place, key_place, *sends)


def combine_kernel(heads, part_ref, fac_ref, den_ref, out_ref):
    senders = part_ref.shape[0]
    width = part_ref.shape[3]
    half = width // DH

    def sender_body(i, acc):
        fac = fac_ref[i]
        out = []
        for h in range(heads):
            j, c = divmod(h, half)
            blk = part_ref[i, j][:, c * DH : (c + 1) * DH].astype(jnp.float32)
            out.append(acc[h] + blk * fac[:, h : h + 1])
        return tuple(out)

    rows = out_ref.shape[0]
    start = tuple(jnp.zeros((rows, DH), jnp.float32) for _ in range(heads))
    acc = lax.fori_loop(0, senders, sender_body, start)
    den = den_ref[...]
    for h in range(heads):
        out_ref[:, h * DH : (h + 1) * DH] = (acc[h] / den[:, h : h + 1]).astype(out_ref.dtype)


def combine(part_sum, factor, denominator):
    senders, groups, rows, width = part_sum.shape
    heads = groups * width // DH
    vmem = pl.BlockSpec(memory_space=pltpu.VMEM)
    return pl.pallas_call(
        functools.partial(combine_kernel, heads),
        out_shape=jax.ShapeDtypeStruct((rows, heads * DH), jnp.bfloat16),
        in_specs=[vmem, vmem, vmem],
        out_specs=vmem,
        compiler_params=pltpu.CompilerParams(vmem_limit_bytes=32 * 1024 * 1024),
    )(part_sum, factor, denominator)


def body(
    queries,
    new_keys,
    new_values,
    cache_keys,
    cache_values,
    keep_tiles,
    tile_count,
    owner_slot,
    out_weight,
):
    q_dev = queries.shape[0]
    kv_local = new_keys.shape[1] // DH
    q_local = queries.shape[1] // DH
    group_size = q_local // kv_local
    ctx_count = lax.axis_size("ctx")
    tp_count = lax.axis_size("tp")
    total_rows = q_dev * ctx_count
    my_index = lax.axis_index("ctx")
    key_place = owner_slot[my_index] * q_dev + jnp.arange(q_dev, dtype=jnp.int32)
    splits = SPLITS
    pieces = len(splits)
    offsets = [sum(splits[:i]) * DH for i in range(pieces + 1)]
    (q_blocks,) = push((queries[:, : offsets[1]],), "ctx", ctx_count, False, 0)
    query_place = (
        owner_slot[:, None] * q_dev + jnp.arange(q_dev, dtype=jnp.int32)[None, :]
    ).reshape(total_rows, 1)
    key_place = key_place.reshape(1, q_dev)
    slots = keep_tiles.shape[2]
    slot_ids = jnp.arange(slots * TILE, dtype=jnp.int32) // TILE

    def dense_head(g):
        cols = slice(g * DH, (g + 1) * DH)
        tiles_k = cache_keys[:, cols].reshape(-1, TILE, DH)
        tiles_v = cache_values[:, cols].reshape(-1, TILE, DH)
        kept_k = jnp.take(tiles_k, keep_tiles[0, g], axis=0).reshape(slots * TILE, DH)
        kept_v = jnp.take(tiles_v, keep_tiles[0, g], axis=0).reshape(slots * TILE, DH)
        bias = jnp.where(slot_ids < tile_count[0, g], 0.0, NEG_INF).astype(jnp.float32)
        return kept_k.T, kept_v, bias.reshape(1, slots * TILE), new_keys[:, cols].T, new_values[:, cols]

    head_data = [dense_head(g) for g in range(kv_local)]
    coef = DH ** (-0.5) * LOG2E

    def combine_piece(parts):
        part_sum, part_max, part_total = parts
        top_max = jnp.max(part_max, axis=0)
        factor = jnp.exp2((part_max - top_max[None]) * coef)
        denominator = jnp.sum(part_total * factor, axis=0)
        return combine(part_sum[:, None], factor, denominator)

    attn_pieces = []
    attn_blocks = []
    previous = None
    for i in range(pieces):
        sends = []
        flags = []
        if i + 1 < pieces:
            sends.append(queries[:, offsets[i + 1] : offsets[i + 2]])
            flags.append(False)
        if previous is not None:
            sends.extend(previous)
            flags.extend([True, True, True])
        if i >= 2:
            sends.append(attn_pieces[i - 2])
            flags.append(False)
        width = offsets[i + 1] - offsets[i]
        outs = attention_with_push(
            q_blocks.reshape(total_rows, width),
            *head_data[offsets[i] // DH // group_size],
            query_place,
            key_place,
            tuple(sends),
            ctx_count,
            tuple(flags),
            4 + i,
        )
        sums_i, maxima_i, totals_i = outs[:3]
        rest = list(outs[3:])
        if i + 1 < pieces:
            q_blocks = rest.pop(0)
        if previous is not None:
            got = (rest.pop(0), rest.pop(0), rest.pop(0))
            attn_pieces.append(combine_piece(got))
        if i >= 2:
            attn_blocks.append(rest.pop(0))
        previous = (
            sums_i.reshape(ctx_count, q_dev, width),
            maxima_i.reshape(ctx_count, q_dev, splits[i]),
            totals_i.reshape(ctx_count, q_dev, splits[i]),
        )
    attn_pieces.append(combine_piece(push(previous, "ctx", ctx_count, True, 1)))
    attn_blocks.extend(push(tuple(attn_pieces[pieces - 2 :]), "ctx", ctx_count, False, 2))
    projected = None
    for j, blocks in enumerate(attn_blocks):
        term = jnp.dot(
            blocks.reshape(total_rows, offsets[j + 1] - offsets[j]),
            out_weight[offsets[j] : offsets[j + 1]],
            preferred_element_type=jnp.float32,
        )
        projected = term if projected is None else projected + term
    out_rows = total_rows // tp_count
    (proj_parts,) = push(
        (projected.reshape(tp_count, out_rows, projected.shape[1]),), "tp", tp_count, True, 3
    )
    return jnp.sum(proj_parts, axis=0)


def solution(mesh):
    return jax.shard_map(
        body,
        mesh=mesh,
        in_specs=(
            P("ctx", "tp"),
            P("ctx", "tp"),
            P("ctx", "tp"),
            P("ctx", "tp"),
            P("ctx", "tp"),
            P("ctx", "tp", None),
            P("ctx", "tp"),
            P(),
            P("tp", "ctx"),
        ),
        out_specs=P("tp", "ctx"),
        check_vma=False,
    )
```

```python
import functools

import jax
import jax.numpy as jnp
from jax import lax
from jax.experimental import pallas as pl
from jax.experimental.pallas import tpu as pltpu
from jax.sharding import PartitionSpec as P

DH = 128
TILE = 128
TB = 4
MESH = pl.DeviceIdType.MESH

NEG_INF = -jnp.inf


def push_kernel(axis, n, per_dest, count, *refs):
    x_refs = refs[:count]
    y_refs = refs[count : 2 * count]
    send_sem, recv_sem, local_sem = refs[2 * count :]
    me = lax.axis_index(axis)
    barrier = pltpu.get_barrier_semaphore()
    for k in range(1, n):
        peer = lax.rem(me + k, n)
        pl.semaphore_signal(barrier, inc=1, device_id={axis: peer}, device_id_type=MESH)
    pl.semaphore_wait(barrier, n - 1)
    copies = []
    for a in range(count):
        for k in range(1, n):
            peer = lax.rem(me + k, n)
            src = x_refs[a].at[peer] if per_dest[a] else x_refs[a]
            copy = pltpu.make_async_remote_copy(
                src_ref=src,
                dst_ref=y_refs[a].at[me],
                send_sem=send_sem.at[a, k],
                recv_sem=recv_sem.at[a, k],
                device_id={axis: peer},
                device_id_type=MESH,
            )
            copy.start()
            copies.append(copy)
    locals_ = []
    for a in range(count):
        src = x_refs[a].at[me] if per_dest[a] else x_refs[a]
        local = pltpu.make_async_copy(src, y_refs[a].at[me], local_sem.at[a])
        local.start()
        locals_.append(local)
    for local in locals_:
        local.wait()
    for copy in copies:
        copy.wait()


def push(xs, axis, n, per_dest, collective_id):
    count = len(xs)
    if isinstance(per_dest, bool):
        per_dest = (per_dest,) * count
    out_shape = []
    for x, d in zip(xs, per_dest):
        block = x.shape[1:] if d else x.shape
        out_shape.append(jax.ShapeDtypeStruct((n,) + tuple(block), x.dtype))
    any_spec = pl.BlockSpec(memory_space=pl.ANY)
    return pl.pallas_call(
        functools.partial(push_kernel, axis, n, per_dest, count),
        out_shape=tuple(out_shape),
        in_specs=[any_spec] * count,
        out_specs=tuple([any_spec] * count),
        scratch_shapes=[
            pltpu.SemaphoreType.DMA((count, n)),
            pltpu.SemaphoreType.DMA((count, n)),
            pltpu.SemaphoreType.DMA((count,)),
        ],
        compiler_params=pltpu.CompilerParams(collective_id=collective_id, has_side_effects=True),
    )(*xs)


TPB = 8
LOG2E = 1.4426950408889634


def dot_nt(a, b):
    return jnp.dot(a, b, preferred_element_type=jnp.float32)


def attn_kernel(tpb, group_size, kt_ref, cnt_ref, q_ref, *refs):
    k_refs = refs[:tpb]
    v_refs = refs[tpb : 2 * tpb]
    nk_ref, nv_ref, qp_ref, kp_ref = refs[2 * tpb : 2 * tpb + 4]
    sum_out, m_out, l_out = refs[2 * tpb + 4 : 2 * tpb + 7]
    m_scr, acc_ref = refs[2 * tpb + 7 :]
    g = pl.program_id(0)
    t = pl.program_id(1)
    last = pl.num_programs(1) - 1
    live = cnt_ref[g]
    coef = DH ** (-0.5) * LOG2E

    @pl.when(t == 0)
    def _():
        m_scr[...] = jnp.full(m_scr.shape, NEG_INF, jnp.float32)
        acc_ref[...] = jnp.zeros(acc_ref.shape, jnp.float32)

    def fold(h, keys, values_ext, mask):
        cols = pl.ds(pl.multiple_of(h * DH, DH), DH)
        s = dot_nt(q_ref[:, cols], keys)
        if mask is not None:
            s = s + mask
        m_prev = m_scr[h]
        m_new = jnp.maximum(m_prev, s.max(axis=1, keepdims=True))
        alpha = jnp.exp2((m_prev - m_new) * coef)
        p = jnp.exp2(s * coef - m_new[:, :1] * coef)
        m_scr[h] = m_new
        acc_ref[h] = acc_ref[h] * alpha[:, :1] + jnp.dot(
            p.astype(jnp.bfloat16), values_ext, preferred_element_type=jnp.float32
        )

    def with_ones(values):
        return jnp.concatenate([values, jnp.ones(values.shape, values.dtype)], axis=1)

    def tiles_step(masked):
        keys = jnp.concatenate([k[...] for k in k_refs], axis=1)
        values_ext = with_ones(jnp.concatenate([v[...] for v in v_refs], axis=0))
        mask = None
        if masked:
            slot = t * tpb + lax.broadcasted_iota(jnp.int32, (1, tpb * TILE), 1) // TILE
            mask = jnp.where(slot < live, 0.0, NEG_INF).astype(jnp.float32)

        def head_body(h, carry):
            fold(h, keys, values_ext, mask)
            return carry

        lax.fori_loop(0, group_size, head_body, 0)

    @pl.when((t + 1) * tpb <= live)
    def _():
        tiles_step(False)

    @pl.when(jnp.logical_and(t * tpb < live, (t + 1) * tpb > live))
    def _():
        tiles_step(True)

    @pl.when(t == last)
    def _():
        causal = jnp.where(qp_ref[...] >= kp_ref[...], 0.0, NEG_INF).astype(jnp.float32)
        nk = nk_ref[...]
        nv_ext = with_ones(nv_ref[...])

        def head_body(h, carry):
            fold(h, nk, nv_ext, causal)
            return carry

        lax.fori_loop(0, group_size, head_body, 0)
        for h in range(group_size):
            acc = acc_ref[h]
            sum_out[:, h * DH : (h + 1) * DH] = acc[:, :DH].astype(sum_out.dtype)
            m_out[:, h : h + 1] = m_scr[h][:, :1]
            l_out[:, h : h + 1] = acc[:, DH : DH + 1]


def local_attention(query_rows, cache_keys, cache_values, new_keys, new_values, keep, live, query_place, key_place):
    rows, width = query_rows.shape
    kv_local = new_keys.shape[1] // DH
    group_size = width // DH // kv_local
    slots = keep.shape[1]
    steps = slots // TPB
    q_new = new_keys.shape[0]

    def tile_map(j):
        def index_map(g, t, kt_ref, cnt_ref):
            return (kt_ref[g, jnp.minimum(t * TPB + j, cnt_ref[g] - 1)], g)

        return index_map

    tile_spec = [pl.BlockSpec((TILE, DH), tile_map(j)) for j in range(TPB)]

    def tile_map_t(j):
        def index_map(g, t, kt_ref, cnt_ref):
            return (g, kt_ref[g, jnp.minimum(t * TPB + j, cnt_ref[g] - 1)])

        return index_map

    tile_spec_t = [pl.BlockSpec((DH, TILE), tile_map_t(j)) for j in range(TPB)]
    grid_spec = pltpu.PrefetchScalarGridSpec(
        num_scalar_prefetch=2,
        grid=(kv_local, steps),
        in_specs=[pl.BlockSpec((rows, group_size * DH), lambda g, t, kt, cn: (0, g))]
        + tile_spec_t
        + tile_spec
        + [
            pl.BlockSpec((DH, q_new), lambda g, t, kt, cn: (g, 0)),
            pl.BlockSpec((q_new, DH), lambda g, t, kt, cn: (0, g)),
            pl.BlockSpec((rows, 1), lambda g, t, kt, cn: (0, 0)),
            pl.BlockSpec((1, q_new), lambda g, t, kt, cn: (0, 0)),
        ],
        out_specs=[
            pl.BlockSpec((rows, group_size * DH), lambda g, t, kt, cn: (0, g)),
            pl.BlockSpec((None, rows, group_size), lambda g, t, kt, cn: (g, 0, 0)),
            pl.BlockSpec((None, rows, group_size), lambda g, t, kt, cn: (g, 0, 0)),
        ],
        scratch_shapes=[
            pltpu.VMEM((group_size, rows, DH), jnp.float32),
            pltpu.VMEM((group_size, rows, 2 * DH), jnp.float32),
        ],
    )
    keys_total = slots * TILE + q_new
    flops = 4 * rows * kv_local * group_size * keys_total * DH
    cost = pl.CostEstimate(
        flops=flops,
        transcendentals=rows * kv_local * group_size * keys_total,
        bytes_accessed=rows * width * 2 + rows * width * 4 + 2 * kv_local * slots * TILE * DH * 2,
    )
    return pl.pallas_call(
        functools.partial(attn_kernel, TPB, group_size),
        grid_spec=grid_spec,
        out_shape=[
            jax.ShapeDtypeStruct((rows, width), jnp.bfloat16),
            jax.ShapeDtypeStruct((kv_local, rows, group_size), jnp.float32),
            jax.ShapeDtypeStruct((kv_local, rows, group_size), jnp.float32),
        ],
        compiler_params=pltpu.CompilerParams(
            dimension_semantics=("arbitrary", "arbitrary"), vmem_limit_bytes=56 * 1024 * 1024
        ),
        cost_estimate=cost,
    )(keep, live, query_rows, *([cache_keys.T] * TPB), *([cache_values] * TPB), new_keys.T, new_values, query_place, key_place)


def dense_fold(q_ref, h, keys_t, values_ext, mask, m_scr, acc_ref):
    coef = DH ** (-0.5) * LOG2E
    cols = pl.ds(pl.multiple_of(h * DH, DH), DH)
    s = jnp.dot(q_ref[:, cols], keys_t, preferred_element_type=jnp.float32) + mask
    m_prev = m_scr[h]
    m_new = jnp.maximum(m_prev, s.max(axis=1, keepdims=True))
    alpha = jnp.exp2((m_prev - m_new) * coef)
    p = jnp.exp2(s * coef - m_new[:, :1] * coef)
    m_scr[h] = m_new
    acc_ref[h] = acc_ref[h] * alpha[:, :1] + jnp.dot(
        p.astype(jnp.bfloat16), values_ext, preferred_element_type=jnp.float32
    )


def attn_push_kernel(n, group_size, per_dest, count, *refs):
    q_ref, kt_ref, v_ref, bias_ref, nkt_ref, nv_ref, qp_ref, kp_ref = refs[:8]
    srcs = refs[8 : 8 + count]
    sum_out, m_out, l_out = refs[8 + count : 11 + count]
    dsts = refs[11 + count : 11 + 2 * count]
    m_scr, acc_ref, send_sem, recv_sem, local_sem = refs[11 + 2 * count :]
    t = pl.program_id(0)
    last = pl.num_programs(0) - 1
    me = lax.axis_index("ctx")

    def remote_copies():
        out = []
        for a in range(count):
            for k in range(1, n):
                peer = lax.rem(me + k, n)
                out.append(
                    pltpu.make_async_remote_copy(
                        src_ref=srcs[a].at[peer] if per_dest[a] else srcs[a],
                        dst_ref=dsts[a].at[me],
                        send_sem=send_sem.at[a, k],
                        recv_sem=recv_sem.at[a, k],
                        device_id={"ctx": peer},
                        device_id_type=MESH,
                    )
                )
        return out

    def local_copies():
        return [
            pltpu.make_async_copy(
                srcs[a].at[me] if per_dest[a] else srcs[a], dsts[a].at[me], local_sem.at[a]
            )
            for a in range(count)
        ]

    def with_ones(values):
        return jnp.concatenate([values, jnp.ones(values.shape, values.dtype)], axis=1)

    @pl.when(t == 0)
    def _():
        barrier = pltpu.get_barrier_semaphore()
        for k in range(1, n):
            peer = lax.rem(me + k, n)
            pl.semaphore_signal(barrier, inc=1, device_id={"ctx": peer}, device_id_type=MESH)
        pl.semaphore_wait(barrier, n - 1)
        for c in remote_copies():
            c.start()
        for c in local_copies():
            c.start()
        m_scr[...] = jnp.full(m_scr.shape, NEG_INF, jnp.float32)
        acc_ref[...] = jnp.zeros(acc_ref.shape, jnp.float32)

    keys_t = kt_ref[...]
    values_ext = with_ones(v_ref[...])
    mask = bias_ref[...]

    def head_body(h, carry):
        dense_fold(q_ref, h, keys_t, values_ext, mask, m_scr, acc_ref)
        return carry

    lax.fori_loop(0, group_size, head_body, 0)

    @pl.when(t == last)
    def _():
        causal = jnp.where(qp_ref[...] >= kp_ref[...], 0.0, NEG_INF).astype(jnp.float32)
        nkt = nkt_ref[...]
        nv_ext = with_ones(nv_ref[...])

        def new_body(h, carry):
            dense_fold(q_ref, h, nkt, nv_ext, causal, m_scr, acc_ref)
            return carry

        lax.fori_loop(0, group_size, new_body, 0)
        for h in range(group_size):
            acc = acc_ref[h]
            sum_out[:, h * DH : (h + 1) * DH] = acc[:, :DH].astype(sum_out.dtype)
            m_out[:, h : h + 1] = m_scr[h][:, :1]
            l_out[:, h : h + 1] = acc[:, DH : DH + 1]
        for c in local_copies():
            c.wait()
        for c in remote_copies():
            c.wait()


def attention_with_push(query_rows, keys_t, values, bias, new_keys_t, new_values, query_place, key_place, sends, n, per_dest, collective_id):
    rows, width = query_rows.shape
    group_size = width // DH
    total_keys = keys_t.shape[1]
    step_keys = TPB * TILE
    steps = total_keys // step_keys
    q_new = new_values.shape[0]
    any_spec = pl.BlockSpec(memory_space=pl.ANY)
    count = len(sends)
    recv_shapes = [
        jax.ShapeDtypeStruct((n,) + tuple(x.shape[1:] if d else x.shape), x.dtype)
        for x, d in zip(sends, per_dest)
    ]
    flops = 4 * rows * group_size * (total_keys + q_new) * DH
    cost = pl.CostEstimate(
        flops=flops,
        transcendentals=rows * group_size * (total_keys + q_new),
        bytes_accessed=rows * width * 4 + 2 * total_keys * DH * 2,
    )
    return pl.pallas_call(
        functools.partial(attn_push_kernel, n, group_size, per_dest, count),
        grid=(steps,),
        in_specs=[
            pl.BlockSpec((rows, width), lambda t: (0, 0)),
            pl.BlockSpec((DH, step_keys), lambda t: (0, t)),
            pl.BlockSpec((step_keys, DH), lambda t: (t, 0)),
            pl.BlockSpec((1, step_keys), lambda t: (0, t)),
            pl.BlockSpec((DH, q_new), lambda t: (0, 0)),
            pl.BlockSpec((q_new, DH), lambda t: (0, 0)),
            pl.BlockSpec((rows, 1), lambda t: (0, 0)),
            pl.BlockSpec((1, q_new), lambda t: (0, 0)),
        ]
        + [any_spec] * count,
        out_specs=[
            pl.BlockSpec((rows, width), lambda t: (0, 0)),
            pl.BlockSpec((rows, group_size), lambda t: (0, 0)),
            pl.BlockSpec((rows, group_size), lambda t: (0, 0)),
        ]
        + [any_spec] * count,
        out_shape=[
            jax.ShapeDtypeStruct((rows, width), jnp.bfloat16),
            jax.ShapeDtypeStruct((rows, group_size), jnp.float32),
            jax.ShapeDtypeStruct((rows, group_size), jnp.float32),
        ]
        + recv_shapes,
        scratch_shapes=[
            pltpu.VMEM((group_size, rows, DH), jnp.float32),
            pltpu.VMEM((group_size, rows, 2 * DH), jnp.float32),
            pltpu.SemaphoreType.DMA((count, n)),
            pltpu.SemaphoreType.DMA((count, n)),
            pltpu.SemaphoreType.DMA((count,)),
        ],
        compiler_params=pltpu.CompilerParams(
            collective_id=collective_id, has_side_effects=True, vmem_limit_bytes=56 * 1024 * 1024
        ),
        cost_estimate=cost,
    )(query_rows, keys_t, values, bias, new_keys_t, new_values, query_place, key_place, *sends)


def combine_kernel(heads, part_ref, fac_ref, den_ref, out_ref):
    senders = part_ref.shape[0]
    width = part_ref.shape[3]
    half = width // DH

    def sender_body(i, acc):
        fac = fac_ref[i]
        out = []
        for h in range(heads):
            j, c = divmod(h, half)
            blk = part_ref[i, j][:, c * DH : (c + 1) * DH].astype(jnp.float32)
            out.append(acc[h] + blk * fac[:, h : h + 1])
        return tuple(out)

    rows = out_ref.shape[0]
    start = tuple(jnp.zeros((rows, DH), jnp.float32) for _ in range(heads))
    acc = lax.fori_loop(0, senders, sender_body, start)
    den = den_ref[...]
    for h in range(heads):
        out_ref[:, h * DH : (h + 1) * DH] = (acc[h] / den[:, h : h + 1]).astype(out_ref.dtype)


def combine(part_sum, factor, denominator):
    senders, groups, rows, width = part_sum.shape
    heads = groups * width // DH
    vmem = pl.BlockSpec(memory_space=pltpu.VMEM)
    return pl.pallas_call(
        functools.partial(combine_kernel, heads),
        out_shape=jax.ShapeDtypeStruct((rows, heads * DH), jnp.bfloat16),
        in_specs=[vmem, vmem, vmem],
        out_specs=vmem,
        compiler_params=pltpu.CompilerParams(vmem_limit_bytes=32 * 1024 * 1024),
    )(part_sum, factor, denominator)


def body(
    queries,
    new_keys,
    new_values,
    cache_keys,
    cache_values,
    keep_tiles,
    tile_count,
    owner_slot,
    out_weight,
):
    q_dev = queries.shape[0]
    kv_local = new_keys.shape[1] // DH
    q_local = queries.shape[1] // DH
    group_size = q_local // kv_local
    ctx_count = lax.axis_size("ctx")
    tp_count = lax.axis_size("tp")
    total_rows = q_dev * ctx_count
    my_index = lax.axis_index("ctx")
    key_place = owner_slot[my_index] * q_dev + jnp.arange(q_dev, dtype=jnp.int32)
    pieces = 4
    piece_heads = q_local // pieces
    width = piece_heads * DH
    (q_blocks,) = push((queries[:, :width],), "ctx", ctx_count, False, 0)
    query_place = (
        owner_slot[:, None] * q_dev + jnp.arange(q_dev, dtype=jnp.int32)[None, :]
    ).reshape(total_rows, 1)
    key_place = key_place.reshape(1, q_dev)
    slots = keep_tiles.shape[2]
    slot_ids = jnp.arange(slots * TILE, dtype=jnp.int32) // TILE

    def dense_head(g):
        cols = slice(g * DH, (g + 1) * DH)
        tiles_k = cache_keys[:, cols].reshape(-1, TILE, DH)
        tiles_v = cache_values[:, cols].reshape(-1, TILE, DH)
        kept_k = jnp.take(tiles_k, keep_tiles[0, g], axis=0).reshape(slots * TILE, DH)
        kept_v = jnp.take(tiles_v, keep_tiles[0, g], axis=0).reshape(slots * TILE, DH)
        bias = jnp.where(slot_ids < tile_count[0, g], 0.0, NEG_INF).astype(jnp.float32)
        return kept_k.T, kept_v, bias.reshape(1, slots * TILE), new_keys[:, cols].T, new_values[:, cols]

    head_data = [dense_head(g) for g in range(kv_local)]
    coef = DH ** (-0.5) * LOG2E

    def combine_piece(parts):
        part_sum, part_max, part_total = parts
        top_max = jnp.max(part_max, axis=0)
        factor = jnp.exp2((part_max - top_max[None]) * coef)
        denominator = jnp.sum(part_total * factor, axis=0)
        return combine(part_sum[:, None], factor, denominator)

    attn_pieces = []
    attn_blocks = []
    previous = None
    for i in range(pieces):
        sends = []
        flags = []
        if i + 1 < pieces:
            sends.append(queries[:, (i + 1) * width : (i + 2) * width])
            flags.append(False)
        if previous is not None:
            sends.extend(previous)
            flags.extend([True, True, True])
        if i >= 2:
            sends.append(attn_pieces[i - 2])
            flags.append(False)
        outs = attention_with_push(
            q_blocks.reshape(total_rows, width),
            *head_data[i * kv_local // pieces],
            query_place,
            key_place,
            tuple(sends),
            ctx_count,
            tuple(flags),
            4 + i,
        )
        sums_i, maxima_i, totals_i = outs[:3]
        rest = list(outs[3:])
        if i + 1 < pieces:
            q_blocks = rest.pop(0)
        if previous is not None:
            got = (rest.pop(0), rest.pop(0), rest.pop(0))
            attn_pieces.append(combine_piece(got))
        if i >= 2:
            attn_blocks.append(rest.pop(0))
        previous = (
            sums_i.reshape(ctx_count, q_dev, width),
            maxima_i.reshape(ctx_count, q_dev, piece_heads),
            totals_i.reshape(ctx_count, q_dev, piece_heads),
        )
    last_parts = push(
        previous + (attn_pieces[pieces - 2],), "ctx", ctx_count, (True, True, True, False), 1
    )
    attn_blocks.append(last_parts[3])
    attn_pieces.append(combine_piece(last_parts[:3]))
    attn_blocks.extend(push((attn_pieces[pieces - 1],), "ctx", ctx_count, False, 2))
    projected = None
    for j, blocks in enumerate(attn_blocks):
        term = jnp.dot(
            blocks.reshape(total_rows, width),
            out_weight[j * width : (j + 1) * width],
            preferred_element_type=jnp.float32,
        )
        projected = term if projected is None else projected + term
    out_rows = total_rows // tp_count
    (proj_parts,) = push(
        (projected.reshape(tp_count, out_rows, projected.shape[1]),), "tp", tp_count, True, 3
    )
    return jnp.sum(proj_parts, axis=0)


def solution(mesh):
    return jax.shard_map(
        body,
        mesh=mesh,
        in_specs=(
            P("ctx", "tp"),
            P("ctx", "tp"),
            P("ctx", "tp"),
            P("ctx", "tp"),
            P("ctx", "tp"),
            P("ctx", "tp", None),
            P("ctx", "tp"),
            P(),
            P("tp", "ctx"),
        ),
        out_specs=P("tp", "ctx"),
        check_vma=False,
    )
```

```python
import functools

import jax
import jax.numpy as jnp
from jax import lax
from jax.experimental import pallas as pl
from jax.experimental.pallas import tpu as pltpu
from jax.sharding import PartitionSpec as P

DH = 128
TILE = 128
TB = 4
MESH = pl.DeviceIdType.MESH

NEG_INF = -jnp.inf


def push_kernel(axis, n, per_dest, count, *refs):
    x_refs = refs[:count]
    y_refs = refs[count : 2 * count]
    send_sem, recv_sem, local_sem = refs[2 * count :]
    me = lax.axis_index(axis)
    barrier = pltpu.get_barrier_semaphore()
    for k in range(1, n):
        peer = lax.rem(me + k, n)
        pl.semaphore_signal(barrier, inc=1, device_id={axis: peer}, device_id_type=MESH)
    pl.semaphore_wait(barrier, n - 1)
    copies = []
    for a in range(count):
        for k in range(1, n):
            peer = lax.rem(me + k, n)
            src = x_refs[a].at[peer] if per_dest else x_refs[a]
            copy = pltpu.make_async_remote_copy(
                src_ref=src,
                dst_ref=y_refs[a].at[me],
                send_sem=send_sem.at[a, k],
                recv_sem=recv_sem.at[a, k],
                device_id={axis: peer},
                device_id_type=MESH,
            )
            copy.start()
            copies.append(copy)
    locals_ = []
    for a in range(count):
        src = x_refs[a].at[me] if per_dest else x_refs[a]
        local = pltpu.make_async_copy(src, y_refs[a].at[me], local_sem.at[a])
        local.start()
        locals_.append(local)
    for local in locals_:
        local.wait()
    for copy in copies:
        copy.wait()


def push(xs, axis, n, per_dest, collective_id):
    count = len(xs)
    out_shape = []
    for x in xs:
        block = x.shape[1:] if per_dest else x.shape
        out_shape.append(jax.ShapeDtypeStruct((n,) + tuple(block), x.dtype))
    any_spec = pl.BlockSpec(memory_space=pl.ANY)
    return pl.pallas_call(
        functools.partial(push_kernel, axis, n, per_dest, count),
        out_shape=tuple(out_shape),
        in_specs=[any_spec] * count,
        out_specs=tuple([any_spec] * count),
        scratch_shapes=[
            pltpu.SemaphoreType.DMA((count, n)),
            pltpu.SemaphoreType.DMA((count, n)),
            pltpu.SemaphoreType.DMA((count,)),
        ],
        compiler_params=pltpu.CompilerParams(collective_id=collective_id, has_side_effects=True),
    )(*xs)


TPB = 8
LOG2E = 1.4426950408889634


def dot_nt(a, b):
    return jnp.dot(a, b, preferred_element_type=jnp.float32)


def attn_kernel(tpb, group_size, kt_ref, cnt_ref, q_ref, *refs):
    k_refs = refs[:tpb]
    v_refs = refs[tpb : 2 * tpb]
    nk_ref, nv_ref, qp_ref, kp_ref = refs[2 * tpb : 2 * tpb + 4]
    sum_out, m_out, l_out = refs[2 * tpb + 4 : 2 * tpb + 7]
    m_scr, acc_ref = refs[2 * tpb + 7 :]
    g = pl.program_id(0)
    t = pl.program_id(1)
    last = pl.num_programs(1) - 1
    live = cnt_ref[g]
    coef = DH ** (-0.5) * LOG2E

    @pl.when(t == 0)
    def _():
        m_scr[...] = jnp.full(m_scr.shape, NEG_INF, jnp.float32)
        acc_ref[...] = jnp.zeros(acc_ref.shape, jnp.float32)

    def fold(h, keys, values_ext, mask):
        cols = pl.ds(pl.multiple_of(h * DH, DH), DH)
        s = dot_nt(q_ref[:, cols], keys)
        if mask is not None:
            s = s + mask
        m_prev = m_scr[h]
        m_new = jnp.maximum(m_prev, s.max(axis=1, keepdims=True))
        alpha = jnp.exp2((m_prev - m_new) * coef)
        p = jnp.exp2(s * coef - m_new[:, :1] * coef)
        m_scr[h] = m_new
        acc_ref[h] = acc_ref[h] * alpha[:, :1] + jnp.dot(
            p.astype(jnp.bfloat16), values_ext, preferred_element_type=jnp.float32
        )

    def with_ones(values):
        return jnp.concatenate([values, jnp.ones(values.shape, values.dtype)], axis=1)

    def tiles_step(masked):
        keys = jnp.concatenate([k[...] for k in k_refs], axis=1)
        values_ext = with_ones(jnp.concatenate([v[...] for v in v_refs], axis=0))
        mask = None
        if masked:
            slot = t * tpb + lax.broadcasted_iota(jnp.int32, (1, tpb * TILE), 1) // TILE
            mask = jnp.where(slot < live, 0.0, NEG_INF).astype(jnp.float32)

        def head_body(h, carry):
            fold(h, keys, values_ext, mask)
            return carry

        lax.fori_loop(0, group_size, head_body, 0)

    @pl.when((t + 1) * tpb <= live)
    def _():
        tiles_step(False)

    @pl.when(jnp.logical_and(t * tpb < live, (t + 1) * tpb > live))
    def _():
        tiles_step(True)

    @pl.when(t == last)
    def _():
        causal = jnp.where(qp_ref[...] >= kp_ref[...], 0.0, NEG_INF).astype(jnp.float32)
        nk = nk_ref[...]
        nv_ext = with_ones(nv_ref[...])

        def head_body(h, carry):
            fold(h, nk, nv_ext, causal)
            return carry

        lax.fori_loop(0, group_size, head_body, 0)
        for h in range(group_size):
            acc = acc_ref[h]
            sum_out[:, h * DH : (h + 1) * DH] = acc[:, :DH].astype(sum_out.dtype)
            m_out[:, h : h + 1] = m_scr[h][:, :1]
            l_out[:, h : h + 1] = acc[:, DH : DH + 1]


def local_attention(query_rows, cache_keys, cache_values, new_keys, new_values, keep, live, query_place, key_place):
    rows, width = query_rows.shape
    kv_local = new_keys.shape[1] // DH
    group_size = width // DH // kv_local
    slots = keep.shape[1]
    steps = slots // TPB
    q_new = new_keys.shape[0]

    def tile_map(j):
        def index_map(g, t, kt_ref, cnt_ref):
            return (kt_ref[g, jnp.minimum(t * TPB + j, cnt_ref[g] - 1)], g)

        return index_map

    tile_spec = [pl.BlockSpec((TILE, DH), tile_map(j)) for j in range(TPB)]

    def tile_map_t(j):
        def index_map(g, t, kt_ref, cnt_ref):
            return (g, kt_ref[g, jnp.minimum(t * TPB + j, cnt_ref[g] - 1)])

        return index_map

    tile_spec_t = [pl.BlockSpec((DH, TILE), tile_map_t(j)) for j in range(TPB)]
    grid_spec = pltpu.PrefetchScalarGridSpec(
        num_scalar_prefetch=2,
        grid=(kv_local, steps),
        in_specs=[pl.BlockSpec((rows, group_size * DH), lambda g, t, kt, cn: (0, g))]
        + tile_spec_t
        + tile_spec
        + [
            pl.BlockSpec((DH, q_new), lambda g, t, kt, cn: (g, 0)),
            pl.BlockSpec((q_new, DH), lambda g, t, kt, cn: (0, g)),
            pl.BlockSpec((rows, 1), lambda g, t, kt, cn: (0, 0)),
            pl.BlockSpec((1, q_new), lambda g, t, kt, cn: (0, 0)),
        ],
        out_specs=[
            pl.BlockSpec((rows, group_size * DH), lambda g, t, kt, cn: (0, g)),
            pl.BlockSpec((None, rows, group_size), lambda g, t, kt, cn: (g, 0, 0)),
            pl.BlockSpec((None, rows, group_size), lambda g, t, kt, cn: (g, 0, 0)),
        ],
        scratch_shapes=[
            pltpu.VMEM((group_size, rows, DH), jnp.float32),
            pltpu.VMEM((group_size, rows, 2 * DH), jnp.float32),
        ],
    )
    keys_total = slots * TILE + q_new
    flops = 4 * rows * kv_local * group_size * keys_total * DH
    cost = pl.CostEstimate(
        flops=flops,
        transcendentals=rows * kv_local * group_size * keys_total,
        bytes_accessed=rows * width * 2 + rows * width * 4 + 2 * kv_local * slots * TILE * DH * 2,
    )
    return pl.pallas_call(
        functools.partial(attn_kernel, TPB, group_size),
        grid_spec=grid_spec,
        out_shape=[
            jax.ShapeDtypeStruct((rows, width), jnp.bfloat16),
            jax.ShapeDtypeStruct((kv_local, rows, group_size), jnp.float32),
            jax.ShapeDtypeStruct((kv_local, rows, group_size), jnp.float32),
        ],
        compiler_params=pltpu.CompilerParams(
            dimension_semantics=("arbitrary", "arbitrary"), vmem_limit_bytes=56 * 1024 * 1024
        ),
        cost_estimate=cost,
    )(keep, live, query_rows, *([cache_keys.T] * TPB), *([cache_values] * TPB), new_keys.T, new_values, query_place, key_place)


def dense_fold(q_ref, h, keys_t, values_ext, mask, m_scr, acc_ref):
    coef = DH ** (-0.5) * LOG2E
    cols = pl.ds(pl.multiple_of(h * DH, DH), DH)
    s = lax.dot_general(
        q_ref[:, cols], keys_t, (((1,), (1,)), ((), ())), preferred_element_type=jnp.float32
    ) + mask
    m_prev = m_scr[h]
    m_new = jnp.maximum(m_prev, s.max(axis=1, keepdims=True))
    alpha = jnp.exp2((m_prev - m_new) * coef)
    p = jnp.exp2(s * coef - m_new[:, :1] * coef)
    m_scr[h] = m_new
    acc_ref[h] = acc_ref[h] * alpha[:, :1] + jnp.dot(
        p.astype(jnp.bfloat16), values_ext, preferred_element_type=jnp.float32
    )


def attn_push_kernel(n, group_size, per_dest, count, *refs):
    q_ref, kt_ref, v_ref, bias_ref, nkt_ref, nv_ref, qp_ref, kp_ref = refs[:8]
    srcs = refs[8 : 8 + count]
    sum_out, m_out, l_out = refs[8 + count : 11 + count]
    dsts = refs[11 + count : 11 + 2 * count]
    m_scr, acc_ref, send_sem, recv_sem, local_sem = refs[11 + 2 * count :]
    t = pl.program_id(0)
    last = pl.num_programs(0) - 1
    me = lax.axis_index("ctx")

    def remote_copies():
        out = []
        for a in range(count):
            for k in range(1, n):
                peer = lax.rem(me + k, n)
                out.append(
                    pltpu.make_async_remote_copy(
                        src_ref=srcs[a].at[peer] if per_dest[a] else srcs[a],
                        dst_ref=dsts[a].at[me],
                        send_sem=send_sem.at[a, k],
                        recv_sem=recv_sem.at[a, k],
                        device_id={"ctx": peer},
                        device_id_type=MESH,
                    )
                )
        return out

    def local_copies():
        return [
            pltpu.make_async_copy(
                srcs[a].at[me] if per_dest[a] else srcs[a], dsts[a].at[me], local_sem.at[a]
            )
            for a in range(count)
        ]

    def with_ones(values):
        return jnp.concatenate([values, jnp.ones(values.shape, values.dtype)], axis=1)

    @pl.when(t == 0)
    def _():
        barrier = pltpu.get_barrier_semaphore()
        for k in range(1, n):
            peer = lax.rem(me + k, n)
            pl.semaphore_signal(barrier, inc=1, device_id={"ctx": peer}, device_id_type=MESH)
        pl.semaphore_wait(barrier, n - 1)
        for c in remote_copies():
            c.start()
        for c in local_copies():
            c.start()
        m_scr[...] = jnp.full(m_scr.shape, NEG_INF, jnp.float32)
        acc_ref[...] = jnp.zeros(acc_ref.shape, jnp.float32)

    keys_t = kt_ref[...]
    values_ext = with_ones(v_ref[...])
    mask = bias_ref[...]

    def head_body(h, carry):
        dense_fold(q_ref, h, keys_t, values_ext, mask, m_scr, acc_ref)
        return carry

    lax.fori_loop(0, group_size, head_body, 0)

    @pl.when(t == last)
    def _():
        causal = jnp.where(qp_ref[...] >= kp_ref[...], 0.0, NEG_INF).astype(jnp.float32)
        nkt = nkt_ref[...]
        nv_ext = with_ones(nv_ref[...])

        def new_body(h, carry):
            dense_fold(q_ref, h, nkt, nv_ext, causal, m_scr, acc_ref)
            return carry

        lax.fori_loop(0, group_size, new_body, 0)
        for h in range(group_size):
            acc = acc_ref[h]
            sum_out[:, h * DH : (h + 1) * DH] = acc[:, :DH].astype(sum_out.dtype)
            m_out[:, h : h + 1] = m_scr[h][:, :1]
            l_out[:, h : h + 1] = acc[:, DH : DH + 1]
        for c in local_copies():
            c.wait()
        for c in remote_copies():
            c.wait()


def attention_with_push(query_rows, keys_t, values, bias, new_keys_t, new_values, query_place, key_place, sends, n, per_dest, collective_id):
    rows, width = query_rows.shape
    group_size = width // DH
    total_keys = keys_t.shape[0]
    step_keys = TPB * TILE
    steps = total_keys // step_keys
    q_new = new_values.shape[0]
    any_spec = pl.BlockSpec(memory_space=pl.ANY)
    count = len(sends)
    recv_shapes = [
        jax.ShapeDtypeStruct((n,) + tuple(x.shape[1:] if d else x.shape), x.dtype)
        for x, d in zip(sends, per_dest)
    ]
    flops = 4 * rows * group_size * (total_keys + q_new) * DH
    cost = pl.CostEstimate(
        flops=flops,
        transcendentals=rows * group_size * (total_keys + q_new),
        bytes_accessed=rows * width * 4 + 2 * total_keys * DH * 2,
    )
    return pl.pallas_call(
        functools.partial(attn_push_kernel, n, group_size, per_dest, count),
        grid=(steps,),
        in_specs=[
            pl.BlockSpec((rows, width), lambda t: (0, 0)),
            pl.BlockSpec((step_keys, DH), lambda t: (t, 0)),
            pl.BlockSpec((step_keys, DH), lambda t: (t, 0)),
            pl.BlockSpec((1, step_keys), lambda t: (0, t)),
            pl.BlockSpec((q_new, DH), lambda t: (0, 0)),
            pl.BlockSpec((q_new, DH), lambda t: (0, 0)),
            pl.BlockSpec((rows, 1), lambda t: (0, 0)),
            pl.BlockSpec((1, q_new), lambda t: (0, 0)),
        ]
        + [any_spec] * count,
        out_specs=[
            pl.BlockSpec((rows, width), lambda t: (0, 0)),
            pl.BlockSpec((rows, group_size), lambda t: (0, 0)),
            pl.BlockSpec((rows, group_size), lambda t: (0, 0)),
        ]
        + [any_spec] * count,
        out_shape=[
            jax.ShapeDtypeStruct((rows, width), jnp.bfloat16),
            jax.ShapeDtypeStruct((rows, group_size), jnp.float32),
            jax.ShapeDtypeStruct((rows, group_size), jnp.float32),
        ]
        + recv_shapes,
        scratch_shapes=[
            pltpu.VMEM((group_size, rows, DH), jnp.float32),
            pltpu.VMEM((group_size, rows, 2 * DH), jnp.float32),
            pltpu.SemaphoreType.DMA((count, n)),
            pltpu.SemaphoreType.DMA((count, n)),
            pltpu.SemaphoreType.DMA((count,)),
        ],
        compiler_params=pltpu.CompilerParams(
            collective_id=collective_id, has_side_effects=True, vmem_limit_bytes=56 * 1024 * 1024
        ),
        cost_estimate=cost,
    )(query_rows, keys_t, values, bias, new_keys_t, new_values, query_place, key_place, *sends)


def combine_kernel(heads, part_ref, fac_ref, den_ref, out_ref):
    senders = part_ref.shape[0]
    width = part_ref.shape[3]
    half = width // DH

    def sender_body(i, acc):
        fac = fac_ref[i]
        out = []
        for h in range(heads):
            j, c = divmod(h, half)
            blk = part_ref[i, j][:, c * DH : (c + 1) * DH].astype(jnp.float32)
            out.append(acc[h] + blk * fac[:, h : h + 1])
        return tuple(out)

    rows = out_ref.shape[0]
    start = tuple(jnp.zeros((rows, DH), jnp.float32) for _ in range(heads))
    acc = lax.fori_loop(0, senders, sender_body, start)
    den = den_ref[...]
    for h in range(heads):
        out_ref[:, h * DH : (h + 1) * DH] = (acc[h] / den[:, h : h + 1]).astype(out_ref.dtype)


def combine(part_sum, factor, denominator):
    senders, groups, rows, width = part_sum.shape
    heads = groups * width // DH
    vmem = pl.BlockSpec(memory_space=pltpu.VMEM)
    return pl.pallas_call(
        functools.partial(combine_kernel, heads),
        out_shape=jax.ShapeDtypeStruct((rows, heads * DH), jnp.bfloat16),
        in_specs=[vmem, vmem, vmem],
        out_specs=vmem,
        compiler_params=pltpu.CompilerParams(vmem_limit_bytes=32 * 1024 * 1024),
    )(part_sum, factor, denominator)


def body(
    queries,
    new_keys,
    new_values,
    cache_keys,
    cache_values,
    keep_tiles,
    tile_count,
    owner_slot,
    out_weight,
):
    q_dev = queries.shape[0]
    kv_local = new_keys.shape[1] // DH
    q_local = queries.shape[1] // DH
    group_size = q_local // kv_local
    ctx_count = lax.axis_size("ctx")
    tp_count = lax.axis_size("tp")
    total_rows = q_dev * ctx_count
    my_index = lax.axis_index("ctx")
    key_place = owner_slot[my_index] * q_dev + jnp.arange(q_dev, dtype=jnp.int32)
    pieces = 4
    piece_heads = q_local // pieces
    width = piece_heads * DH
    (q_blocks,) = push((queries[:, :width],), "ctx", ctx_count, False, 0)
    query_place = (
        owner_slot[:, None] * q_dev + jnp.arange(q_dev, dtype=jnp.int32)[None, :]
    ).reshape(total_rows, 1)
    key_place = key_place.reshape(1, q_dev)
    slots = keep_tiles.shape[2]
    slot_ids = jnp.arange(slots * TILE, dtype=jnp.int32) // TILE

    def dense_head(g):
        cols = slice(g * DH, (g + 1) * DH)
        tiles_k = cache_keys[:, cols].reshape(-1, TILE, DH)
        tiles_v = cache_values[:, cols].reshape(-1, TILE, DH)
        kept_k = jnp.take(tiles_k, keep_tiles[0, g], axis=0).reshape(slots * TILE, DH)
        kept_v = jnp.take(tiles_v, keep_tiles[0, g], axis=0).reshape(slots * TILE, DH)
        bias = jnp.where(slot_ids < tile_count[0, g], 0.0, NEG_INF).astype(jnp.float32)
        return kept_k, kept_v, bias.reshape(1, slots * TILE), new_keys[:, cols], new_values[:, cols]

    head_data = [dense_head(g) for g in range(kv_local)]
    coef = DH ** (-0.5) * LOG2E

    def combine_piece(parts):
        part_sum, part_max, part_total = parts
        top_max = jnp.max(part_max, axis=0)
        factor = jnp.exp2((part_max - top_max[None]) * coef)
        denominator = jnp.sum(part_total * factor, axis=0)
        return combine(part_sum[:, None], factor, denominator)

    attn_pieces = []
    attn_blocks = []
    previous = None
    for i in range(pieces):
        sends = []
        flags = []
        if i + 1 < pieces:
            sends.append(queries[:, (i + 1) * width : (i + 2) * width])
            flags.append(False)
        if previous is not None:
            sends.extend(previous)
            flags.extend([True, True, True])
        if i >= 2:
            sends.append(attn_pieces[i - 2])
            flags.append(False)
        outs = attention_with_push(
            q_blocks.reshape(total_rows, width),
            *head_data[i * kv_local // pieces],
            query_place,
            key_place,
            tuple(sends),
            ctx_count,
            tuple(flags),
            4 + i,
        )
        sums_i, maxima_i, totals_i = outs[:3]
        rest = list(outs[3:])
        if i + 1 < pieces:
            q_blocks = rest.pop(0)
        if previous is not None:
            got = (rest.pop(0), rest.pop(0), rest.pop(0))
            attn_pieces.append(combine_piece(got))
        if i >= 2:
            attn_blocks.append(rest.pop(0))
        previous = (
            sums_i.reshape(ctx_count, q_dev, width),
            maxima_i.reshape(ctx_count, q_dev, piece_heads),
            totals_i.reshape(ctx_count, q_dev, piece_heads),
        )
    attn_pieces.append(combine_piece(push(previous, "ctx", ctx_count, True, 1)))
    attn_blocks.extend(push(tuple(attn_pieces[pieces - 2 :]), "ctx", ctx_count, False, 2))
    projected = None
    for j, blocks in enumerate(attn_blocks):
        term = jnp.dot(
            blocks.reshape(total_rows, width),
            out_weight[j * width : (j + 1) * width],
            preferred_element_type=jnp.float32,
        )
        projected = term if projected is None else projected + term
    out_rows = total_rows // tp_count
    (proj_parts,) = push(
        (projected.reshape(tp_count, out_rows, projected.shape[1]),), "tp", tp_count, True, 3
    )
    return jnp.sum(proj_parts, axis=0)


def solution(mesh):
    return jax.shard_map(
        body,
        mesh=mesh,
        in_specs=(
            P("ctx", "tp"),
            P("ctx", "tp"),
            P("ctx", "tp"),
            P("ctx", "tp"),
            P("ctx", "tp"),
            P("ctx", "tp", None),
            P("ctx", "tp"),
            P(),
            P("tp", "ctx"),
        ),
        out_specs=P("tp", "ctx"),
        check_vma=False,
    )
```

```python
import functools

import jax
import jax.numpy as jnp
from jax import lax
from jax.experimental import pallas as pl
from jax.experimental.pallas import tpu as pltpu
from jax.sharding import PartitionSpec as P

DH = 128
TILE = 128
TB = 4
MESH = pl.DeviceIdType.MESH

NEG_INF = -jnp.inf


def push_kernel(axis, n, per_dest, count, *refs):
    x_refs = refs[:count]
    y_refs = refs[count : 2 * count]
    send_sem, recv_sem, local_sem = refs[2 * count :]
    me = lax.axis_index(axis)
    barrier = pltpu.get_barrier_semaphore()
    for k in range(1, n):
        peer = lax.rem(me + k, n)
        pl.semaphore_signal(barrier, inc=1, device_id={axis: peer}, device_id_type=MESH)
    pl.semaphore_wait(barrier, n - 1)
    copies = []
    for a in range(count):
        for k in range(1, n):
            peer = lax.rem(me + k, n)
            src = x_refs[a].at[peer] if per_dest[a] else x_refs[a]
            copy = pltpu.make_async_remote_copy(
                src_ref=src,
                dst_ref=y_refs[a].at[me],
                send_sem=send_sem.at[a, k],
                recv_sem=recv_sem.at[a, k],
                device_id={axis: peer},
                device_id_type=MESH,
            )
            copy.start()
            copies.append(copy)
    locals_ = []
    for a in range(count):
        src = x_refs[a].at[me] if per_dest[a] else x_refs[a]
        local = pltpu.make_async_copy(src, y_refs[a].at[me], local_sem.at[a])
        local.start()
        locals_.append(local)
    for local in locals_:
        local.wait()
    for copy in copies:
        copy.wait()


def push(xs, axis, n, per_dest, collective_id):
    count = len(xs)
    if isinstance(per_dest, bool):
        per_dest = (per_dest,) * count
    out_shape = []
    for x, d in zip(xs, per_dest):
        block = x.shape[1:] if d else x.shape
        out_shape.append(jax.ShapeDtypeStruct((n,) + tuple(block), x.dtype))
    any_spec = pl.BlockSpec(memory_space=pl.ANY)
    return pl.pallas_call(
        functools.partial(push_kernel, axis, n, per_dest, count),
        out_shape=tuple(out_shape),
        in_specs=[any_spec] * count,
        out_specs=tuple([any_spec] * count),
        scratch_shapes=[
            pltpu.SemaphoreType.DMA((count, n)),
            pltpu.SemaphoreType.DMA((count, n)),
            pltpu.SemaphoreType.DMA((count,)),
        ],
        compiler_params=pltpu.CompilerParams(collective_id=collective_id, has_side_effects=True),
    )(*xs)


TPB = 8
LOG2E = 1.4426950408889634


def dot_nt(a, b):
    return jnp.dot(a, b, preferred_element_type=jnp.float32)


def attn_kernel(tpb, group_size, kt_ref, cnt_ref, q_ref, *refs):
    k_refs = refs[:tpb]
    v_refs = refs[tpb : 2 * tpb]
    nk_ref, nv_ref, qp_ref, kp_ref = refs[2 * tpb : 2 * tpb + 4]
    sum_out, m_out, l_out = refs[2 * tpb + 4 : 2 * tpb + 7]
    m_scr, acc_ref = refs[2 * tpb + 7 :]
    g = pl.program_id(0)
    t = pl.program_id(1)
    last = pl.num_programs(1) - 1
    live = cnt_ref[g]
    coef = DH ** (-0.5) * LOG2E

    @pl.when(t == 0)
    def _():
        m_scr[...] = jnp.full(m_scr.shape, NEG_INF, jnp.float32)
        acc_ref[...] = jnp.zeros(acc_ref.shape, jnp.float32)

    def fold(h, keys, values_ext, mask):
        cols = pl.ds(pl.multiple_of(h * DH, DH), DH)
        s = dot_nt(q_ref[:, cols], keys)
        if mask is not None:
            s = s + mask
        m_prev = m_scr[h]
        m_new = jnp.maximum(m_prev, s.max(axis=1, keepdims=True))
        alpha = jnp.exp2((m_prev - m_new) * coef)
        p = jnp.exp2(s * coef - m_new[:, :1] * coef)
        m_scr[h] = m_new
        acc_ref[h] = acc_ref[h] * alpha[:, :1] + jnp.dot(
            p.astype(jnp.bfloat16), values_ext, preferred_element_type=jnp.float32
        )

    def with_ones(values):
        return jnp.concatenate([values, jnp.ones(values.shape, values.dtype)], axis=1)

    def tiles_step(masked):
        keys = jnp.concatenate([k[...] for k in k_refs], axis=1)
        values_ext = with_ones(jnp.concatenate([v[...] for v in v_refs], axis=0))
        mask = None
        if masked:
            slot = t * tpb + lax.broadcasted_iota(jnp.int32, (1, tpb * TILE), 1) // TILE
            mask = jnp.where(slot < live, 0.0, NEG_INF).astype(jnp.float32)

        def head_body(h, carry):
            fold(h, keys, values_ext, mask)
            return carry

        lax.fori_loop(0, group_size, head_body, 0)

    @pl.when((t + 1) * tpb <= live)
    def _():
        tiles_step(False)

    @pl.when(jnp.logical_and(t * tpb < live, (t + 1) * tpb > live))
    def _():
        tiles_step(True)

    @pl.when(t == last)
    def _():
        causal = jnp.where(qp_ref[...] >= kp_ref[...], 0.0, NEG_INF).astype(jnp.float32)
        nk = nk_ref[...]
        nv_ext = with_ones(nv_ref[...])

        def head_body(h, carry):
            fold(h, nk, nv_ext, causal)
            return carry

        lax.fori_loop(0, group_size, head_body, 0)
        for h in range(group_size):
            acc = acc_ref[h]
            sum_out[:, h * DH : (h + 1) * DH] = acc[:, :DH].astype(sum_out.dtype)
            m_out[:, h : h + 1] = m_scr[h][:, :1]
            l_out[:, h : h + 1] = acc[:, DH : DH + 1]


def local_attention(query_rows, cache_keys, cache_values, new_keys, new_values, keep, live, query_place, key_place):
    rows, width = query_rows.shape
    kv_local = new_keys.shape[1] // DH
    group_size = width // DH // kv_local
    slots = keep.shape[1]
    steps = slots // TPB
    q_new = new_keys.shape[0]

    def tile_map(j):
        def index_map(g, t, kt_ref, cnt_ref):
            return (kt_ref[g, jnp.minimum(t * TPB + j, cnt_ref[g] - 1)], g)

        return index_map

    tile_spec = [pl.BlockSpec((TILE, DH), tile_map(j)) for j in range(TPB)]

    def tile_map_t(j):
        def index_map(g, t, kt_ref, cnt_ref):
            return (g, kt_ref[g, jnp.minimum(t * TPB + j, cnt_ref[g] - 1)])

        return index_map

    tile_spec_t = [pl.BlockSpec((DH, TILE), tile_map_t(j)) for j in range(TPB)]
    grid_spec = pltpu.PrefetchScalarGridSpec(
        num_scalar_prefetch=2,
        grid=(kv_local, steps),
        in_specs=[pl.BlockSpec((rows, group_size * DH), lambda g, t, kt, cn: (0, g))]
        + tile_spec_t
        + tile_spec
        + [
            pl.BlockSpec((DH, q_new), lambda g, t, kt, cn: (g, 0)),
            pl.BlockSpec((q_new, DH), lambda g, t, kt, cn: (0, g)),
            pl.BlockSpec((rows, 1), lambda g, t, kt, cn: (0, 0)),
            pl.BlockSpec((1, q_new), lambda g, t, kt, cn: (0, 0)),
        ],
        out_specs=[
            pl.BlockSpec((rows, group_size * DH), lambda g, t, kt, cn: (0, g)),
            pl.BlockSpec((None, rows, group_size), lambda g, t, kt, cn: (g, 0, 0)),
            pl.BlockSpec((None, rows, group_size), lambda g, t, kt, cn: (g, 0, 0)),
        ],
        scratch_shapes=[
            pltpu.VMEM((group_size, rows, DH), jnp.float32),
            pltpu.VMEM((group_size, rows, 2 * DH), jnp.float32),
        ],
    )
    keys_total = slots * TILE + q_new
    flops = 4 * rows * kv_local * group_size * keys_total * DH
    cost = pl.CostEstimate(
        flops=flops,
        transcendentals=rows * kv_local * group_size * keys_total,
        bytes_accessed=rows * width * 2 + rows * width * 4 + 2 * kv_local * slots * TILE * DH * 2,
    )
    return pl.pallas_call(
        functools.partial(attn_kernel, TPB, group_size),
        grid_spec=grid_spec,
        out_shape=[
            jax.ShapeDtypeStruct((rows, width), jnp.bfloat16),
            jax.ShapeDtypeStruct((kv_local, rows, group_size), jnp.float32),
            jax.ShapeDtypeStruct((kv_local, rows, group_size), jnp.float32),
        ],
        compiler_params=pltpu.CompilerParams(
            dimension_semantics=("arbitrary", "arbitrary"), vmem_limit_bytes=56 * 1024 * 1024
        ),
        cost_estimate=cost,
    )(keep, live, query_rows, *([cache_keys.T] * TPB), *([cache_values] * TPB), new_keys.T, new_values, query_place, key_place)


def dense_fold(q_ref, h, keys_t, values_ext, mask, m_scr, acc_ref):
    coef = DH ** (-0.5) * LOG2E
    cols = pl.ds(pl.multiple_of(h * DH, DH), DH)
    s = jnp.dot(q_ref[:, cols], keys_t, preferred_element_type=jnp.float32) + mask
    m_prev = m_scr[h]
    m_new = jnp.maximum(m_prev, s.max(axis=1, keepdims=True))
    alpha = jnp.exp2((m_prev - m_new) * coef)
    p = jnp.exp2(s * coef - m_new[:, :1] * coef)
    m_scr[h] = m_new
    acc_ref[h] = acc_ref[h] * alpha[:, :1] + jnp.dot(
        p.astype(jnp.bfloat16), values_ext, preferred_element_type=jnp.float32
    )


def attn_push_kernel(n, group_size, per_dest, count, *refs):
    q_ref, kt_ref, v_ref, bias_ref, nkt_ref, nv_ref, qp_ref, kp_ref = refs[:8]
    srcs = refs[8 : 8 + count]
    sum_out, m_out, l_out = refs[8 + count : 11 + count]
    dsts = refs[11 + count : 11 + 2 * count]
    m_scr, acc_ref, send_sem, recv_sem, local_sem = refs[11 + 2 * count :]
    t = pl.program_id(0)
    last = pl.num_programs(0) - 1
    me = lax.axis_index("ctx")

    def remote_copies():
        out = []
        for a in range(count):
            for k in range(1, n):
                peer = lax.rem(me + k, n)
                out.append(
                    pltpu.make_async_remote_copy(
                        src_ref=srcs[a].at[peer] if per_dest[a] else srcs[a],
                        dst_ref=dsts[a].at[me],
                        send_sem=send_sem.at[a, k],
                        recv_sem=recv_sem.at[a, k],
                        device_id={"ctx": peer},
                        device_id_type=MESH,
                    )
                )
        return out

    def local_copies():
        return [
            pltpu.make_async_copy(
                srcs[a].at[me] if per_dest[a] else srcs[a], dsts[a].at[me], local_sem.at[a]
            )
            for a in range(count)
        ]

    def with_ones(values):
        return jnp.concatenate([values, jnp.ones(values.shape, values.dtype)], axis=1)

    @pl.when(t == 0)
    def _():
        barrier = pltpu.get_barrier_semaphore()
        for k in range(1, n):
            peer = lax.rem(me + k, n)
            pl.semaphore_signal(barrier, inc=1, device_id={"ctx": peer}, device_id_type=MESH)
        pl.semaphore_wait(barrier, n - 1)
        for c in remote_copies():
            c.start()
        for c in local_copies():
            c.start()
        m_scr[...] = jnp.full(m_scr.shape, NEG_INF, jnp.float32)
        acc_ref[...] = jnp.zeros(acc_ref.shape, jnp.float32)

    keys_t = kt_ref[...]
    values_ext = with_ones(v_ref[...])
    mask = bias_ref[...]

    def head_body(h, carry):
        dense_fold(q_ref, h, keys_t, values_ext, mask, m_scr, acc_ref)
        return carry

    lax.fori_loop(0, group_size, head_body, 0)

    @pl.when(t == last)
    def _():
        causal = jnp.where(qp_ref[...] >= kp_ref[...], 0.0, NEG_INF).astype(jnp.float32)
        nkt = nkt_ref[...]
        nv_ext = with_ones(nv_ref[...])

        def new_body(h, carry):
            dense_fold(q_ref, h, nkt, nv_ext, causal, m_scr, acc_ref)
            return carry

        lax.fori_loop(0, group_size, new_body, 0)
        for h in range(group_size):
            acc = acc_ref[h]
            sum_out[:, h * DH : (h + 1) * DH] = acc[:, :DH].astype(sum_out.dtype)
            m_out[:, h : h + 1] = m_scr[h][:, :1]
            l_out[:, h : h + 1] = acc[:, DH : DH + 1]
        for c in local_copies():
            c.wait()
        for c in remote_copies():
            c.wait()


def attention_with_push(query_rows, keys_t, values, bias, new_keys_t, new_values, query_place, key_place, sends, n, per_dest, collective_id):
    rows, width = query_rows.shape
    group_size = width // DH
    total_keys = keys_t.shape[1]
    step_keys = TPB * TILE
    steps = total_keys // step_keys
    q_new = new_values.shape[0]
    any_spec = pl.BlockSpec(memory_space=pl.ANY)
    count = len(sends)
    recv_shapes = [
        jax.ShapeDtypeStruct((n,) + tuple(x.shape[1:] if d else x.shape), x.dtype)
        for x, d in zip(sends, per_dest)
    ]
    flops = 4 * rows * group_size * (total_keys + q_new) * DH
    cost = pl.CostEstimate(
        flops=flops,
        transcendentals=rows * group_size * (total_keys + q_new),
        bytes_accessed=rows * width * 4 + 2 * total_keys * DH * 2,
    )
    return pl.pallas_call(
        functools.partial(attn_push_kernel, n, group_size, per_dest, count),
        grid=(steps,),
        in_specs=[
            pl.BlockSpec((rows, width), lambda t: (0, 0)),
            pl.BlockSpec((DH, step_keys), lambda t: (0, t)),
            pl.BlockSpec((step_keys, DH), lambda t: (t, 0)),
            pl.BlockSpec((1, step_keys), lambda t: (0, t)),
            pl.BlockSpec((DH, q_new), lambda t: (0, 0)),
            pl.BlockSpec((q_new, DH), lambda t: (0, 0)),
            pl.BlockSpec((rows, 1), lambda t: (0, 0)),
            pl.BlockSpec((1, q_new), lambda t: (0, 0)),
        ]
        + [any_spec] * count,
        out_specs=[
            pl.BlockSpec((rows, width), lambda t: (0, 0)),
            pl.BlockSpec((rows, group_size), lambda t: (0, 0)),
            pl.BlockSpec((rows, group_size), lambda t: (0, 0)),
        ]
        + [any_spec] * count,
        out_shape=[
            jax.ShapeDtypeStruct((rows, width), jnp.bfloat16),
            jax.ShapeDtypeStruct((rows, group_size), jnp.float32),
            jax.ShapeDtypeStruct((rows, group_size), jnp.float32),
        ]
        + recv_shapes,
        scratch_shapes=[
            pltpu.VMEM((group_size, rows, DH), jnp.float32),
            pltpu.VMEM((group_size, rows, 2 * DH), jnp.float32),
            pltpu.SemaphoreType.DMA((count, n)),
            pltpu.SemaphoreType.DMA((count, n)),
            pltpu.SemaphoreType.DMA((count,)),
        ],
        compiler_params=pltpu.CompilerParams(
            collective_id=collective_id, has_side_effects=True, vmem_limit_bytes=56 * 1024 * 1024
        ),
        cost_estimate=cost,
    )(query_rows, keys_t, values, bias, new_keys_t, new_values, query_place, key_place, *sends)


def combine_kernel(heads, part_ref, fac_ref, den_ref, out_ref):
    senders = part_ref.shape[0]
    width = part_ref.shape[3]
    half = width // DH

    def sender_body(i, acc):
        fac = fac_ref[i]
        out = []
        for h in range(heads):
            j, c = divmod(h, half)
            blk = part_ref[i, j][:, c * DH : (c + 1) * DH].astype(jnp.float32)
            out.append(acc[h] + blk * fac[:, h : h + 1])
        return tuple(out)

    rows = out_ref.shape[0]
    start = tuple(jnp.zeros((rows, DH), jnp.float32) for _ in range(heads))
    acc = lax.fori_loop(0, senders, sender_body, start)
    den = den_ref[...]
    for h in range(heads):
        out_ref[:, h * DH : (h + 1) * DH] = (acc[h] / den[:, h : h + 1]).astype(out_ref.dtype)


def combine(part_sum, factor, denominator):
    senders, groups, rows, width = part_sum.shape
    heads = groups * width // DH
    vmem = pl.BlockSpec(memory_space=pltpu.VMEM)
    return pl.pallas_call(
        functools.partial(combine_kernel, heads),
        out_shape=jax.ShapeDtypeStruct((rows, heads * DH), jnp.bfloat16),
        in_specs=[vmem, vmem, vmem],
        out_specs=vmem,
        compiler_params=pltpu.CompilerParams(vmem_limit_bytes=32 * 1024 * 1024),
    )(part_sum, factor, denominator)


def body(
    queries,
    new_keys,
    new_values,
    cache_keys,
    cache_values,
    keep_tiles,
    tile_count,
    owner_slot,
    out_weight,
):
    q_dev = queries.shape[0]
    kv_local = new_keys.shape[1] // DH
    q_local = queries.shape[1] // DH
    group_size = q_local // kv_local
    ctx_count = lax.axis_size("ctx")
    tp_count = lax.axis_size("tp")
    total_rows = q_dev * ctx_count
    my_index = lax.axis_index("ctx")
    key_place = owner_slot[my_index] * q_dev + jnp.arange(q_dev, dtype=jnp.int32)
    pieces = 4
    piece_heads = q_local // pieces
    width = piece_heads * DH
    (q_blocks,) = push((queries[:, :width],), "ctx", ctx_count, False, 0)
    query_place = (
        owner_slot[:, None] * q_dev + jnp.arange(q_dev, dtype=jnp.int32)[None, :]
    ).reshape(total_rows, 1)
    key_place = key_place.reshape(1, q_dev)
    slots = keep_tiles.shape[2]
    slot_ids = jnp.arange(slots * TILE, dtype=jnp.int32) // TILE

    def dense_head(g):
        cols = slice(g * DH, (g + 1) * DH)
        tiles_k = cache_keys[:, cols].reshape(-1, TILE, DH)
        tiles_v = cache_values[:, cols].reshape(-1, TILE, DH)
        kept_k = jnp.take(tiles_k, keep_tiles[0, g], axis=0).reshape(slots * TILE, DH)
        kept_v = jnp.take(tiles_v, keep_tiles[0, g], axis=0).reshape(slots * TILE, DH)
        bias = jnp.where(slot_ids < tile_count[0, g], 0.0, NEG_INF).astype(jnp.float32)
        return kept_k.T, kept_v, bias.reshape(1, slots * TILE), new_keys[:, cols].T, new_values[:, cols]

    head_data = [dense_head(g) for g in range(kv_local)]
    coef = DH ** (-0.5) * LOG2E

    def combine_piece(parts):
        part_sum, part_max, part_total = parts
        top_max = jnp.max(part_max, axis=0)
        factor = jnp.exp2((part_max - top_max[None]) * coef)
        denominator = jnp.sum(part_total * factor, axis=0)
        return combine(part_sum[:, None], factor, denominator)

    attn_pieces = []
    attn_blocks = []
    previous = None
    for i in range(pieces):
        sends = []
        flags = []
        if i + 1 < pieces:
            sends.append(queries[:, (i + 1) * width : (i + 2) * width])
            flags.append(False)
        if previous is not None:
            sends.extend(previous)
            flags.extend([True, True, True])
        if i >= 3:
            sends.append(attn_pieces[i - 3])
            flags.append(False)
        outs = attention_with_push(
            q_blocks.reshape(total_rows, width),
            *head_data[i * kv_local // pieces],
            query_place,
            key_place,
            tuple(sends),
            ctx_count,
            tuple(flags),
            4 + i,
        )
        sums_i, maxima_i, totals_i = outs[:3]
        rest = list(outs[3:])
        if i + 1 < pieces:
            q_blocks = rest.pop(0)
        if previous is not None:
            got = (rest.pop(0), rest.pop(0), rest.pop(0))
            attn_pieces.append(combine_piece(got))
        if i >= 3:
            attn_blocks.append(rest.pop(0))
        previous = (
            sums_i.reshape(ctx_count, q_dev, width),
            maxima_i.reshape(ctx_count, q_dev, piece_heads),
            totals_i.reshape(ctx_count, q_dev, piece_heads),
        )
    last_parts = push(
        previous + tuple(attn_pieces[pieces - 3 :]),
        "ctx",
        ctx_count,
        (True, True, True, False, False),
        1,
    )
    attn_blocks.extend(last_parts[3:])
    attn_pieces.append(combine_piece(last_parts[:3]))
    attn_blocks.extend(push((attn_pieces[pieces - 1],), "ctx", ctx_count, False, 2))
    projected = None
    for j, blocks in enumerate(attn_blocks):
        term = jnp.dot(
            blocks.reshape(total_rows, width),
            out_weight[j * width : (j + 1) * width],
            preferred_element_type=jnp.float32,
        )
        projected = term if projected is None else projected + term
    out_rows = total_rows // tp_count
    (proj_parts,) = push(
        (projected.reshape(tp_count, out_rows, projected.shape[1]),), "tp", tp_count, True, 3
    )
    return jnp.sum(proj_parts, axis=0)


def solution(mesh):
    return jax.shard_map(
        body,
        mesh=mesh,
        in_specs=(
            P("ctx", "tp"),
            P("ctx", "tp"),
            P("ctx", "tp"),
            P("ctx", "tp"),
            P("ctx", "tp"),
            P("ctx", "tp", None),
            P("ctx", "tp"),
            P(),
            P("tp", "ctx"),
        ),
        out_specs=P("tp", "ctx"),
        check_vma=False,
    )
```

```python
import functools

import jax
import jax.numpy as jnp
from jax import lax
from jax.experimental import pallas as pl
from jax.experimental.pallas import tpu as pltpu
from jax.sharding import PartitionSpec as P

DH = 128
TILE = 128
TB = 4
MESH = pl.DeviceIdType.MESH

NEG_INF = -jnp.inf


def push_kernel(axis, n, per_dest, count, *refs):
    x_refs = refs[:count]
    y_refs = refs[count : 2 * count]
    send_sem, recv_sem, local_sem = refs[2 * count :]
    me = lax.axis_index(axis)
    barrier = pltpu.get_barrier_semaphore()
    for k in range(1, n):
        peer = lax.rem(me + k, n)
        pl.semaphore_signal(barrier, inc=1, device_id={axis: peer}, device_id_type=MESH)
    pl.semaphore_wait(barrier, n - 1)
    copies = []
    for a in range(count):
        for k in range(1, n):
            peer = lax.rem(me + k, n)
            src = x_refs[a].at[peer] if per_dest else x_refs[a]
            copy = pltpu.make_async_remote_copy(
                src_ref=src,
                dst_ref=y_refs[a].at[me],
                send_sem=send_sem.at[a, k],
                recv_sem=recv_sem.at[a, k],
                device_id={axis: peer},
                device_id_type=MESH,
            )
            copy.start()
            copies.append(copy)
    locals_ = []
    for a in range(count):
        src = x_refs[a].at[me] if per_dest else x_refs[a]
        local = pltpu.make_async_copy(src, y_refs[a].at[me], local_sem.at[a])
        local.start()
        locals_.append(local)
    for local in locals_:
        local.wait()
    for copy in copies:
        copy.wait()


def push(xs, axis, n, per_dest, collective_id):
    count = len(xs)
    out_shape = []
    for x in xs:
        block = x.shape[1:] if per_dest else x.shape
        out_shape.append(jax.ShapeDtypeStruct((n,) + tuple(block), x.dtype))
    any_spec = pl.BlockSpec(memory_space=pl.ANY)
    return pl.pallas_call(
        functools.partial(push_kernel, axis, n, per_dest, count),
        out_shape=tuple(out_shape),
        in_specs=[any_spec] * count,
        out_specs=tuple([any_spec] * count),
        scratch_shapes=[
            pltpu.SemaphoreType.DMA((count, n)),
            pltpu.SemaphoreType.DMA((count, n)),
            pltpu.SemaphoreType.DMA((count,)),
        ],
        compiler_params=pltpu.CompilerParams(collective_id=collective_id, has_side_effects=True),
    )(*xs)


TPB = 8
LOG2E = 1.4426950408889634


def dot_nt(a, b):
    return jnp.dot(a, b, preferred_element_type=jnp.float32)


def attn_kernel(tpb, group_size, kt_ref, cnt_ref, q_ref, *refs):
    k_refs = refs[:tpb]
    v_refs = refs[tpb : 2 * tpb]
    nk_ref, nv_ref, qp_ref, kp_ref = refs[2 * tpb : 2 * tpb + 4]
    sum_out, m_out, l_out = refs[2 * tpb + 4 : 2 * tpb + 7]
    m_scr, acc_ref = refs[2 * tpb + 7 :]
    g = pl.program_id(0)
    t = pl.program_id(1)
    last = pl.num_programs(1) - 1
    live = cnt_ref[g]
    coef = DH ** (-0.5) * LOG2E

    @pl.when(t == 0)
    def _():
        m_scr[...] = jnp.full(m_scr.shape, NEG_INF, jnp.float32)
        acc_ref[...] = jnp.zeros(acc_ref.shape, jnp.float32)

    def fold(h, keys, values_ext, mask):
        cols = pl.ds(pl.multiple_of(h * DH, DH), DH)
        s = dot_nt(q_ref[:, cols], keys)
        if mask is not None:
            s = s + mask
        m_prev = m_scr[h]
        m_new = jnp.maximum(m_prev, s.max(axis=1, keepdims=True))
        alpha = jnp.exp2((m_prev - m_new) * coef)
        p = jnp.exp2(s * coef - m_new[:, :1] * coef)
        m_scr[h] = m_new
        acc_ref[h] = acc_ref[h] * alpha[:, :1] + jnp.dot(
            p.astype(jnp.bfloat16), values_ext, preferred_element_type=jnp.float32
        )

    def with_ones(values):
        return jnp.concatenate([values, jnp.ones(values.shape, values.dtype)], axis=1)

    def tiles_step(masked):
        keys = jnp.concatenate([k[...] for k in k_refs], axis=1)
        values_ext = with_ones(jnp.concatenate([v[...] for v in v_refs], axis=0))
        mask = None
        if masked:
            slot = t * tpb + lax.broadcasted_iota(jnp.int32, (1, tpb * TILE), 1) // TILE
            mask = jnp.where(slot < live, 0.0, NEG_INF).astype(jnp.float32)

        def head_body(h, carry):
            fold(h, keys, values_ext, mask)
            return carry

        lax.fori_loop(0, group_size, head_body, 0)

    @pl.when((t + 1) * tpb <= live)
    def _():
        tiles_step(False)

    @pl.when(jnp.logical_and(t * tpb < live, (t + 1) * tpb > live))
    def _():
        tiles_step(True)

    @pl.when(t == last)
    def _():
        causal = jnp.where(qp_ref[...] >= kp_ref[...], 0.0, NEG_INF).astype(jnp.float32)
        nk = nk_ref[...]
        nv_ext = with_ones(nv_ref[...])

        def head_body(h, carry):
            fold(h, nk, nv_ext, causal)
            return carry

        lax.fori_loop(0, group_size, head_body, 0)
        for h in range(group_size):
            acc = acc_ref[h]
            sum_out[:, h * DH : (h + 1) * DH] = acc[:, :DH].astype(sum_out.dtype)
            m_out[:, h : h + 1] = m_scr[h][:, :1]
            l_out[:, h : h + 1] = acc[:, DH : DH + 1]


def local_attention(query_rows, cache_keys, cache_values, new_keys, new_values, keep, live, query_place, key_place):
    rows, width = query_rows.shape
    kv_local = new_keys.shape[1] // DH
    group_size = width // DH // kv_local
    slots = keep.shape[1]
    steps = slots // TPB
    q_new = new_keys.shape[0]

    def tile_map(j):
        def index_map(g, t, kt_ref, cnt_ref):
            return (kt_ref[g, jnp.minimum(t * TPB + j, cnt_ref[g] - 1)], g)

        return index_map

    tile_spec = [pl.BlockSpec((TILE, DH), tile_map(j)) for j in range(TPB)]

    def tile_map_t(j):
        def index_map(g, t, kt_ref, cnt_ref):
            return (g, kt_ref[g, jnp.minimum(t * TPB + j, cnt_ref[g] - 1)])

        return index_map

    tile_spec_t = [pl.BlockSpec((DH, TILE), tile_map_t(j)) for j in range(TPB)]
    grid_spec = pltpu.PrefetchScalarGridSpec(
        num_scalar_prefetch=2,
        grid=(kv_local, steps),
        in_specs=[pl.BlockSpec((rows, group_size * DH), lambda g, t, kt, cn: (0, g))]
        + tile_spec_t
        + tile_spec
        + [
            pl.BlockSpec((DH, q_new), lambda g, t, kt, cn: (g, 0)),
            pl.BlockSpec((q_new, DH), lambda g, t, kt, cn: (0, g)),
            pl.BlockSpec((rows, 1), lambda g, t, kt, cn: (0, 0)),
            pl.BlockSpec((1, q_new), lambda g, t, kt, cn: (0, 0)),
        ],
        out_specs=[
            pl.BlockSpec((rows, group_size * DH), lambda g, t, kt, cn: (0, g)),
            pl.BlockSpec((None, rows, group_size), lambda g, t, kt, cn: (g, 0, 0)),
            pl.BlockSpec((None, rows, group_size), lambda g, t, kt, cn: (g, 0, 0)),
        ],
        scratch_shapes=[
            pltpu.VMEM((group_size, rows, DH), jnp.float32),
            pltpu.VMEM((group_size, rows, 2 * DH), jnp.float32),
        ],
    )
    keys_total = slots * TILE + q_new
    flops = 4 * rows * kv_local * group_size * keys_total * DH
    cost = pl.CostEstimate(
        flops=flops,
        transcendentals=rows * kv_local * group_size * keys_total,
        bytes_accessed=rows * width * 2 + rows * width * 4 + 2 * kv_local * slots * TILE * DH * 2,
    )
    return pl.pallas_call(
        functools.partial(attn_kernel, TPB, group_size),
        grid_spec=grid_spec,
        out_shape=[
            jax.ShapeDtypeStruct((rows, width), jnp.bfloat16),
            jax.ShapeDtypeStruct((kv_local, rows, group_size), jnp.float32),
            jax.ShapeDtypeStruct((kv_local, rows, group_size), jnp.float32),
        ],
        compiler_params=pltpu.CompilerParams(
            dimension_semantics=("arbitrary", "arbitrary"), vmem_limit_bytes=56 * 1024 * 1024
        ),
        cost_estimate=cost,
    )(keep, live, query_rows, *([cache_keys.T] * TPB), *([cache_values] * TPB), new_keys.T, new_values, query_place, key_place)


def dense_fold(q_ref, h, keys_t, values_ext, mask, m_scr, acc_ref):
    coef = DH ** (-0.5) * LOG2E
    cols = pl.ds(pl.multiple_of(h * DH, DH), DH)
    s = jnp.dot(q_ref[:, cols], keys_t, preferred_element_type=jnp.float32) + mask
    m_prev = m_scr[h]
    m_new = jnp.maximum(m_prev, s.max(axis=1, keepdims=True))
    alpha = jnp.exp2((m_prev - m_new) * coef)
    p = jnp.exp2(s * coef - m_new[:, :1] * coef)
    m_scr[h] = m_new
    acc_ref[h] = acc_ref[h] * alpha[:, :1] + jnp.dot(
        p.astype(jnp.bfloat16), values_ext, preferred_element_type=jnp.float32
    )


def attn_push_kernel(n, group_size, per_dest, count, *refs):
    q_ref, kt_ref, v_ref, bias_ref, nkt_ref, nv_ref, qp_ref, kp_ref = refs[:8]
    srcs = refs[8 : 8 + count]
    sum_out, m_out, l_out = refs[8 + count : 11 + count]
    dsts = refs[11 + count : 11 + 2 * count]
    m_scr, acc_ref, send_sem, recv_sem, local_sem = refs[11 + 2 * count :]
    t = pl.program_id(0)
    last = pl.num_programs(0) - 1
    me = lax.axis_index("ctx")

    def remote_copies():
        out = []
        for a in range(count):
            for k in range(1, n):
                peer = lax.rem(me + k, n)
                out.append(
                    pltpu.make_async_remote_copy(
                        src_ref=srcs[a].at[peer] if per_dest[a] else srcs[a],
                        dst_ref=dsts[a].at[me],
                        send_sem=send_sem.at[a, k],
                        recv_sem=recv_sem.at[a, k],
                        device_id={"ctx": peer},
                        device_id_type=MESH,
                    )
                )
        return out

    def local_copies():
        return [
            pltpu.make_async_copy(
                srcs[a].at[me] if per_dest[a] else srcs[a], dsts[a].at[me], local_sem.at[a]
            )
            for a in range(count)
        ]

    def with_ones(values):
        return jnp.concatenate([values, jnp.ones(values.shape, values.dtype)], axis=1)

    @pl.when(t == 0)
    def _():
        barrier = pltpu.get_barrier_semaphore()
        for k in range(1, n):
            peer = lax.rem(me + k, n)
            pl.semaphore_signal(barrier, inc=1, device_id={"ctx": peer}, device_id_type=MESH)
        pl.semaphore_wait(barrier, n - 1)
        for c in remote_copies():
            c.start()
        for c in local_copies():
            c.start()
        m_scr[...] = jnp.full(m_scr.shape, NEG_INF, jnp.float32)
        acc_ref[...] = jnp.zeros(acc_ref.shape, jnp.float32)

    keys_t = kt_ref[...]
    values_ext = with_ones(v_ref[...])
    mask = bias_ref[...]

    def head_body(h, carry):
        dense_fold(q_ref, h, keys_t, values_ext, mask, m_scr, acc_ref)
        return carry

    lax.fori_loop(0, group_size, head_body, 0)

    @pl.when(t == last)
    def _():
        causal = jnp.where(qp_ref[...] >= kp_ref[...], 0.0, NEG_INF).astype(jnp.float32)
        nkt = nkt_ref[...]
        nv_ext = with_ones(nv_ref[...])

        def new_body(h, carry):
            dense_fold(q_ref, h, nkt, nv_ext, causal, m_scr, acc_ref)
            return carry

        lax.fori_loop(0, group_size, new_body, 0)
        for h in range(group_size):
            acc = acc_ref[h]
            sum_out[:, h * DH : (h + 1) * DH] = acc[:, :DH].astype(sum_out.dtype)
            m_out[:, h : h + 1] = m_scr[h][:, :1]
            l_out[:, h : h + 1] = acc[:, DH : DH + 1]
        for c in local_copies():
            c.wait()
        for c in remote_copies():
            c.wait()


def attention_with_push(query_rows, keys_t, values, bias, new_keys_t, new_values, query_place, key_place, sends, n, per_dest, collective_id):
    rows, width = query_rows.shape
    group_size = width // DH
    total_keys = keys_t.shape[1]
    step_keys = total_keys
    steps = total_keys // step_keys
    q_new = new_values.shape[0]
    any_spec = pl.BlockSpec(memory_space=pl.ANY)
    count = len(sends)
    recv_shapes = [
        jax.ShapeDtypeStruct((n,) + tuple(x.shape[1:] if d else x.shape), x.dtype)
        for x, d in zip(sends, per_dest)
    ]
    flops = 4 * rows * group_size * (total_keys + q_new) * DH
    cost = pl.CostEstimate(
        flops=flops,
        transcendentals=rows * group_size * (total_keys + q_new),
        bytes_accessed=rows * width * 4 + 2 * total_keys * DH * 2,
    )
    return pl.pallas_call(
        functools.partial(attn_push_kernel, n, group_size, per_dest, count),
        grid=(steps,),
        in_specs=[
            pl.BlockSpec((rows, width), lambda t: (0, 0)),
            pl.BlockSpec((DH, step_keys), lambda t: (0, t)),
            pl.BlockSpec((step_keys, DH), lambda t: (t, 0)),
            pl.BlockSpec((1, step_keys), lambda t: (0, t)),
            pl.BlockSpec((DH, q_new), lambda t: (0, 0)),
            pl.BlockSpec((q_new, DH), lambda t: (0, 0)),
            pl.BlockSpec((rows, 1), lambda t: (0, 0)),
            pl.BlockSpec((1, q_new), lambda t: (0, 0)),
        ]
        + [any_spec] * count,
        out_specs=[
            pl.BlockSpec((rows, width), lambda t: (0, 0)),
            pl.BlockSpec((rows, group_size), lambda t: (0, 0)),
            pl.BlockSpec((rows, group_size), lambda t: (0, 0)),
        ]
        + [any_spec] * count,
        out_shape=[
            jax.ShapeDtypeStruct((rows, width), jnp.bfloat16),
            jax.ShapeDtypeStruct((rows, group_size), jnp.float32),
            jax.ShapeDtypeStruct((rows, group_size), jnp.float32),
        ]
        + recv_shapes,
        scratch_shapes=[
            pltpu.VMEM((group_size, rows, DH), jnp.float32),
            pltpu.VMEM((group_size, rows, 2 * DH), jnp.float32),
            pltpu.SemaphoreType.DMA((count, n)),
            pltpu.SemaphoreType.DMA((count, n)),
            pltpu.SemaphoreType.DMA((count,)),
        ],
        compiler_params=pltpu.CompilerParams(
            collective_id=collective_id, has_side_effects=True, vmem_limit_bytes=56 * 1024 * 1024
        ),
        cost_estimate=cost,
    )(query_rows, keys_t, values, bias, new_keys_t, new_values, query_place, key_place, *sends)


def combine_kernel(heads, part_ref, fac_ref, den_ref, out_ref):
    senders = part_ref.shape[0]
    width = part_ref.shape[3]
    half = width // DH

    def sender_body(i, acc):
        fac = fac_ref[i]
        out = []
        for h in range(heads):
            j, c = divmod(h, half)
            blk = part_ref[i, j][:, c * DH : (c + 1) * DH].astype(jnp.float32)
            out.append(acc[h] + blk * fac[:, h : h + 1])
        return tuple(out)

    rows = out_ref.shape[0]
    start = tuple(jnp.zeros((rows, DH), jnp.float32) for _ in range(heads))
    acc = lax.fori_loop(0, senders, sender_body, start)
    den = den_ref[...]
    for h in range(heads):
        out_ref[:, h * DH : (h + 1) * DH] = (acc[h] / den[:, h : h + 1]).astype(out_ref.dtype)


def combine(part_sum, factor, denominator):
    senders, groups, rows, width = part_sum.shape
    heads = groups * width // DH
    vmem = pl.BlockSpec(memory_space=pltpu.VMEM)
    return pl.pallas_call(
        functools.partial(combine_kernel, heads),
        out_shape=jax.ShapeDtypeStruct((rows, heads * DH), jnp.bfloat16),
        in_specs=[vmem, vmem, vmem],
        out_specs=vmem,
        compiler_params=pltpu.CompilerParams(vmem_limit_bytes=32 * 1024 * 1024),
    )(part_sum, factor, denominator)


def body(
    queries,
    new_keys,
    new_values,
    cache_keys,
    cache_values,
    keep_tiles,
    tile_count,
    owner_slot,
    out_weight,
):
    q_dev = queries.shape[0]
    kv_local = new_keys.shape[1] // DH
    q_local = queries.shape[1] // DH
    group_size = q_local // kv_local
    ctx_count = lax.axis_size("ctx")
    tp_count = lax.axis_size("tp")
    total_rows = q_dev * ctx_count
    my_index = lax.axis_index("ctx")
    key_place = owner_slot[my_index] * q_dev + jnp.arange(q_dev, dtype=jnp.int32)
    pieces = 4
    piece_heads = q_local // pieces
    width = piece_heads * DH
    (q_blocks,) = push((queries[:, :width],), "ctx", ctx_count, False, 0)
    query_place = (
        owner_slot[:, None] * q_dev + jnp.arange(q_dev, dtype=jnp.int32)[None, :]
    ).reshape(total_rows, 1)
    key_place = key_place.reshape(1, q_dev)
    slots = keep_tiles.shape[2]
    slot_ids = jnp.arange(slots * TILE, dtype=jnp.int32) // TILE

    def dense_head(g):
        cols = slice(g * DH, (g + 1) * DH)
        tiles_k = cache_keys[:, cols].reshape(-1, TILE, DH)
        tiles_v = cache_values[:, cols].reshape(-1, TILE, DH)
        kept_k = jnp.take(tiles_k, keep_tiles[0, g], axis=0).reshape(slots * TILE, DH)
        kept_v = jnp.take(tiles_v, keep_tiles[0, g], axis=0).reshape(slots * TILE, DH)
        bias = jnp.where(slot_ids < tile_count[0, g], 0.0, NEG_INF).astype(jnp.float32)
        return kept_k.T, kept_v, bias.reshape(1, slots * TILE), new_keys[:, cols].T, new_values[:, cols]

    head_data = [dense_head(g) for g in range(kv_local)]
    coef = DH ** (-0.5) * LOG2E

    def combine_piece(parts):
        part_sum, part_max, part_total = parts
        top_max = jnp.max(part_max, axis=0)
        factor = jnp.exp2((part_max - top_max[None]) * coef)
        denominator = jnp.sum(part_total * factor, axis=0)
        return combine(part_sum[:, None], factor, denominator)

    attn_pieces = []
    attn_blocks = []
    previous = None
    for i in range(pieces):
        sends = []
        flags = []
        if i + 1 < pieces:
            sends.append(queries[:, (i + 1) * width : (i + 2) * width])
            flags.append(False)
        if previous is not None:
            sends.extend(previous)
            flags.extend([True, True, True])
        if i >= 2:
            sends.append(attn_pieces[i - 2])
            flags.append(False)
        outs = attention_with_push(
            q_blocks.reshape(total_rows, width),
            *head_data[i * kv_local // pieces],
            query_place,
            key_place,
            tuple(sends),
            ctx_count,
            tuple(flags),
            4 + i,
        )
        sums_i, maxima_i, totals_i = outs[:3]
        rest = list(outs[3:])
        if i + 1 < pieces:
            q_blocks = rest.pop(0)
        if previous is not None:
            got = (rest.pop(0), rest.pop(0), rest.pop(0))
            attn_pieces.append(combine_piece(got))
        if i >= 2:
            attn_blocks.append(rest.pop(0))
        previous = (
            sums_i.reshape(ctx_count, q_dev, width),
            maxima_i.reshape(ctx_count, q_dev, piece_heads),
            totals_i.reshape(ctx_count, q_dev, piece_heads),
        )
    attn_pieces.append(combine_piece(push(previous, "ctx", ctx_count, True, 1)))
    attn_blocks.extend(push(tuple(attn_pieces[pieces - 2 :]), "ctx", ctx_count, False, 2))
    projected = None
    for j, blocks in enumerate(attn_blocks):
        term = jnp.dot(
            blocks.reshape(total_rows, width),
            out_weight[j * width : (j + 1) * width],
            preferred_element_type=jnp.float32,
        )
        projected = term if projected is None else projected + term
    out_rows = total_rows // tp_count
    (proj_parts,) = push(
        (projected.reshape(tp_count, out_rows, projected.shape[1]),), "tp", tp_count, True, 3
    )
    return jnp.sum(proj_parts, axis=0)


def solution(mesh):
    return jax.shard_map(
        body,
        mesh=mesh,
        in_specs=(
            P("ctx", "tp"),
            P("ctx", "tp"),
            P("ctx", "tp"),
            P("ctx", "tp"),
            P("ctx", "tp"),
            P("ctx", "tp", None),
            P("ctx", "tp"),
            P(),
            P("tp", "ctx"),
        ),
        out_specs=P("tp", "ctx"),
        check_vma=False,
    )
```

```python
import functools

import jax
import jax.numpy as jnp
from jax import lax
from jax.experimental import pallas as pl
from jax.experimental.pallas import tpu as pltpu
from jax.sharding import PartitionSpec as P

DH = 128
TILE = 128
TB = 4
MESH = pl.DeviceIdType.MESH

NEG_INF = -jnp.inf


def push_kernel(axis, n, per_dest, count, *refs):
    x_refs = refs[:count]
    y_refs = refs[count : 2 * count]
    send_sem, recv_sem, local_sem = refs[2 * count :]
    me = lax.axis_index(axis)
    barrier = pltpu.get_barrier_semaphore()
    for k in range(1, n):
        peer = lax.rem(me + k, n)
        pl.semaphore_signal(barrier, inc=1, device_id={axis: peer}, device_id_type=MESH)
    pl.semaphore_wait(barrier, n - 1)
    copies = []
    for a in range(count):
        for k in range(1, n):
            peer = lax.rem(me + k, n)
            src = x_refs[a].at[peer] if per_dest else x_refs[a]
            copy = pltpu.make_async_remote_copy(
                src_ref=src,
                dst_ref=y_refs[a].at[me],
                send_sem=send_sem.at[a, k],
                recv_sem=recv_sem.at[a, k],
                device_id={axis: peer},
                device_id_type=MESH,
            )
            copy.start()
            copies.append(copy)
    locals_ = []
    for a in range(count):
        src = x_refs[a].at[me] if per_dest else x_refs[a]
        local = pltpu.make_async_copy(src, y_refs[a].at[me], local_sem.at[a])
        local.start()
        locals_.append(local)
    for local in locals_:
        local.wait()
    for copy in copies:
        copy.wait()


def push(xs, axis, n, per_dest, collective_id):
    count = len(xs)
    out_shape = []
    for x in xs:
        block = x.shape[1:] if per_dest else x.shape
        out_shape.append(jax.ShapeDtypeStruct((n,) + tuple(block), x.dtype))
    any_spec = pl.BlockSpec(memory_space=pl.ANY)
    return pl.pallas_call(
        functools.partial(push_kernel, axis, n, per_dest, count),
        out_shape=tuple(out_shape),
        in_specs=[any_spec] * count,
        out_specs=tuple([any_spec] * count),
        scratch_shapes=[
            pltpu.SemaphoreType.DMA((count, n)),
            pltpu.SemaphoreType.DMA((count, n)),
            pltpu.SemaphoreType.DMA((count,)),
        ],
        compiler_params=pltpu.CompilerParams(collective_id=collective_id, has_side_effects=True),
    )(*xs)


TPB = 8
LOG2E = 1.4426950408889634


def dot_nt(a, b):
    return jnp.dot(a, b, preferred_element_type=jnp.float32)


def attn_kernel(tpb, group_size, kt_ref, cnt_ref, q_ref, *refs):
    k_refs = refs[:tpb]
    v_refs = refs[tpb : 2 * tpb]
    nk_ref, nv_ref, qp_ref, kp_ref = refs[2 * tpb : 2 * tpb + 4]
    sum_out, m_out, l_out = refs[2 * tpb + 4 : 2 * tpb + 7]
    m_scr, acc_ref = refs[2 * tpb + 7 :]
    g = pl.program_id(0)
    t = pl.program_id(1)
    last = pl.num_programs(1) - 1
    live = cnt_ref[g]
    coef = DH ** (-0.5) * LOG2E

    @pl.when(t == 0)
    def _():
        m_scr[...] = jnp.full(m_scr.shape, NEG_INF, jnp.float32)
        acc_ref[...] = jnp.zeros(acc_ref.shape, jnp.float32)

    def fold(h, keys, values_ext, mask):
        cols = pl.ds(pl.multiple_of(h * DH, DH), DH)
        s = dot_nt(q_ref[:, cols], keys)
        if mask is not None:
            s = s + mask
        m_prev = m_scr[h]
        m_new = jnp.maximum(m_prev, s.max(axis=1, keepdims=True))
        alpha = jnp.exp2((m_prev - m_new) * coef)
        p = jnp.exp2(s * coef - m_new[:, :1] * coef)
        m_scr[h] = m_new
        acc_ref[h] = acc_ref[h] * alpha[:, :1] + jnp.dot(
            p.astype(jnp.bfloat16), values_ext, preferred_element_type=jnp.float32
        )

    def with_ones(values):
        return jnp.concatenate([values, jnp.ones(values.shape, values.dtype)], axis=1)

    def tiles_step(masked):
        keys = jnp.concatenate([k[...] for k in k_refs], axis=1)
        values_ext = with_ones(jnp.concatenate([v[...] for v in v_refs], axis=0))
        mask = None
        if masked:
            slot = t * tpb + lax.broadcasted_iota(jnp.int32, (1, tpb * TILE), 1) // TILE
            mask = jnp.where(slot < live, 0.0, NEG_INF).astype(jnp.float32)

        def head_body(h, carry):
            fold(h, keys, values_ext, mask)
            return carry

        lax.fori_loop(0, group_size, head_body, 0)

    @pl.when((t + 1) * tpb <= live)
    def _():
        tiles_step(False)

    @pl.when(jnp.logical_and(t * tpb < live, (t + 1) * tpb > live))
    def _():
        tiles_step(True)

    @pl.when(t == last)
    def _():
        causal = jnp.where(qp_ref[...] >= kp_ref[...], 0.0, NEG_INF).astype(jnp.float32)
        nk = nk_ref[...]
        nv_ext = with_ones(nv_ref[...])

        def head_body(h, carry):
            fold(h, nk, nv_ext, causal)
            return carry

        lax.fori_loop(0, group_size, head_body, 0)
        for h in range(group_size):
            acc = acc_ref[h]
            sum_out[:, h * DH : (h + 1) * DH] = acc[:, :DH].astype(sum_out.dtype)
            m_out[:, h : h + 1] = m_scr[h][:, :1]
            l_out[:, h : h + 1] = acc[:, DH : DH + 1]


def local_attention(query_rows, cache_keys, cache_values, new_keys, new_values, keep, live, query_place, key_place):
    rows, width = query_rows.shape
    kv_local = new_keys.shape[1] // DH
    group_size = width // DH // kv_local
    slots = keep.shape[1]
    steps = slots // TPB
    q_new = new_keys.shape[0]

    def tile_map(j):
        def index_map(g, t, kt_ref, cnt_ref):
            return (kt_ref[g, jnp.minimum(t * TPB + j, cnt_ref[g] - 1)], g)

        return index_map

    tile_spec = [pl.BlockSpec((TILE, DH), tile_map(j)) for j in range(TPB)]

    def tile_map_t(j):
        def index_map(g, t, kt_ref, cnt_ref):
            return (g, kt_ref[g, jnp.minimum(t * TPB + j, cnt_ref[g] - 1)])

        return index_map

    tile_spec_t = [pl.BlockSpec((DH, TILE), tile_map_t(j)) for j in range(TPB)]
    grid_spec = pltpu.PrefetchScalarGridSpec(
        num_scalar_prefetch=2,
        grid=(kv_local, steps),
        in_specs=[pl.BlockSpec((rows, group_size * DH), lambda g, t, kt, cn: (0, g))]
        + tile_spec_t
        + tile_spec
        + [
            pl.BlockSpec((DH, q_new), lambda g, t, kt, cn: (g, 0)),
            pl.BlockSpec((q_new, DH), lambda g, t, kt, cn: (0, g)),
            pl.BlockSpec((rows, 1), lambda g, t, kt, cn: (0, 0)),
            pl.BlockSpec((1, q_new), lambda g, t, kt, cn: (0, 0)),
        ],
        out_specs=[
            pl.BlockSpec((rows, group_size * DH), lambda g, t, kt, cn: (0, g)),
            pl.BlockSpec((None, rows, group_size), lambda g, t, kt, cn: (g, 0, 0)),
            pl.BlockSpec((None, rows, group_size), lambda g, t, kt, cn: (g, 0, 0)),
        ],
        scratch_shapes=[
            pltpu.VMEM((group_size, rows, DH), jnp.float32),
            pltpu.VMEM((group_size, rows, 2 * DH), jnp.float32),
        ],
    )
    keys_total = slots * TILE + q_new
    flops = 4 * rows * kv_local * group_size * keys_total * DH
    cost = pl.CostEstimate(
        flops=flops,
        transcendentals=rows * kv_local * group_size * keys_total,
        bytes_accessed=rows * width * 2 + rows * width * 4 + 2 * kv_local * slots * TILE * DH * 2,
    )
    return pl.pallas_call(
        functools.partial(attn_kernel, TPB, group_size),
        grid_spec=grid_spec,
        out_shape=[
            jax.ShapeDtypeStruct((rows, width), jnp.bfloat16),
            jax.ShapeDtypeStruct((kv_local, rows, group_size), jnp.float32),
            jax.ShapeDtypeStruct((kv_local, rows, group_size), jnp.float32),
        ],
        compiler_params=pltpu.CompilerParams(
            dimension_semantics=("arbitrary", "arbitrary"), vmem_limit_bytes=56 * 1024 * 1024
        ),
        cost_estimate=cost,
    )(keep, live, query_rows, *([cache_keys.T] * TPB), *([cache_values] * TPB), new_keys.T, new_values, query_place, key_place)


def dense_fold(q_ref, h, keys_t, values_ext, mask, m_scr, acc_ref):
    coef = DH ** (-0.5) * LOG2E
    cols = pl.ds(pl.multiple_of(h * DH, DH), DH)
    s = jnp.dot(q_ref[:, cols], keys_t, preferred_element_type=jnp.float32) + mask
    m_prev = m_scr[h]
    m_new = jnp.maximum(m_prev, s.max(axis=1, keepdims=True))
    alpha = jnp.exp2((m_prev - m_new) * coef)
    p = jnp.exp2(s * coef - m_new[:, :1] * coef)
    m_scr[h] = m_new
    acc_ref[h] = acc_ref[h] * alpha[:, :1] + jnp.dot(
        p.astype(jnp.bfloat16), values_ext, preferred_element_type=jnp.float32
    )


def attn_push_kernel(n, group_size, per_dest, count, *refs):
    q_ref, kt_ref, v_ref, bias_ref, nkt_ref, nv_ref, qp_ref, kp_ref = refs[:8]
    srcs = refs[8 : 8 + count]
    sum_out, m_out, l_out = refs[8 + count : 11 + count]
    dsts = refs[11 + count : 11 + 2 * count]
    m_scr, acc_ref, send_sem, recv_sem, local_sem = refs[11 + 2 * count :]
    t = pl.program_id(0)
    last = pl.num_programs(0) - 1
    me = lax.axis_index("ctx")

    def remote_copies():
        out = []
        for a in range(count):
            for k in range(1, n):
                peer = lax.rem(me + k, n)
                out.append(
                    pltpu.make_async_remote_copy(
                        src_ref=srcs[a].at[peer] if per_dest[a] else srcs[a],
                        dst_ref=dsts[a].at[me],
                        send_sem=send_sem.at[a, k],
                        recv_sem=recv_sem.at[a, k],
                        device_id={"ctx": peer},
                        device_id_type=MESH,
                    )
                )
        return out

    def local_copies():
        return [
            pltpu.make_async_copy(
                srcs[a].at[me] if per_dest[a] else srcs[a], dsts[a].at[me], local_sem.at[a]
            )
            for a in range(count)
        ]

    def with_ones(values):
        return jnp.concatenate([values, jnp.ones(values.shape, values.dtype)], axis=1)

    @pl.when(t == 0)
    def _():
        barrier = pltpu.get_barrier_semaphore()
        for k in range(1, n):
            peer = lax.rem(me + k, n)
            pl.semaphore_signal(barrier, inc=1, device_id={"ctx": peer}, device_id_type=MESH)
        pl.semaphore_wait(barrier, n - 1)
        for c in remote_copies():
            c.start()
        for c in local_copies():
            c.start()
        m_scr[...] = jnp.full(m_scr.shape, NEG_INF, jnp.float32)
        acc_ref[...] = jnp.zeros(acc_ref.shape, jnp.float32)

    keys_t = kt_ref[...]
    values_ext = with_ones(v_ref[...])
    mask = bias_ref[...]

    def head_body(h, carry):
        dense_fold(q_ref, h, keys_t, values_ext, mask, m_scr, acc_ref)
        return carry

    lax.fori_loop(0, group_size, head_body, 0)

    @pl.when(t == last)
    def _():
        causal = jnp.where(qp_ref[...] >= kp_ref[...], 0.0, NEG_INF).astype(jnp.float32)
        nkt = nkt_ref[...]
        nv_ext = with_ones(nv_ref[...])

        def new_body(h, carry):
            dense_fold(q_ref, h, nkt, nv_ext, causal, m_scr, acc_ref)
            return carry

        lax.fori_loop(0, group_size, new_body, 0)
        for h in range(group_size):
            acc = acc_ref[h]
            sum_out[:, h * DH : (h + 1) * DH] = acc[:, :DH].astype(sum_out.dtype)
            m_out[:, h : h + 1] = m_scr[h][:, :1]
            l_out[:, h : h + 1] = acc[:, DH : DH + 1]
        for c in local_copies():
            c.wait()
        for c in remote_copies():
            c.wait()


def attention_with_push(query_rows, keys_t, values, bias, new_keys_t, new_values, query_place, key_place, sends, n, per_dest, collective_id):
    rows, width = query_rows.shape
    group_size = width // DH
    total_keys = keys_t.shape[1]
    step_keys = TPB * TILE
    steps = total_keys // step_keys
    q_new = new_values.shape[0]
    any_spec = pl.BlockSpec(memory_space=pl.ANY)
    count = len(sends)
    recv_shapes = [
        jax.ShapeDtypeStruct((n,) + tuple(x.shape[1:] if d else x.shape), x.dtype)
        for x, d in zip(sends, per_dest)
    ]
    flops = 4 * rows * group_size * (total_keys + q_new) * DH
    cost = pl.CostEstimate(
        flops=flops,
        transcendentals=rows * group_size * (total_keys + q_new),
        bytes_accessed=rows * width * 4 + 2 * total_keys * DH * 2,
    )
    return pl.pallas_call(
        functools.partial(attn_push_kernel, n, group_size, per_dest, count),
        grid=(steps,),
        in_specs=[
            pl.BlockSpec((rows, width), lambda t: (0, 0)),
            pl.BlockSpec((DH, step_keys), lambda t: (0, t)),
            pl.BlockSpec((step_keys, DH), lambda t: (t, 0)),
            pl.BlockSpec((1, step_keys), lambda t: (0, t)),
            pl.BlockSpec((DH, q_new), lambda t: (0, 0)),
            pl.BlockSpec((q_new, DH), lambda t: (0, 0)),
            pl.BlockSpec((rows, 1), lambda t: (0, 0)),
            pl.BlockSpec((1, q_new), lambda t: (0, 0)),
        ]
        + [any_spec] * count,
        out_specs=[
            pl.BlockSpec((rows, width), lambda t: (0, 0)),
            pl.BlockSpec((rows, group_size), lambda t: (0, 0)),
            pl.BlockSpec((rows, group_size), lambda t: (0, 0)),
        ]
        + [any_spec] * count,
        out_shape=[
            jax.ShapeDtypeStruct((rows, width), jnp.bfloat16),
            jax.ShapeDtypeStruct((rows, group_size), jnp.float32),
            jax.ShapeDtypeStruct((rows, group_size), jnp.float32),
        ]
        + recv_shapes,
        scratch_shapes=[
            pltpu.VMEM((group_size, rows, DH), jnp.float32),
            pltpu.VMEM((group_size, rows, 2 * DH), jnp.float32),
            pltpu.SemaphoreType.DMA((count, n)),
            pltpu.SemaphoreType.DMA((count, n)),
            pltpu.SemaphoreType.DMA((count,)),
        ],
        compiler_params=pltpu.CompilerParams(
            collective_id=collective_id, has_side_effects=True, vmem_limit_bytes=56 * 1024 * 1024
        ),
        cost_estimate=cost,
    )(query_rows, keys_t, values, bias, new_keys_t, new_values, query_place, key_place, *sends)


def combine_kernel(heads, part_ref, fac_ref, den_ref, out_ref):
    senders = part_ref.shape[0]
    width = part_ref.shape[3]
    half = width // DH

    def sender_body(i, acc):
        fac = fac_ref[i]
        out = []
        for h in range(heads):
            j, c = divmod(h, half)
            blk = part_ref[i, j][:, c * DH : (c + 1) * DH].astype(jnp.float32)
            out.append(acc[h] + blk * fac[:, h : h + 1])
        return tuple(out)

    rows = out_ref.shape[0]
    start = tuple(jnp.zeros((rows, DH), jnp.float32) for _ in range(heads))
    acc = lax.fori_loop(0, senders, sender_body, start)
    den = den_ref[...]
    for h in range(heads):
        out_ref[:, h * DH : (h + 1) * DH] = (acc[h] / den[:, h : h + 1]).astype(out_ref.dtype)


def combine(part_sum, factor, denominator):
    senders, groups, rows, width = part_sum.shape
    heads = groups * width // DH
    vmem = pl.BlockSpec(memory_space=pltpu.VMEM)
    return pl.pallas_call(
        functools.partial(combine_kernel, heads),
        out_shape=jax.ShapeDtypeStruct((rows, heads * DH), jnp.bfloat16),
        in_specs=[vmem, vmem, vmem],
        out_specs=vmem,
        compiler_params=pltpu.CompilerParams(vmem_limit_bytes=32 * 1024 * 1024),
    )(part_sum, factor, denominator)


def combine_fused_kernel(heads, part_ref, max_ref, tot_ref, out_ref):
    senders = part_ref.shape[0]
    coef = DH ** (-0.5) * LOG2E
    top = lax.fori_loop(1, senders, lambda i, m: jnp.maximum(m, max_ref[i]), max_ref[0])

    def sender_body(i, carry):
        acc, den = carry
        fac = jnp.exp2((max_ref[i] - top) * coef)
        blk = part_ref[i].astype(jnp.float32)
        acc = tuple(
            acc[h] + blk[:, h * DH : (h + 1) * DH] * fac[:, h : h + 1] for h in range(heads)
        )
        return acc, den + tot_ref[i] * fac

    rows = out_ref.shape[0]
    start = tuple(jnp.zeros((rows, DH), jnp.float32) for _ in range(heads))
    acc, den = lax.fori_loop(0, senders, sender_body, (start, jnp.zeros_like(top)))
    for h in range(heads):
        out_ref[:, h * DH : (h + 1) * DH] = (acc[h] / den[:, h : h + 1]).astype(out_ref.dtype)


def combine_fused(part_sum, part_max, part_total):
    senders, rows, width = part_sum.shape
    heads = width // DH
    vmem = pl.BlockSpec(memory_space=pltpu.VMEM)
    return pl.pallas_call(
        functools.partial(combine_fused_kernel, heads),
        out_shape=jax.ShapeDtypeStruct((rows, width), jnp.bfloat16),
        in_specs=[vmem, vmem, vmem],
        out_specs=vmem,
        compiler_params=pltpu.CompilerParams(vmem_limit_bytes=32 * 1024 * 1024),
    )(part_sum, part_max, part_total)


def body(
    queries,
    new_keys,
    new_values,
    cache_keys,
    cache_values,
    keep_tiles,
    tile_count,
    owner_slot,
    out_weight,
):
    q_dev = queries.shape[0]
    kv_local = new_keys.shape[1] // DH
    q_local = queries.shape[1] // DH
    group_size = q_local // kv_local
    ctx_count = lax.axis_size("ctx")
    tp_count = lax.axis_size("tp")
    total_rows = q_dev * ctx_count
    my_index = lax.axis_index("ctx")
    key_place = owner_slot[my_index] * q_dev + jnp.arange(q_dev, dtype=jnp.int32)
    pieces = 4
    piece_heads = q_local // pieces
    width = piece_heads * DH
    (q_blocks,) = push((queries[:, :width],), "ctx", ctx_count, False, 0)
    query_place = (
        owner_slot[:, None] * q_dev + jnp.arange(q_dev, dtype=jnp.int32)[None, :]
    ).reshape(total_rows, 1)
    key_place = key_place.reshape(1, q_dev)
    slots = keep_tiles.shape[2]
    slot_ids = jnp.arange(slots * TILE, dtype=jnp.int32) // TILE

    def dense_head(g):
        cols = slice(g * DH, (g + 1) * DH)
        tiles_k = cache_keys[:, cols].reshape(-1, TILE, DH)
        tiles_v = cache_values[:, cols].reshape(-1, TILE, DH)
        kept_k = jnp.take(tiles_k, keep_tiles[0, g], axis=0).reshape(slots * TILE, DH)
        kept_v = jnp.take(tiles_v, keep_tiles[0, g], axis=0).reshape(slots * TILE, DH)
        bias = jnp.where(slot_ids < tile_count[0, g], 0.0, NEG_INF).astype(jnp.float32)
        return kept_k.T, kept_v, bias.reshape(1, slots * TILE), new_keys[:, cols].T, new_values[:, cols]

    head_data = [dense_head(g) for g in range(kv_local)]
    coef = DH ** (-0.5) * LOG2E

    def combine_piece(parts):
        part_sum, part_max, part_total = parts
        return combine_fused(part_sum, part_max, part_total)

    attn_pieces = []
    attn_blocks = []
    previous = None
    for i in range(pieces):
        sends = []
        flags = []
        if i + 1 < pieces:
            sends.append(queries[:, (i + 1) * width : (i + 2) * width])
            flags.append(False)
        if previous is not None:
            sends.extend(previous)
            flags.extend([True, True, True])
        if i >= 2:
            sends.append(attn_pieces[i - 2])
            flags.append(False)
        outs = attention_with_push(
            q_blocks.reshape(total_rows, width),
            *head_data[i * kv_local // pieces],
            query_place,
            key_place,
            tuple(sends),
            ctx_count,
            tuple(flags),
            4 + i,
        )
        sums_i, maxima_i, totals_i = outs[:3]
        rest = list(outs[3:])
        if i + 1 < pieces:
            q_blocks = rest.pop(0)
        if previous is not None:
            got = (rest.pop(0), rest.pop(0), rest.pop(0))
            attn_pieces.append(combine_piece(got))
        if i >= 2:
            attn_blocks.append(rest.pop(0))
        previous = (
            sums_i.reshape(ctx_count, q_dev, width),
            maxima_i.reshape(ctx_count, q_dev, piece_heads),
            totals_i.reshape(ctx_count, q_dev, piece_heads),
        )
    attn_pieces.append(combine_piece(push(previous, "ctx", ctx_count, True, 1)))
    attn_blocks.extend(push(tuple(attn_pieces[pieces - 2 :]), "ctx", ctx_count, False, 2))
    projected = None
    for j, blocks in enumerate(attn_blocks):
        term = jnp.dot(
            blocks.reshape(total_rows, width),
            out_weight[j * width : (j + 1) * width],
            preferred_element_type=jnp.float32,
        )
        projected = term if projected is None else projected + term
    out_rows = total_rows // tp_count
    (proj_parts,) = push(
        (projected.reshape(tp_count, out_rows, projected.shape[1]),), "tp", tp_count, True, 3
    )
    return jnp.sum(proj_parts, axis=0)


def solution(mesh):
    return jax.shard_map(
        body,
        mesh=mesh,
        in_specs=(
            P("ctx", "tp"),
            P("ctx", "tp"),
            P("ctx", "tp"),
            P("ctx", "tp"),
            P("ctx", "tp"),
            P("ctx", "tp", None),
            P("ctx", "tp"),
            P(),
            P("tp", "ctx"),
        ),
        out_specs=P("tp", "ctx"),
        check_vma=False,
    )
```
